512 devices in a mesh: gx: 32 (over z_hi, x, core), gy: 16 (over y, z_lo).
Axes of the slice: x: 4, y: 8, z: 8 (z_hi: 4, z_lo: 2; z = z_hi * 2 + z_lo), core: 2. Of those that a mesh axis runs over, the one named last changes fastest.
Arguments:
- tokens: bfloat16 [2304, 4608], P('gx', 'gy'), may hold values from -6 to 6
- pre_gain: bfloat16 [4608], P('gy'), may hold values from -0.5 to 0.5
- w_q: bfloat16 [4608, 4096], P('gx', 'gy'), may hold values from -0.09375 to 0.09375
- w_k: bfloat16 [4608, 2048], P('gx', 'gy'), may hold values from -0.09375 to 0.09375
- w_v: bfloat16 [4608, 2048], P('gx', 'gy'), may hold values from -0.09375 to 0.09375
- w_o: bfloat16 [4096, 4608], P('gy', 'gx')
- post_gain: bfloat16 [4608], P('gy'), may hold values from -0.5 to 0.5
- k_cache: bfloat16 [32768, 2048], P('gx', 'gy'), may hold values from -6 to 6
- v_cache: bfloat16 [32768, 2048], P('gx', 'gy')
- cached_len: int32 [12], replicated, may hold values from 1 to 10240, as said below
- new_len: int32 [12], replicated, may hold values from 48 to 192, as said below
- slot_offset: int32 [12], replicated, may hold values from 0 to 32575, as said below
Outputs:
- layer_out: bfloat16 [2304, 4608], P('gx', 'gy')
- k_pool: bfloat16 [32768, 2048], P('gx', 'gy')
- v_pool: bfloat16 [32768, 2048], P('gx', 'gy')
The draws below stay inside these ranges and needn't reach their ends.
Inputs may be any that keep to these rules, and one draw needn't show every extreme that they name: `cached_len`: two requests are long: one has exactly 10240 cached tokens, the other between 10049 and 10240; the others have at most 512, and one of them has exactly 1. `new_len`: some request has all 192 slots real. Request r owns pool slots slot_offset[r] to slot_offset[r] + cached_len[r] + 191; these regions are disjoint and lie inside the pool; one starts at slot 0 and one ends at the pool's last slot.
All inputs are finite; a program needn't handle non-finite values.
Results may differ from the reference program's by a relative error of at most 0.02.
Values may be sent and summed in bfloat16 or wider, within the bound.
No kernel may reach another device: no remote copies, remote signals or barrier semaphores. Data moves between devices by JAX's collectives and lax.ppermute only.
A program may use at most 64 MiB of HBM per device.

```python
import jax
import jax.numpy as jnp
from jax import lax

D = 4608
QH = 32
KVH = 16
HD = 128
REQS = 12
NEWTOK = 192
SLOT_DEV = 1024
TOKENS = 2304
SLOTS = 32768
LONG = 10240
SHORT_MAX = 512
N_GY = 16


def pool_layout(key):
    base_key = jax.random.fold_in(key, 7)
    key_pick, key_short, key_trim, key_fresh, key_order, key_lead = jax.random.split(base_key, 6)
    picked = jax.random.permutation(key_pick, REQS)
    ident = jnp.arange(REQS, dtype=jnp.int32)
    lengths = jax.random.randint(key_short, (REQS,), 1, SHORT_MAX + 1)
    lengths = jnp.where(ident == picked[0], LONG, lengths)
    trimmed = LONG - jax.random.randint(key_trim, (), 0, NEWTOK)
    lengths = jnp.where(ident == picked[1], trimmed, lengths)
    lengths = jnp.where(ident == picked[3], 1, lengths).astype(jnp.int32)
    fresh = jax.random.randint(key_fresh, (REQS,), max(1, NEWTOK // 4), NEWTOK + 1)
    fresh = jnp.where(ident == picked[2], NEWTOK, fresh).astype(jnp.int32)
    scores = jax.random.permutation(key_order, REQS).astype(jnp.int32)
    scores = jnp.where(ident == picked[3], REQS, scores)
    ordering = jnp.argsort(scores, stable=True)
    spans = (lengths + NEWTOK)[ordering]
    starts = jnp.cumsum(spans) - spans
    slack = SLOTS - jnp.sum(spans)
    gap_at = jax.random.randint(key_lead, (), 1, REQS)
    shifted = starts + jnp.where(ident >= gap_at, slack, 0)
    offsets = jnp.zeros((REQS,), jnp.int32).at[ordering].set(shifted.astype(jnp.int32))
    return (lengths, fresh, offsets)


def draw_cached_len(key, part):
    return pool_layout(key)[0]


def draw_new_len(key, part):
    return pool_layout(key)[1]


def draw_slot_offset(key, part):
    return pool_layout(key)[2]


def draw_w_o(key, part):
    row_count = QH * HD
    key_entries, key_column = jax.random.split(jax.random.fold_in(key, 11))
    entries = jnp.clip(jax.random.normal(key_entries, (row_count, D), jnp.float32), -6.0, 6.0)
    column = jnp.clip(jax.random.normal(key_column, (D,), jnp.float32), -4.0, 4.0)
    strength = 1.5
    shaped = entries * row_count ** (-0.5) + strength * column[None, :] / row_count
    return shaped.astype(jnp.bfloat16)


def draw_v_cache(key, part):
    key_values = jax.random.fold_in(key, 13)
    values = jnp.clip(jax.random.normal(key_values, (SLOTS, KVH * HD), jnp.float32), -6.0, 6.0)
    offset_mean = 0.02
    return (values + offset_mean).astype(jnp.bfloat16)


def level_of(own_key, shape, pieces, low, top_value):
    def one(axis_at, blocks):
        heights = jax.random.uniform(jax.random.fold_in(jax.random.fold_in(own_key, 6), axis_at), (blocks,), jnp.float32, low / len(pieces), top_value / len(pieces))
        return jnp.repeat(jnp.exp(heights), shape[axis_at] // blocks).reshape((-1,) + (1,) * (len(shape) - axis_at - 1))

    gain = one(*pieces[0])
    for cut in pieces[1:]:
        gain = gain * one(*cut)
    return gain


def centred(rng, extent, width, limit, cuts=(), held_as=jnp.bfloat16):
    values = jax.random.normal(rng, extent, jnp.float32) * width
    if len(cuts) > 0:
        values = level_of(rng, extent, cuts, -0.22, 0.18) * values
    return jnp.clip(values, min=-limit, max=limit).astype(held_as)


def setup_inputs(seed: int = 0) -> dict:
    splits = jax.random.split(jax.random.key(seed), 13)
    tokens = centred(splits[0], (TOKENS, D), 1.0, 6.0, ((0, 32), (1, 16)))
    pre_gain = jnp.clip(jax.random.uniform(splits[1], (D,), jnp.float32, -0.5, 0.5) * level_of(splits[1], (D,), ((0, 16),), -0.4, 0.0), -0.5, 0.5).astype(jnp.bfloat16)
    w_q = centred(splits[2], (D, QH * HD), D ** -0.5, 0.09375, ((0, 32), (1, 16)))
    w_k = centred(splits[3], (D, KVH * HD), D ** -0.5, 0.09375, ((0, 32), (1, 16)))
    w_v = centred(splits[4], (D, KVH * HD), D ** -0.5, 0.09375, ((0, 32), (1, 16)))
    w_o = draw_w_o(jax.random.fold_in(splits[12], 71), 0)
    post_gain = jnp.clip(jax.random.uniform(splits[6], (D,), jnp.float32, -0.5, 0.5) * level_of(splits[6], (D,), ((0, 16),), -0.4, 0.0), -0.5, 0.5).astype(jnp.bfloat16)
    k_cache = centred(splits[7], (SLOTS, KVH * HD), 1.0, 6.0, ((0, 32), (1, 16)))
    v_cache = draw_v_cache(jax.random.fold_in(splits[12], 71), 0)
    cached_len = draw_cached_len(jax.random.fold_in(splits[12], 71), 0)
    new_len = draw_new_len(jax.random.fold_in(splits[12], 71), 0)
    slot_offset = draw_slot_offset(jax.random.fold_in(splits[12], 71), 0)
    return dict(tokens=tokens, pre_gain=pre_gain, w_q=w_q, w_k=w_k, w_v=w_v, w_o=w_o, post_gain=post_gain, k_cache=k_cache, v_cache=v_cache, cached_len=cached_len, new_len=new_len, slot_offset=slot_offset)


epsilon = 1e-06
soft_cap = 50.0
query_scale = 144.0 ** (-0.5)

def rotate(values, position, head_size):
    rows = values.shape[0]
    parts = values.reshape(rows, -1, head_size)
    half = head_size // 2
    inverse = jnp.power(10000.0, -2.0 * jnp.arange(half, dtype=jnp.float32) / head_size)
    angle = position.astype(jnp.float32)[:, None] * inverse[None, :]
    cosine = jnp.cos(angle)[:, None, :]
    sine = jnp.sin(angle)[:, None, :]
    first = parts[:, :, :half]
    second = parts[:, :, half:]
    turned = jnp.concatenate([first * cosine - second * sine, second * cosine + first * sine], axis=2)
    return turned.reshape(rows, -1)

def reference(tokens, pre_gain, w_q, w_k, w_v, w_o, post_gain, k_cache, v_cache, cached_len, new_len, slot_offset):
    float_in = tokens.astype(jnp.float32)
    scale_rows = lax.rsqrt(lax.optimization_barrier(jnp.mean(float_in * float_in, axis=1, keepdims=True)) + epsilon)
    normed = (float_in * scale_rows * (1.0 + pre_gain.astype(jnp.float32))).astype(jnp.bfloat16)
    q_lin = jnp.dot(normed, w_q, preferred_element_type=jnp.float32)
    k_lin = jnp.dot(normed, w_k, preferred_element_type=jnp.float32)
    v_lin = jnp.dot(normed, w_v, preferred_element_type=jnp.float32)
    row_ids = jnp.arange(TOKENS, dtype=jnp.int32)
    request = row_ids // NEWTOK
    within = row_ids % NEWTOK
    position = cached_len[request] + within
    queries = (rotate(q_lin, position, HD) * query_scale).astype(jnp.bfloat16)
    k_new = rotate(k_lin, position, HD).astype(jnp.bfloat16)
    v_new = v_lin.astype(jnp.bfloat16)
    target = jnp.where(within < new_len[request], slot_offset[request] + cached_len[request] + within, SLOTS)
    k_pool = k_cache.at[target].set(k_new, mode='drop')
    v_pool = v_cache.at[target].set(v_new, mode='drop')
    group_size = QH // KVH

    def attend_request(request_id):
        rows = lax.dynamic_slice_in_dim(queries, request_id * NEWTOK, NEWTOK, 0).astype(jnp.float32)
        rows = rows.reshape(NEWTOK, KVH, group_size, HD)
        offset = slot_offset[request_id]
        cached = cached_len[request_id]
        fresh_count = new_len[request_id]
        last_seen = cached + jnp.minimum(jnp.arange(NEWTOK, dtype=jnp.int32), fresh_count - 1)
        first_block = offset // SLOT_DEV
        final_block = (offset + cached + fresh_count - 1) // SLOT_DEV

        def block_terms(block, running):
            numerator, denominator = running
            key_rows = lax.dynamic_slice_in_dim(k_pool, block * SLOT_DEV, SLOT_DEV, 0).astype(jnp.float32)
            key_rows = key_rows.reshape(SLOT_DEV, KVH, HD)
            value_rows = lax.dynamic_slice_in_dim(v_pool, block * SLOT_DEV, SLOT_DEV, 0).astype(jnp.float32)
            value_rows = value_rows.reshape(SLOT_DEV, KVH, HD)
            key_pos = block * SLOT_DEV + jnp.arange(SLOT_DEV, dtype=jnp.int32) - offset
            visible = (key_pos[None, :] >= 0) & (key_pos[None, :] <= last_seen[:, None])
            logits = jnp.einsum('cgjd,sgd->cgjs', rows, key_rows)
            weight = jnp.where(visible[:, None, None, :], jnp.exp(soft_cap * jnp.tanh(logits / soft_cap)), 0.0)
            part_den = lax.optimization_barrier(jnp.sum(weight, axis=3)).astype(jnp.bfloat16)
            rounded = lax.optimization_barrier(weight.astype(jnp.bfloat16)).astype(jnp.float32)
            part_num = jnp.einsum('cgjs,sgd->cgjd', rounded, value_rows).astype(jnp.bfloat16)
            part_num, part_den = lax.optimization_barrier((part_num, part_den))
            return (numerator + part_num.astype(jnp.float32), denominator + part_den.astype(jnp.float32))
        initial = (jnp.zeros((NEWTOK, KVH, group_size, HD), jnp.float32), jnp.zeros((NEWTOK, KVH, group_size), jnp.float32))
        numerator, denominator = lax.fori_loop(first_block, final_block + 1, block_terms, initial)
        result = numerator / denominator[:, :, :, None]
        real_rows = jnp.arange(NEWTOK, dtype=jnp.int32) < fresh_count
        result = jnp.where(real_rows[:, None, None, None], result, 0.0)
        return result.reshape(NEWTOK, QH * HD).astype(jnp.bfloat16)
    attended = lax.map(attend_request, jnp.arange(REQS, dtype=jnp.int32)).reshape(TOKENS, QH * HD)
    group_cols = QH * HD // N_GY

    def add_group(group, summed):
        left = lax.dynamic_slice_in_dim(attended, group * group_cols, group_cols, 1)
        right = lax.dynamic_slice_in_dim(w_o, group * group_cols, group_cols, 0)
        part = jnp.dot(left, right, preferred_element_type=jnp.float32).astype(jnp.bfloat16)
        part = lax.optimization_barrier(part)
        return summed + part.astype(jnp.float32)
    branch = lax.fori_loop(0, N_GY, add_group, jnp.zeros((TOKENS, D), jnp.float32))
    mean_square = lax.optimization_barrier(jnp.mean(branch * branch, axis=1, keepdims=True))
    layer_out = (float_in + branch * lax.rsqrt(mean_square + epsilon) * (1.0 + post_gain.astype(jnp.float32))).astype(jnp.bfloat16)
    return (layer_out, k_pool, v_pool)
```

```python
import jax
import jax.numpy as jnp
from jax import lax
from jax.experimental import pallas as pl
from jax.experimental.pallas import tpu as pltpu
from jax.sharding import Mesh, PartitionSpec as P

D = 4608
HD = 128
REQS = 12
NEWTOK = 192
TILE = 256
PIECE = 48
epsilon = 1e-06
soft_cap = 50.0
query_scale = 144.0 ** (-0.5)
F32 = jnp.float32
BF16 = jnp.bfloat16

CHIPS = ("zh", "x")
GX = ("zh", "x", "c")
GY = ("y", "zl")


def everywhere(value, axes, count):
    return lax.all_to_all(jnp.broadcast_to(value[None], (count,) + value.shape), axes, 0, 0)


def attend_kernel(meta, qkv, k_old, v_old, k_pool, v_pool, sums, num, den, totals):
    slots = k_old.shape[0]
    tiles = slots // TILE
    first = meta[3 * REQS]
    chunk = sums.shape[1] // (REQS * NEWTOK // (3 * PIECE))
    heads = sums.shape[0]

    k_pool[...] = k_old[...]
    v_pool[...] = v_old[...]
    totals[...] = jnp.zeros_like(totals)

    def write_request(r, carry):
        cached, fresh, offset = meta[r], meta[REQS + r], meta[2 * REQS + r]
        begin = offset + cached - first
        for t in range(tiles):

            @pl.when((begin < (t + 1) * TILE) & (begin + fresh > t * TILE))
            def _():
                rows = qkv[1, pl.ds(pl.multiple_of(r * NEWTOK, 64), NEWTOK), :]
                slot = lax.broadcasted_iota(jnp.int32, (TILE, NEWTOK), 0) + (t * TILE - begin)
                index = lax.broadcasted_iota(jnp.int32, (TILE, NEWTOK), 1)
                pick = jnp.where((slot == index) & (index < fresh), 1.0, 0.0).astype(BF16)
                new = jnp.dot(pick, rows, preferred_element_type=F32)
                place = lax.broadcasted_iota(jnp.int32, (TILE, HD), 0) + (t * TILE - begin)
                written = (place >= 0) & (place < fresh)
                here = pl.ds(t * TILE, TILE)
                k_pool[here, :] = jnp.where(written, new[:, :HD], k_pool[here, :].astype(F32)).astype(BF16)
                v_pool[here, :] = jnp.where(written, new[:, HD:], v_pool[here, :].astype(F32)).astype(BF16)

        return carry

    lax.fori_loop(0, REQS, write_request, 0)

    def read_request(r, carry):
        cached, fresh, offset = meta[r], meta[REQS + r], meta[2 * REQS + r]
        begin = offset - first
        end = begin + cached + fresh
        num[...] = jnp.zeros_like(num)
        den[...] = jnp.zeros_like(den)

        @pl.when((begin < slots) & (end > 0))
        def _():
            rows = qkv[0, pl.ds(pl.multiple_of(r * NEWTOK, 64), NEWTOK), :]
            rows = jnp.concatenate([rows[:, h * HD : (h + 1) * HD] for h in range(heads)], axis=0)
            row = lax.broadcasted_iota(jnp.int32, (heads * NEWTOK, 1), 0)
            row = jnp.where(row >= NEWTOK, row - NEWTOK, row)
            last = cached + jnp.minimum(row, fresh - 1) + begin
            for t in range(tiles):

                @pl.when((begin < (t + 1) * TILE) & (end > t * TILE))
                def _():
                    here = pl.ds(t * TILE, TILE)
                    logits = lax.dot_general(
                        rows, k_pool[here, :], (((1,), (1,)), ((), ())), preferred_element_type=F32
                    )
                    slot = lax.broadcasted_iota(jnp.int32, logits.shape, 1) + t * TILE
                    visible = (slot >= begin) & (slot <= last)
                    weight = jnp.exp(soft_cap * jnp.tanh(logits * (1.0 / soft_cap)))
                    weight = jnp.where(visible, weight, 0.0).astype(BF16)
                    num[...] += jnp.dot(weight, v_pool[here, :], preferred_element_type=F32)
                    den[...] += lax.dot_general(
                        jnp.ones((8, TILE), BF16), weight, (((1,), (1,)), ((), ())), preferred_element_type=F32
                    )

        for piece in range(NEWTOK // PIECE):
            at = r * (NEWTOK // PIECE) + piece
            block, part = at // 3, at % 3
            to = pl.multiple_of(block * chunk + part * PIECE, 16)
            for h in range(heads):
                low = h * NEWTOK + piece * PIECE
                sums[h, pl.ds(to, PIECE), :] = num[low : low + PIECE, :].astype(BF16)
                totals[h, pl.ds(block * 8 + part, 1), 0:PIECE] = den[0:1, low : low + PIECE]
        return carry

    lax.fori_loop(0, REQS, read_request, 0)
    for h in range(heads):
        for block in range(REQS * NEWTOK // (3 * PIECE)):
            rows = totals[h, block * 8 : block * 8 + 8, :]
            rows = jnp.concatenate([rows, jnp.zeros_like(rows)], axis=0)
            sums[h, block * chunk + 3 * PIECE : (block + 1) * chunk, :] = rows.astype(BF16)


def attend(meta, qkv, k_cache, v_cache):
    heads = 2
    blocks = REQS * NEWTOK // (3 * PIECE)
    chunk = 3 * PIECE + 16
    vmem = pl.BlockSpec(memory_space=pltpu.VMEM)
    return pl.pallas_call(
        attend_kernel,
        out_shape=(
            jax.ShapeDtypeStruct(k_cache.shape, BF16),
            jax.ShapeDtypeStruct(v_cache.shape, BF16),
            jax.ShapeDtypeStruct((heads, blocks * chunk, HD), BF16),
        ),
        in_specs=[pl.BlockSpec(memory_space=pltpu.SMEM), vmem, vmem, vmem],
        out_specs=(vmem, vmem, vmem),
        scratch_shapes=[
            pltpu.VMEM((heads * NEWTOK, HD), F32),
            pltpu.VMEM((8, heads * NEWTOK), F32),
            pltpu.VMEM((heads, blocks * 8, HD), F32),
        ],
        compiler_params=pltpu.CompilerParams(vmem_limit_bytes=32 << 20),
        name="attend",
    )(meta, qkv, k_cache, v_cache)


def divide_kernel(meta, parts, out):
    fresh_at = REQS
    begin = meta[3 * REQS + 1]
    total = jnp.sum(parts[...].astype(F32), axis=0)
    for part in range(3):
        row = begin + part * PIECE
        request = row // NEWTOK
        fresh = meta[fresh_at + request]
        within = lax.broadcasted_iota(jnp.int32, (PIECE, HD), 0) + (row - request * NEWTOK)
        den = total[3 * PIECE + part : 3 * PIECE + part + 1, 0:PIECE]
        diagonal = lax.broadcasted_iota(jnp.int32, (PIECE, PIECE), 0) == lax.broadcasted_iota(
            jnp.int32, (PIECE, PIECE), 1
        )
        den = jnp.sum(jnp.where(diagonal, den, 0.0), axis=1, keepdims=True)
        value = total[part * PIECE : (part + 1) * PIECE, :] / den
        out[part * PIECE : (part + 1) * PIECE, :] = jnp.where(within < fresh, value, 0.0).astype(BF16)


def divide(meta, parts):
    vmem = pl.BlockSpec(memory_space=pltpu.VMEM)
    return pl.pallas_call(
        divide_kernel,
        out_shape=jax.ShapeDtypeStruct((3 * PIECE, HD), BF16),
        in_specs=[pl.BlockSpec(memory_space=pltpu.SMEM), vmem],
        out_specs=vmem,
        compiler_params=pltpu.CompilerParams(vmem_limit_bytes=16 << 20),
        name="divide",
    )(meta, parts)


def on_device(
    tokens, pre_gain, w_q, w_k, w_v, w_o, post_gain, k_cache, v_cache, cached_len, new_len, slot_offset
):
    tok_rows = tokens.shape[0]
    n_gy = lax.axis_size(GY)
    n_chips = lax.axis_size(CHIPS)
    me = lax.axis_index(GX)
    weights = lax.all_gather(jnp.concatenate([w_q, w_k, w_v], axis=1), GX, axis=0, tiled=True)
    w_out = lax.all_gather(w_o.T, GX, axis=0, tiled=True)

    float_in = tokens.astype(F32)
    squares = jnp.sum(float_in * float_in, axis=1, keepdims=True)
    high = lax.reduce_precision(squares, 8, 7)
    gained = float_in * (1.0 + pre_gain.astype(F32))
    gained = jnp.concatenate([gained, high, squares - high], axis=1).astype(BF16)
    gained = everywhere(gained, GY, n_gy)
    features = tokens.shape[1]
    mean = jnp.sum(gained[:, :, features:].astype(F32), axis=(0, 2)) / D
    scale_rows = lax.rsqrt(mean + epsilon)[:, None]
    whole = jnp.swapaxes(gained[:, :, :features], 0, 1).reshape(tok_rows, D)
    lin = jnp.dot(whole, weights, preferred_element_type=F32) * scale_rows

    row_ids = me * tok_rows + jnp.arange(tok_rows, dtype=jnp.int32)
    request = row_ids // NEWTOK
    owner_mask = request[:, None] == jnp.arange(REQS, dtype=jnp.int32)[None, :]
    position = jnp.sum(jnp.where(owner_mask, cached_len[None, :], 0), axis=1) + row_ids % NEWTOK
    half = HD // 2
    inverse = jnp.power(10000.0, -2.0 * jnp.arange(half, dtype=F32) / HD)
    angle = position.astype(F32)[:, None] * inverse[None, :]
    cosine, sine = jnp.cos(angle), jnp.sin(angle)

    def rotate(values):
        first, second = values[:, :half], values[:, half:]
        return jnp.concatenate([first * cosine - second * sine, second * cosine + first * sine], axis=1)

    q_cols = w_q.shape[1]
    pieces = [rotate(lin[:, h * HD : (h + 1) * HD]) * query_scale for h in range(q_cols // HD)]
    pieces += [rotate(lin[:, q_cols : q_cols + HD]), lin[:, q_cols + HD :]]
    fresh_rows = jnp.concatenate(pieces, axis=1).astype(BF16)

    mine = lax.all_to_all(fresh_rows, "c", 1, 0, tiled=True)
    mine = everywhere(mine, CHIPS, n_chips).reshape(-1, q_cols)
    qkv = everywhere(mine, "c", 2)

    meta = jnp.concatenate(
        [
            cached_len,
            new_len,
            slot_offset,
            jnp.stack([me * k_cache.shape[0], me // 2 * (2 * tok_rows)]).astype(jnp.int32),
        ]
    )
    k_pool, v_pool, sums = attend(meta, qkv, k_cache, v_cache)

    both = lax.all_to_all(sums, "c", 0, 0)
    head = (both[0].astype(F32) + both[1].astype(F32)).astype(BF16)
    parts = lax.all_to_all(head.reshape(n_chips, -1, HD), CHIPS, 0, 0)
    attended = divide(meta, parts)
    attended = lax.all_to_all(attended.reshape(2, tok_rows, HD), "c", 0, 0)
    attended = jnp.swapaxes(attended, 0, 1).reshape(tok_rows, 2 * HD)

    partial_out = lax.dot_general(attended, w_out, (((1,), (1,)), ((), ())), preferred_element_type=F32)
    partial_out = jnp.swapaxes(partial_out.astype(BF16).reshape(tok_rows, n_gy, features), 0, 1)
    branch = jnp.sum(lax.all_to_all(partial_out, GY, 0, 0).astype(F32), axis=0)
    squares = jnp.sum(branch * branch, axis=1)
    mean = jnp.sum(everywhere(squares[None, :], GY, n_gy), axis=(0, 1)) / D
    layer_out = float_in + branch * lax.rsqrt(mean + epsilon)[:, None] * (1.0 + post_gain.astype(F32))
    return (layer_out.astype(BF16), k_pool, v_pool)


def solution(mesh):
    parts = Mesh(mesh.devices.reshape(4, 4, 2, 8, 2), GX + GY)
    both = P(GX, GY)
    placed = (both, P(GY), both, both, both, P(GY, GX), P(GY), both, both, P(), P(), P())
    return jax.shard_map(
        on_device, mesh=parts, in_specs=placed, out_specs=(both, both, both), check_vma=False
    )
```

```python
import jax
import jax.numpy as jnp
from jax import lax
from jax.experimental import pallas as pl
from jax.experimental.pallas import tpu as pltpu
from jax.sharding import Mesh, PartitionSpec as P

D = 4608
HD = 128
REQS = 12
NEWTOK = 192
TILE = 256
PIECE = 48
epsilon = 1e-06
soft_cap = 50.0
query_scale = 144.0 ** (-0.5)
F32 = jnp.float32
BF16 = jnp.bfloat16

CHIPS = ("zh", "x")
GX = ("zh", "x", "c")
GY = ("y", "zl")


def everywhere(value, axes, count):
    return lax.all_to_all(jnp.broadcast_to(value[None], (count,) + value.shape), axes, 0, 0)


def project_kernel(meta, tokens, turns, *rest):
    columns, out = rest[:-1], rest[-1]
    here = meta[3 * REQS + 3]
    features = tokens.shape[3] - 2
    count = len(columns)
    total = jnp.zeros(out.shape, F32)
    squares = jnp.zeros((out.shape[0], 2), F32)
    for step in range(count):
        along = lax.rem(here + step, count)
        for block in range(tokens.shape[1] // count):
            at = block * count + along
            rows = jnp.concatenate([tokens[0, at], tokens[1, at]], axis=0)
            squares += rows[:, features:].astype(F32)
            total += jnp.dot(
                rows[:, :features],
                columns[step][block * features : (block + 1) * features, :],
                preferred_element_type=F32,
            )
    mean = jnp.sum(squares, axis=1, keepdims=True) * (1.0 / D)
    total = total * lax.rsqrt(mean + epsilon)
    for head in range(2):
        value = total[:, head * HD : (head + 1) * HD]
        value = value * turns[2 * head] + pltpu.roll(value, HD // 2, 1) * turns[2 * head + 1]
        out[:, head * HD : (head + 1) * HD] = value.astype(BF16)


def project(meta, tokens, turns, columns):
    vmem = pl.BlockSpec(memory_space=pltpu.VMEM)
    return pl.pallas_call(
        project_kernel,
        out_shape=jax.ShapeDtypeStruct((2 * tokens.shape[2], columns[0].shape[1]), BF16),
        in_specs=[pl.BlockSpec(memory_space=pltpu.SMEM)] + [vmem] * (2 + len(columns)),
        out_specs=vmem,
        compiler_params=pltpu.CompilerParams(vmem_limit_bytes=32 << 20),
        name="project",
    )(meta, tokens, turns, *columns)


def attend_kernel(meta, mine, others, k_old, v_old, k_pool, v_pool, sums, num, den, totals):
    slots = k_old.shape[0]
    tiles = slots // TILE
    first = meta[3 * REQS]
    queries_here = meta[3 * REQS + 2] == 0
    chunk = sums.shape[1] // (REQS * NEWTOK // (3 * PIECE))
    heads = sums.shape[0]

    def rows_of(r, on_core_0, on_core_1):
        here = pl.ds(pl.multiple_of(r * NEWTOK, 64), NEWTOK)
        return jnp.where(queries_here, on_core_0[here, :], on_core_1[here, :])

    k_pool[...] = k_old[...]
    v_pool[...] = v_old[...]
    totals[...] = jnp.zeros_like(totals)

    def write_request(r, carry):
        cached, fresh, offset = meta[r], meta[REQS + r], meta[2 * REQS + r]
        begin = offset + cached - first
        for t in range(tiles):

            @pl.when((begin < (t + 1) * TILE) & (begin + fresh > t * TILE))
            def _():
                rows = rows_of(r, others, mine)
                slot = lax.broadcasted_iota(jnp.int32, (TILE, NEWTOK), 0) + (t * TILE - begin)
                index = lax.broadcasted_iota(jnp.int32, (TILE, NEWTOK), 1)
                pick = jnp.where((slot == index) & (index < fresh), 1.0, 0.0).astype(BF16)
                new = jnp.dot(pick, rows, preferred_element_type=F32)
                place = lax.broadcasted_iota(jnp.int32, (TILE, HD), 0) + (t * TILE - begin)
                written = (place >= 0) & (place < fresh)
                here = pl.ds(t * TILE, TILE)
                k_pool[here, :] = jnp.where(written, new[:, :HD], k_pool[here, :].astype(F32)).astype(BF16)
                v_pool[here, :] = jnp.where(written, new[:, HD:], v_pool[here, :].astype(F32)).astype(BF16)

        return carry

    lax.fori_loop(0, REQS, write_request, 0)

    def read_request(r, carry):
        cached, fresh, offset = meta[r], meta[REQS + r], meta[2 * REQS + r]
        begin = offset - first
        end = begin + cached + fresh
        num[...] = jnp.zeros_like(num)
        den[...] = jnp.zeros_like(den)

        @pl.when((begin < slots) & (end > 0))
        def _():
            rows = rows_of(r, mine, others)
            rows = jnp.concatenate([rows[:, h * HD : (h + 1) * HD] for h in range(heads)], axis=0)
            row = lax.broadcasted_iota(jnp.int32, (heads * NEWTOK, 1), 0)
            row = jnp.where(row >= NEWTOK, row - NEWTOK, row)
            last = cached + jnp.minimum(row, fresh - 1) + begin
            for t in range(tiles):

                @pl.when((begin < (t + 1) * TILE) & (end > t * TILE))
                def _():
                    here = pl.ds(t * TILE, TILE)
                    logits = lax.dot_general(
                        rows, k_pool[here, :], (((1,), (1,)), ((), ())), preferred_element_type=F32
                    )
                    slot = lax.broadcasted_iota(jnp.int32, logits.shape, 1) + t * TILE
                    visible = (slot >= begin) & (slot <= last)
                    weight = jnp.exp(soft_cap * jnp.tanh(logits * (1.0 / soft_cap)))
                    weight = jnp.where(visible, weight, 0.0).astype(BF16)
                    num[...] += jnp.dot(weight, v_pool[here, :], preferred_element_type=F32)
                    den[...] += lax.dot_general(
                        jnp.ones((8, TILE), BF16), weight, (((1,), (1,)), ((), ())), preferred_element_type=F32
                    )

        for piece in range(NEWTOK // PIECE):
            at = r * (NEWTOK // PIECE) + piece
            block, part = at // 3, at % 3
            to = pl.multiple_of(block * chunk + part * PIECE, 16)
            for h in range(heads):
                low = h * NEWTOK + piece * PIECE
                sums[h, pl.ds(to, PIECE), :] = num[low : low + PIECE, :].astype(BF16)
                totals[h, pl.ds(block * 8 + part, 1), 0:PIECE] = den[0:1, low : low + PIECE]
        return carry

    lax.fori_loop(0, REQS, read_request, 0)
    for h in range(heads):
        for block in range(REQS * NEWTOK // (3 * PIECE)):
            rows = totals[h, block * 8 : block * 8 + 8, :]
            rows = jnp.concatenate([rows, jnp.zeros_like(rows)], axis=0)
            sums[h, block * chunk + 3 * PIECE : (block + 1) * chunk, :] = rows.astype(BF16)


def attend(meta, mine, others, k_cache, v_cache):
    heads = 2
    blocks = REQS * NEWTOK // (3 * PIECE)
    chunk = 3 * PIECE + 16
    vmem = pl.BlockSpec(memory_space=pltpu.VMEM)
    return pl.pallas_call(
        attend_kernel,
        out_shape=(
            jax.ShapeDtypeStruct(k_cache.shape, BF16),
            jax.ShapeDtypeStruct(v_cache.shape, BF16),
            jax.ShapeDtypeStruct((heads, blocks * chunk, HD), BF16),
        ),
        in_specs=[pl.BlockSpec(memory_space=pltpu.SMEM), vmem, vmem, vmem, vmem],
        out_specs=(vmem, vmem, vmem),
        scratch_shapes=[
            pltpu.VMEM((heads * NEWTOK, HD), F32),
            pltpu.VMEM((8, heads * NEWTOK), F32),
            pltpu.VMEM((heads, blocks * 8, HD), F32),
        ],
        compiler_params=pltpu.CompilerParams(vmem_limit_bytes=32 << 20),
        name="attend",
    )(meta, mine, others, k_cache, v_cache)


def divide_kernel(meta, parts, out):
    fresh_at = REQS
    begin = meta[3 * REQS + 1]
    total = jnp.sum(parts[...].astype(F32), axis=0)
    for part in range(3):
        row = begin + part * PIECE
        request = row // NEWTOK
        fresh = meta[fresh_at + request]
        within = lax.broadcasted_iota(jnp.int32, (PIECE, HD), 0) + (row - request * NEWTOK)
        den = total[3 * PIECE + part : 3 * PIECE + part + 1, 0:PIECE]
        diagonal = lax.broadcasted_iota(jnp.int32, (PIECE, PIECE), 0) == lax.broadcasted_iota(
            jnp.int32, (PIECE, PIECE), 1
        )
        den = jnp.sum(jnp.where(diagonal, den, 0.0), axis=1, keepdims=True)
        value = total[part * PIECE : (part + 1) * PIECE, :] / den
        out[part * PIECE : (part + 1) * PIECE, :] = jnp.where(within < fresh, value, 0.0).astype(BF16)


def divide(meta, parts):
    vmem = pl.BlockSpec(memory_space=pltpu.VMEM)
    return pl.pallas_call(
        divide_kernel,
        out_shape=jax.ShapeDtypeStruct((3 * PIECE, HD), BF16),
        in_specs=[pl.BlockSpec(memory_space=pltpu.SMEM), vmem],
        out_specs=vmem,
        compiler_params=pltpu.CompilerParams(vmem_limit_bytes=16 << 20),
        name="divide",
    )(meta, parts)


def on_device(
    tokens, pre_gain, w_q, w_k, w_v, w_o, post_gain, k_cache, v_cache, cached_len, new_len, slot_offset
):
    tok_rows = tokens.shape[0]
    features = tokens.shape[1]
    n_gy = lax.axis_size(GY)
    n_chips = lax.axis_size(CHIPS)
    me = lax.axis_index(GX)
    core = lax.axis_index("c")
    cols = w_q.shape[1]

    weights = jnp.concatenate([w_q, w_k, w_v], axis=1)
    weights = lax.all_to_all(weights, "c", 1, 0, tiled=True)
    weights = lax.all_gather(weights, "zh", axis=0, tiled=True)
    w_out = lax.all_gather(w_o.T, GX, axis=0, tiled=True)

    float_in = tokens.astype(F32)
    squares = jnp.sum(float_in * float_in, axis=1, keepdims=True)
    high = lax.reduce_precision(squares, 8, 7)
    gained = float_in * (1.0 + pre_gain.astype(F32))
    gained = jnp.concatenate([gained, high, squares - high], axis=1).astype(BF16)
    gained, weights = lax.optimization_barrier((gained, weights))
    columns = [weights]
    for step in (1, 2, 3):
        columns.append(lax.ppermute(weights, "x", [((i + step) % 4, i) for i in range(4)]))
    gained = everywhere(gained, GY, n_gy)
    gained = everywhere(gained, "c", 2)

    chip_rows = me // 2 * (2 * tok_rows)
    row_ids = chip_rows + jnp.arange(2 * tok_rows, dtype=jnp.int32)
    request = row_ids // NEWTOK
    owner_mask = request[:, None] == jnp.arange(REQS, dtype=jnp.int32)[None, :]
    position = jnp.sum(jnp.where(owner_mask, cached_len[None, :], 0), axis=1) + row_ids % NEWTOK
    half = HD // 2
    inverse = jnp.power(10000.0, -2.0 * jnp.arange(half, dtype=F32) / HD)
    angle = position.astype(F32)[:, None] * inverse[None, :]
    scale = jnp.where(core == 0, query_scale, 1.0).astype(F32)
    cosine, sine = jnp.cos(angle) * scale, jnp.sin(angle) * scale
    cosine = jnp.concatenate([cosine, cosine], axis=1)
    sine = jnp.concatenate([-sine, sine], axis=1)
    turns = jnp.stack([cosine, sine, jnp.where(core == 0, cosine, 1.0), jnp.where(core == 0, sine, 0.0)])
    meta = jnp.concatenate(
        [
            cached_len,
            new_len,
            slot_offset,
            jnp.stack([me * k_cache.shape[0], chip_rows, core, lax.axis_index("x")]).astype(jnp.int32),
        ]
    )
    mine = project(meta, gained, turns, columns)
    mine, w_out = lax.optimization_barrier((mine, w_out))
    mine = everywhere(mine, CHIPS, n_chips).reshape(-1, cols)
    others = lax.ppermute(mine, "c", [(0, 1), (1, 0)])

    k_pool, v_pool, sums = attend(meta, mine, others, k_cache, v_cache)

    both = lax.all_to_all(sums, "c", 0, 0)
    head = (both[0].astype(F32) + both[1].astype(F32)).astype(BF16)
    parts = lax.all_to_all(head.reshape(n_chips, -1, HD), CHIPS, 0, 0)
    attended = divide(meta, parts)
    attended = lax.all_gather(attended, "c", axis=0)
    attended = lax.dynamic_slice_in_dim(attended, core * tok_rows, tok_rows, 1)
    attended = jnp.swapaxes(attended, 0, 1).reshape(tok_rows, 2 * HD)

    partial_out = lax.dot_general(attended, w_out, (((1,), (1,)), ((), ())), preferred_element_type=F32)
    partial_out = jnp.swapaxes(partial_out.astype(BF16).reshape(tok_rows, n_gy, features), 0, 1)
    branch = jnp.sum(lax.all_to_all(partial_out, GY, 0, 0).astype(F32), axis=0)
    squares = jnp.sum(branch * branch, axis=1)
    mean = jnp.sum(everywhere(squares[None, :], GY, n_gy), axis=(0, 1)) / D
    layer_out = float_in + branch * lax.rsqrt(mean + epsilon)[:, None] * (1.0 + post_gain.astype(F32))
    return (layer_out.astype(BF16), k_pool, v_pool)


def solution(mesh):
    parts = Mesh(mesh.devices.reshape(4, 4, 2, 8, 2), GX + GY)
    both = P(GX, GY)
    placed = (both, P(GY), both, both, both, P(GY, GX), P(GY), both, both, P(), P(), P())
    return jax.shard_map(
        on_device, mesh=parts, in_specs=placed, out_specs=(both, both, both), check_vma=False
    )
```

```python
import jax
import jax.numpy as jnp
from jax import lax
from jax.experimental import pallas as pl
from jax.experimental.pallas import tpu as pltpu
from jax.sharding import Mesh, PartitionSpec as P

D = 4608
HD = 128
REQS = 12
NEWTOK = 192
TILE = 256
PIECE = 48
epsilon = 1e-06
soft_cap = 50.0
query_scale = 144.0 ** (-0.5)
F32 = jnp.float32
BF16 = jnp.bfloat16

CHIPS = ("zh", "x")
GX = ("zh", "x", "c")
GY = ("y", "zl")


def everywhere(value, axes, count):
    return lax.all_to_all(jnp.broadcast_to(value[None], (count,) + value.shape), axes, 0, 0)


def project_kernel(meta, mine, others, turns, own, right, ahead, behind, left, out):
    on_core_0 = meta[3 * REQS + 2] == 0
    here = meta[3 * REQS + 3]
    features = mine.shape[2] - 2
    count = 4
    total = jnp.zeros(out.shape, F32)
    squares = jnp.zeros((out.shape[0], 2), F32)
    for step in range(count):
        along = lax.rem(here + step, count)
        for block in range(count):
            at = block * count + along
            a, b = mine[at], others[at]
            rows = jnp.concatenate([jnp.where(on_core_0, a, b), jnp.where(on_core_0, b, a)], axis=0)
            squares += rows[:, features:].astype(F32)
            if step == 2:
                columns = ahead if block < 2 else behind
                low = block % 2 * features
            else:
                columns = (own, right, None, left)[step]
                low = block * features
            total += jnp.dot(rows[:, :features], columns[low : low + features, :], preferred_element_type=F32)
    mean = jnp.sum(squares, axis=1, keepdims=True) * (1.0 / D)
    total = total * lax.rsqrt(mean + epsilon)
    for head in range(2):
        value = total[:, head * HD : (head + 1) * HD]
        value = value * turns[2 * head] + pltpu.roll(value, HD // 2, 1) * turns[2 * head + 1]
        out[:, head * HD : (head + 1) * HD] = value.astype(BF16)


def project(meta, mine, others, turns, columns):
    vmem = pl.BlockSpec(memory_space=pltpu.VMEM)
    return pl.pallas_call(
        project_kernel,
        out_shape=jax.ShapeDtypeStruct((2 * mine.shape[1], columns[0].shape[1]), BF16),
        in_specs=[pl.BlockSpec(memory_space=pltpu.SMEM)] + [vmem] * (3 + len(columns)),
        out_specs=vmem,
        compiler_params=pltpu.CompilerParams(vmem_limit_bytes=32 << 20),
        name="project",
    )(meta, mine, others, turns, *columns)


def attend_kernel(meta, mine, others, k_old, v_old, k_pool, v_pool, sums, num, den, totals):
    slots = k_old.shape[0]
    tiles = slots // TILE
    first = meta[3 * REQS]
    queries_here = meta[3 * REQS + 2] == 0
    chunk = sums.shape[1] // (REQS * NEWTOK // (3 * PIECE))
    heads = sums.shape[0]

    def rows_of(r, on_core_0, on_core_1):
        here = pl.ds(pl.multiple_of(r * NEWTOK, 64), NEWTOK)
        return jnp.where(queries_here, on_core_0[here, :], on_core_1[here, :])

    k_pool[...] = k_old[...]
    v_pool[...] = v_old[...]
    totals[...] = jnp.zeros_like(totals)

    def write_request(r, carry):
        cached, fresh, offset = meta[r], meta[REQS + r], meta[2 * REQS + r]
        begin = offset + cached - first
        for t in range(tiles):

            @pl.when((begin < (t + 1) * TILE) & (begin + fresh > t * TILE))
            def _():
                rows = rows_of(r, others, mine)
                slot = lax.broadcasted_iota(jnp.int32, (TILE, NEWTOK), 0) + (t * TILE - begin)
                index = lax.broadcasted_iota(jnp.int32, (TILE, NEWTOK), 1)
                pick = jnp.where((slot == index) & (index < fresh), 1.0, 0.0).astype(BF16)
                new = jnp.dot(pick, rows, preferred_element_type=F32)
                place = lax.broadcasted_iota(jnp.int32, (TILE, HD), 0) + (t * TILE - begin)
                written = (place >= 0) & (place < fresh)
                here = pl.ds(t * TILE, TILE)
                k_pool[here, :] = jnp.where(written, new[:, :HD], k_pool[here, :].astype(F32)).astype(BF16)
                v_pool[here, :] = jnp.where(written, new[:, HD:], v_pool[here, :].astype(F32)).astype(BF16)

        return carry

    lax.fori_loop(0, REQS, write_request, 0)

    def read_request(r, carry):
        cached, fresh, offset = meta[r], meta[REQS + r], meta[2 * REQS + r]
        begin = offset - first
        end = begin + cached + fresh
        num[...] = jnp.zeros_like(num)
        den[...] = jnp.zeros_like(den)

        @pl.when((begin < slots) & (end > 0))
        def _():
            rows = rows_of(r, mine, others)
            rows = jnp.concatenate([rows[:, h * HD : (h + 1) * HD] for h in range(heads)], axis=0)
            row = lax.broadcasted_iota(jnp.int32, (heads * NEWTOK, 1), 0)
            row = jnp.where(row >= NEWTOK, row - NEWTOK, row)
            last = cached + jnp.minimum(row, fresh - 1) + begin
            for t in range(tiles):

                @pl.when((begin < (t + 1) * TILE) & (end > t * TILE))
                def _():
                    here = pl.ds(t * TILE, TILE)
                    logits = lax.dot_general(
                        rows, k_pool[here, :], (((1,), (1,)), ((), ())), preferred_element_type=F32
                    )
                    slot = lax.broadcasted_iota(jnp.int32, logits.shape, 1) + t * TILE
                    visible = (slot >= begin) & (slot <= last)
                    weight = jnp.exp(soft_cap * jnp.tanh(logits * (1.0 / soft_cap)))
                    weight = jnp.where(visible, weight, 0.0).astype(BF16)
                    num[...] += jnp.dot(weight, v_pool[here, :], preferred_element_type=F32)
                    den[...] += lax.dot_general(
                        jnp.ones((8, TILE), BF16), weight, (((1,), (1,)), ((), ())), preferred_element_type=F32
                    )

        for piece in range(NEWTOK // PIECE):
            at = r * (NEWTOK // PIECE) + piece
            block, part = at // 3, at % 3
            to = pl.multiple_of(block * chunk + part * PIECE, 16)
            for h in range(heads):
                low = h * NEWTOK + piece * PIECE
                sums[h, pl.ds(to, PIECE), :] = num[low : low + PIECE, :].astype(BF16)
                totals[h, pl.ds(block * 8 + part, 1), 0:PIECE] = den[0:1, low : low + PIECE]
        return carry

    lax.fori_loop(0, REQS, read_request, 0)
    for h in range(heads):
        for block in range(REQS * NEWTOK // (3 * PIECE)):
            rows = totals[h, block * 8 : block * 8 + 8, :]
            rows = jnp.concatenate([rows, jnp.zeros_like(rows)], axis=0)
            sums[h, block * chunk + 3 * PIECE : (block + 1) * chunk, :] = rows.astype(BF16)


def attend(meta, mine, others, k_cache, v_cache):
    heads = 2
    blocks = REQS * NEWTOK // (3 * PIECE)
    chunk = 3 * PIECE + 16
    vmem = pl.BlockSpec(memory_space=pltpu.VMEM)
    return pl.pallas_call(
        attend_kernel,
        out_shape=(
            jax.ShapeDtypeStruct(k_cache.shape, BF16),
            jax.ShapeDtypeStruct(v_cache.shape, BF16),
            jax.ShapeDtypeStruct((heads, blocks * chunk, HD), BF16),
        ),
        in_specs=[pl.BlockSpec(memory_space=pltpu.SMEM), vmem, vmem, vmem, vmem],
        out_specs=(vmem, vmem, vmem),
        scratch_shapes=[
            pltpu.VMEM((heads * NEWTOK, HD), F32),
            pltpu.VMEM((8, heads * NEWTOK), F32),
            pltpu.VMEM((heads, blocks * 8, HD), F32),
        ],
        compiler_params=pltpu.CompilerParams(vmem_limit_bytes=32 << 20),
        name="attend",
    )(meta, mine, others, k_cache, v_cache)


def divide_kernel(meta, parts, out):
    fresh_at = REQS
    begin = meta[3 * REQS + 1]
    total = jnp.sum(parts[...].astype(F32), axis=0)
    for part in range(3):
        row = begin + part * PIECE
        request = row // NEWTOK
        fresh = meta[fresh_at + request]
        within = lax.broadcasted_iota(jnp.int32, (PIECE, HD), 0) + (row - request * NEWTOK)
        den = total[3 * PIECE + part : 3 * PIECE + part + 1, 0:PIECE]
        diagonal = lax.broadcasted_iota(jnp.int32, (PIECE, PIECE), 0) == lax.broadcasted_iota(
            jnp.int32, (PIECE, PIECE), 1
        )
        den = jnp.sum(jnp.where(diagonal, den, 0.0), axis=1, keepdims=True)
        value = total[part * PIECE : (part + 1) * PIECE, :] / den
        out[part * PIECE : (part + 1) * PIECE, :] = jnp.where(within < fresh, value, 0.0).astype(BF16)


def divide(meta, parts):
    vmem = pl.BlockSpec(memory_space=pltpu.VMEM)
    return pl.pallas_call(
        divide_kernel,
        out_shape=jax.ShapeDtypeStruct((3 * PIECE, HD), BF16),
        in_specs=[pl.BlockSpec(memory_space=pltpu.SMEM), vmem],
        out_specs=vmem,
        compiler_params=pltpu.CompilerParams(vmem_limit_bytes=16 << 20),
        name="divide",
    )(meta, parts)


def on_device(
    tokens, pre_gain, w_q, w_k, w_v, w_o, post_gain, k_cache, v_cache, cached_len, new_len, slot_offset
):
    tok_rows = tokens.shape[0]
    features = tokens.shape[1]
    n_gy = lax.axis_size(GY)
    n_chips = lax.axis_size(CHIPS)
    me = lax.axis_index(GX)
    core = lax.axis_index("c")
    cols = w_q.shape[1]

    float_in = tokens.astype(F32)
    squares = jnp.sum(float_in * float_in, axis=1, keepdims=True)
    high = lax.reduce_precision(squares, 8, 7)
    gained = float_in * (1.0 + pre_gain.astype(F32))
    gained = jnp.concatenate([gained, high, squares - high], axis=1).astype(BF16)
    weights = jnp.concatenate([w_q, w_k, w_v], axis=1)
    gained, weights = lax.optimization_barrier((gained, weights))
    gained = everywhere(gained, GY, n_gy)
    w_out = lax.all_gather(w_o.T, GX, axis=0, tiled=True)

    weights = lax.all_gather(weights, "c", axis=0, tiled=True)
    weights = lax.dynamic_slice_in_dim(weights, core * cols, cols, 1)
    weights = lax.all_gather(weights, "zh", axis=0, tiled=True)
    from_right = [((i + 1) % 4, i) for i in range(4)]
    from_left = [((i - 1) % 4, i) for i in range(4)]
    right = lax.ppermute(weights, "x", from_right)
    left = lax.ppermute(weights, "x", from_left)
    middle = weights.shape[0] // 2
    columns = [
        weights,
        right,
        lax.ppermute(right[:middle], "x", from_right),
        lax.ppermute(left[middle:], "x", from_left),
        left,
    ]
    swap = [(0, 1), (1, 0)]
    other = lax.ppermute(gained, "c", swap)

    chip_rows = me // 2 * (2 * tok_rows)
    row_ids = chip_rows + jnp.arange(2 * tok_rows, dtype=jnp.int32)
    request = row_ids // NEWTOK
    owner_mask = request[:, None] == jnp.arange(REQS, dtype=jnp.int32)[None, :]
    position = jnp.sum(jnp.where(owner_mask, cached_len[None, :], 0), axis=1) + row_ids % NEWTOK
    half = HD // 2
    inverse = jnp.power(10000.0, -2.0 * jnp.arange(half, dtype=F32) / HD)
    angle = position.astype(F32)[:, None] * inverse[None, :]
    scale = jnp.where(core == 0, query_scale, 1.0).astype(F32)
    cosine, sine = jnp.cos(angle) * scale, jnp.sin(angle) * scale
    cosine = jnp.concatenate([cosine, cosine], axis=1)
    sine = jnp.concatenate([-sine, sine], axis=1)
    turns = jnp.stack([cosine, sine, jnp.where(core == 0, cosine, 1.0), jnp.where(core == 0, sine, 0.0)])
    meta = jnp.concatenate(
        [
            cached_len,
            new_len,
            slot_offset,
            jnp.stack([me * k_cache.shape[0], chip_rows, core, lax.axis_index("x")]).astype(jnp.int32),
        ]
    )
    mine = project(meta, gained, other, turns, columns)
    mine, w_out = lax.optimization_barrier((mine, w_out))
    mine = everywhere(mine, CHIPS, n_chips).reshape(-1, cols)
    others = lax.ppermute(mine, "c", swap)

    k_pool, v_pool, sums = attend(meta, mine, others, k_cache, v_cache)

    both = lax.all_to_all(sums, "c", 0, 0)
    head = (both[0].astype(F32) + both[1].astype(F32)).astype(BF16)
    parts = lax.all_to_all(head.reshape(n_chips, -1, HD), CHIPS, 0, 0)
    attended = divide(meta, parts)
    attended = lax.all_gather(attended, "c", axis=0)
    attended = lax.dynamic_slice_in_dim(attended, core * tok_rows, tok_rows, 1)
    attended = jnp.swapaxes(attended, 0, 1).reshape(tok_rows, 2 * HD)

    partial_out = lax.dot_general(attended, w_out, (((1,), (1,)), ((), ())), preferred_element_type=F32)
    partial_out = jnp.swapaxes(partial_out.astype(BF16).reshape(tok_rows, n_gy, features), 0, 1)
    branch = jnp.sum(lax.all_to_all(partial_out, GY, 0, 0).astype(F32), axis=0)
    squares = jnp.sum(branch * branch, axis=1)
    mean = jnp.sum(everywhere(squares[None, :], GY, n_gy), axis=(0, 1)) / D
    layer_out = float_in + branch * lax.rsqrt(mean + epsilon)[:, None] * (1.0 + post_gain.astype(F32))
    return (layer_out.astype(BF16), k_pool, v_pool)


def solution(mesh):
    parts = Mesh(mesh.devices.reshape(4, 4, 2, 8, 2), GX + GY)
    both = P(GX, GY)
    placed = (both, P(GY), both, both, both, P(GY, GX), P(GY), both, both, P(), P(), P())
    return jax.shard_map(
        on_device, mesh=parts, in_specs=placed, out_specs=(both, both, both), check_vma=False
    )
```

```python
import jax
import jax.numpy as jnp
from jax import lax
from jax.experimental import pallas as pl
from jax.experimental.pallas import tpu as pltpu
from jax.sharding import Mesh, PartitionSpec as P

D = 4608
HD = 128
REQS = 12
NEWTOK = 192
TILE = 256
PIECE = 48
epsilon = 1e-06
soft_cap = 50.0
query_scale = 144.0 ** (-0.5)
F32 = jnp.float32
BF16 = jnp.bfloat16

CHIPS = ("zh", "x")
GX = ("zh", "x", "c")
GY = ("y", "zl")


def everywhere(value, axes, count):
    return lax.all_to_all(jnp.broadcast_to(value[None], (count,) + value.shape), axes, 0, 0)


def project_kernel(meta, mine, others, turns, own, right, ahead, behind, left, out):
    on_core_0 = meta[3 * REQS + 2] == 0
    here = meta[3 * REQS + 3]
    features = mine.shape[2] - 2
    count = 4
    total = jnp.zeros(out.shape, F32)
    squares = jnp.zeros((out.shape[0], 2), F32)
    for step in range(count):
        along = lax.rem(here + step, count)
        for block in range(count):
            at = block * count + along
            a, b = mine[at], others[at]
            rows = jnp.concatenate([jnp.where(on_core_0, a, b), jnp.where(on_core_0, b, a)], axis=0)
            squares += rows[:, features:].astype(F32)
            if step == 2:
                columns = ahead if block < 2 else behind
                low = block % 2 * features
            else:
                columns = (own, right, None, left)[step]
                low = block * features
            total += jnp.dot(rows[:, :features], columns[low : low + features, :], preferred_element_type=F32)
    mean = jnp.sum(squares, axis=1, keepdims=True) * (1.0 / D)
    total = total * lax.rsqrt(mean + epsilon)
    for head in range(2):
        value = total[:, head * HD : (head + 1) * HD]
        value = value * turns[2 * head] + pltpu.roll(value, HD // 2, 1) * turns[2 * head + 1]
        out[:, head * HD : (head + 1) * HD] = value.astype(BF16)


def project(meta, mine, others, turns, columns):
    vmem = pl.BlockSpec(memory_space=pltpu.VMEM)
    return pl.pallas_call(
        project_kernel,
        out_shape=jax.ShapeDtypeStruct((2 * mine.shape[1], columns[0].shape[1]), BF16),
        in_specs=[pl.BlockSpec(memory_space=pltpu.SMEM)] + [vmem] * (3 + len(columns)),
        out_specs=vmem,
        compiler_params=pltpu.CompilerParams(vmem_limit_bytes=32 << 20),
        name="project",
    )(meta, mine, others, turns, *columns)


def attend_kernel(meta, mine, others, k_old, v_old, k_pool, v_pool, sums, num, den, totals):
    slots = k_old.shape[0]
    tiles = slots // TILE
    first = meta[3 * REQS]
    queries_here = meta[3 * REQS + 2] == 0
    chunk = sums.shape[1] // (REQS * NEWTOK // (3 * PIECE))
    heads = sums.shape[0]

    def rows_of(r, on_core_0, on_core_1):
        here = pl.ds(pl.multiple_of(r * NEWTOK, 64), NEWTOK)
        return jnp.where(queries_here, on_core_0[here, :], on_core_1[here, :])

    k_pool[...] = k_old[...]
    v_pool[...] = v_old[...]
    totals[...] = jnp.zeros_like(totals)

    def write_request(r, carry):
        cached, fresh, offset = meta[r], meta[REQS + r], meta[2 * REQS + r]
        begin = offset + cached - first
        for t in range(tiles):

            @pl.when((begin < (t + 1) * TILE) & (begin + fresh > t * TILE))
            def _():
                rows = rows_of(r, others, mine)
                slot = lax.broadcasted_iota(jnp.int32, (TILE, NEWTOK), 0) + (t * TILE - begin)
                index = lax.broadcasted_iota(jnp.int32, (TILE, NEWTOK), 1)
                pick = jnp.where((slot == index) & (index < fresh), 1.0, 0.0).astype(BF16)
                new = jnp.dot(pick, rows, preferred_element_type=F32)
                place = lax.broadcasted_iota(jnp.int32, (TILE, HD), 0) + (t * TILE - begin)
                written = (place >= 0) & (place < fresh)
                here = pl.ds(t * TILE, TILE)
                k_pool[here, :] = jnp.where(written, new[:, :HD], k_pool[here, :].astype(F32)).astype(BF16)
                v_pool[here, :] = jnp.where(written, new[:, HD:], v_pool[here, :].astype(F32)).astype(BF16)

        return carry

    lax.fori_loop(0, REQS, write_request, 0)

    def read_request(r, carry):
        cached, fresh, offset = meta[r], meta[REQS + r], meta[2 * REQS + r]
        begin = offset - first
        end = begin + cached + fresh
        num[...] = jnp.zeros_like(num)
        den[...] = jnp.zeros_like(den)

        @pl.when((begin < slots) & (end > 0))
        def _():
            rows = rows_of(r, mine, others)
            rows = jnp.concatenate([rows[:, h * HD : (h + 1) * HD] for h in range(heads)], axis=0)
            row = lax.broadcasted_iota(jnp.int32, (heads * NEWTOK, 1), 0)
            row = jnp.where(row >= NEWTOK, row - NEWTOK, row)
            last = cached + jnp.minimum(row, fresh - 1) + begin
            for t in range(tiles):

                @pl.when((begin < (t + 1) * TILE) & (end > t * TILE))
                def _():
                    here = pl.ds(t * TILE, TILE)
                    logits = lax.dot_general(
                        rows, k_pool[here, :], (((1,), (1,)), ((), ())), preferred_element_type=F32
                    )
                    slot = lax.broadcasted_iota(jnp.int32, logits.shape, 1) + t * TILE
                    visible = (slot >= begin) & (slot <= last)
                    weight = jnp.exp(soft_cap * jnp.tanh(logits * (1.0 / soft_cap)))
                    weight = jnp.where(visible, weight, 0.0).astype(BF16)
                    num[...] += jnp.dot(weight, v_pool[here, :], preferred_element_type=F32)
                    den[...] += lax.dot_general(
                        jnp.ones((8, TILE), BF16), weight, (((1,), (1,)), ((), ())), preferred_element_type=F32
                    )

        for piece in range(NEWTOK // PIECE):
            at = r * (NEWTOK // PIECE) + piece
            block, part = at // 3, at % 3
            to = pl.multiple_of(block * chunk + part * PIECE, 16)
            for h in range(heads):
                low = h * NEWTOK + piece * PIECE
                sums[h, pl.ds(to, PIECE), :] = num[low : low + PIECE, :].astype(BF16)
                totals[h, pl.ds(block * 8 + part, 1), 0:PIECE] = den[0:1, low : low + PIECE]
        return carry

    lax.fori_loop(0, REQS, read_request, 0)
    for h in range(heads):
        for block in range(REQS * NEWTOK // (3 * PIECE)):
            rows = totals[h, block * 8 : block * 8 + 8, :]
            rows = jnp.concatenate([rows, jnp.zeros_like(rows)], axis=0)
            sums[h, block * chunk + 3 * PIECE : (block + 1) * chunk, :] = rows.astype(BF16)


def attend(meta, mine, others, k_cache, v_cache):
    heads = 2
    blocks = REQS * NEWTOK // (3 * PIECE)
    chunk = 3 * PIECE + 16
    vmem = pl.BlockSpec(memory_space=pltpu.VMEM)
    return pl.pallas_call(
        attend_kernel,
        out_shape=(
            jax.ShapeDtypeStruct(k_cache.shape, BF16),
            jax.ShapeDtypeStruct(v_cache.shape, BF16),
            jax.ShapeDtypeStruct((heads, blocks * chunk, HD), BF16),
        ),
        in_specs=[pl.BlockSpec(memory_space=pltpu.SMEM), vmem, vmem, vmem, vmem],
        out_specs=(vmem, vmem, vmem),
        scratch_shapes=[
            pltpu.VMEM((heads * NEWTOK, HD), F32),
            pltpu.VMEM((8, heads * NEWTOK), F32),
            pltpu.VMEM((heads, blocks * 8, HD), F32),
        ],
        compiler_params=pltpu.CompilerParams(vmem_limit_bytes=32 << 20),
        name="attend",
    )(meta, mine, others, k_cache, v_cache)


def divide_kernel(meta, parts, out):
    fresh_at = REQS
    begin = meta[3 * REQS + 1]
    total = jnp.sum(parts[...].astype(F32), axis=0)
    for part in range(3):
        row = begin + part * PIECE
        request = row // NEWTOK
        fresh = meta[fresh_at + request]
        within = lax.broadcasted_iota(jnp.int32, (PIECE, HD), 0) + (row - request * NEWTOK)
        den = total[3 * PIECE + part : 3 * PIECE + part + 1, 0:PIECE]
        diagonal = lax.broadcasted_iota(jnp.int32, (PIECE, PIECE), 0) == lax.broadcasted_iota(
            jnp.int32, (PIECE, PIECE), 1
        )
        den = jnp.sum(jnp.where(diagonal, den, 0.0), axis=1, keepdims=True)
        value = total[part * PIECE : (part + 1) * PIECE, :] / den
        out[part * PIECE : (part + 1) * PIECE, :] = jnp.where(within < fresh, value, 0.0).astype(BF16)


def divide(meta, parts):
    vmem = pl.BlockSpec(memory_space=pltpu.VMEM)
    return pl.pallas_call(
        divide_kernel,
        out_shape=jax.ShapeDtypeStruct((3 * PIECE, HD), BF16),
        in_specs=[pl.BlockSpec(memory_space=pltpu.SMEM), vmem],
        out_specs=vmem,
        compiler_params=pltpu.CompilerParams(vmem_limit_bytes=16 << 20),
        name="divide",
    )(meta, parts)


def on_device(
    tokens, pre_gain, w_q, w_k, w_v, w_o, post_gain, k_cache, v_cache, cached_len, new_len, slot_offset
):
    tok_rows = tokens.shape[0]
    features = tokens.shape[1]
    n_gy = lax.axis_size(GY)
    n_chips = lax.axis_size(CHIPS)
    me = lax.axis_index(GX)
    core = lax.axis_index("c")
    cols = w_q.shape[1]

    float_in = tokens.astype(F32)
    squares = jnp.sum(float_in * float_in, axis=1, keepdims=True)
    high = lax.reduce_precision(squares, 8, 7)
    gained = float_in * (1.0 + pre_gain.astype(F32))
    gained = jnp.concatenate([gained, high, squares - high], axis=1).astype(BF16)
    weights = jnp.concatenate([w_q, w_k, w_v], axis=1)
    gained, weights = lax.optimization_barrier((gained, weights))
    gained = lax.all_gather(gained, "zl", axis=0, tiled=True)
    gained = everywhere(gained, "y", n_gy // 2).reshape(n_gy, tok_rows, -1)

    weights = lax.all_gather(weights, "c", axis=0, tiled=True)
    weights = lax.dynamic_slice_in_dim(weights, core * cols, cols, 1)
    weights = jnp.concatenate([weights, w_o.T], axis=0)
    weights = lax.all_gather(weights, "zh", axis=0)
    w_out = weights[:, 2 * w_q.shape[0] :, :]
    weights = weights[:, : 2 * w_q.shape[0], :].reshape(-1, cols)
    from_right = [((i + 1) % 4, i) for i in range(4)]
    from_left = [((i - 1) % 4, i) for i in range(4)]
    right = lax.ppermute(weights, "x", from_right)
    left = lax.ppermute(weights, "x", from_left)
    middle = weights.shape[0] // 2
    columns = [
        weights,
        right,
        lax.ppermute(right[:middle], "x", from_right),
        lax.ppermute(left[middle:], "x", from_left),
        left,
    ]
    swap = [(0, 1), (1, 0)]
    other = lax.ppermute(gained, "c", swap)

    chip_rows = me // 2 * (2 * tok_rows)
    row_ids = chip_rows + jnp.arange(2 * tok_rows, dtype=jnp.int32)
    request = row_ids // NEWTOK
    owner_mask = request[:, None] == jnp.arange(REQS, dtype=jnp.int32)[None, :]
    position = jnp.sum(jnp.where(owner_mask, cached_len[None, :], 0), axis=1) + row_ids % NEWTOK
    half = HD // 2
    inverse = jnp.power(10000.0, -2.0 * jnp.arange(half, dtype=F32) / HD)
    angle = position.astype(F32)[:, None] * inverse[None, :]
    scale = jnp.where(core == 0, query_scale, 1.0).astype(F32)
    cosine, sine = jnp.cos(angle) * scale, jnp.sin(angle) * scale
    cosine = jnp.concatenate([cosine, cosine], axis=1)
    sine = jnp.concatenate([-sine, sine], axis=1)
    turns = jnp.stack([cosine, sine, jnp.where(core == 0, cosine, 1.0), jnp.where(core == 0, sine, 0.0)])
    meta = jnp.concatenate(
        [
            cached_len,
            new_len,
            slot_offset,
            jnp.stack([me * k_cache.shape[0], chip_rows, core, lax.axis_index("x")]).astype(jnp.int32),
        ]
    )
    mine = project(meta, gained, other, turns, columns)
    mine, w_out = lax.optimization_barrier((mine, w_out))
    w_out = lax.all_gather(w_out, ("x", "c"), axis=0).reshape((4, 2) + w_out.shape)
    w_out = w_out.transpose(2, 0, 1, 3, 4).reshape(D, cols)
    mine = everywhere(mine, CHIPS, n_chips).reshape(-1, cols)
    others = lax.ppermute(mine, "c", swap)

    k_pool, v_pool, sums = attend(meta, mine, others, k_cache, v_cache)

    both = lax.all_to_all(sums, "c", 0, 0)
    head = (both[0].astype(F32) + both[1].astype(F32)).astype(BF16)
    parts = lax.all_to_all(head.reshape(n_chips, -1, HD), CHIPS, 0, 0)
    attended = divide(meta, parts)
    attended = lax.all_gather(attended, "c", axis=0)
    attended = lax.dynamic_slice_in_dim(attended, core * tok_rows, tok_rows, 1)
    attended = jnp.swapaxes(attended, 0, 1).reshape(tok_rows, 2 * HD)

    partial_out = lax.dot_general(attended, w_out, (((1,), (1,)), ((), ())), preferred_element_type=F32)
    partial_out = jnp.swapaxes(partial_out.astype(BF16).reshape(tok_rows, n_gy, features), 0, 1)
    branch = jnp.sum(lax.all_to_all(partial_out, GY, 0, 0).astype(F32), axis=0)
    squares = jnp.sum(branch * branch, axis=1)
    mean = jnp.sum(everywhere(squares[None, :], GY, n_gy), axis=(0, 1)) / D
    layer_out = float_in + branch * lax.rsqrt(mean + epsilon)[:, None] * (1.0 + post_gain.astype(F32))
    return (layer_out.astype(BF16), k_pool, v_pool)


def solution(mesh):
    parts = Mesh(mesh.devices.reshape(4, 4, 2, 8, 2), GX + GY)
    both = P(GX, GY)
    placed = (both, P(GY), both, both, both, P(GY, GX), P(GY), both, both, P(), P(), P())
    return jax.shard_map(
        on_device, mesh=parts, in_specs=placed, out_specs=(both, both, both), check_vma=False
    )
```

```python
import jax
import jax.numpy as jnp
from jax import lax
from jax.experimental import pallas as pl
from jax.experimental.pallas import tpu as pltpu
from jax.sharding import Mesh, PartitionSpec as P

D = 4608
HD = 128
REQS = 12
NEWTOK = 192
TILE = 256
PIECE = 48
epsilon = 1e-06
soft_cap = 50.0
query_scale = 144.0 ** (-0.5)
F32 = jnp.float32
BF16 = jnp.bfloat16

CHIPS = ("zh", "x")
GX = ("zh", "x", "c")
GY = ("y", "zl")


def everywhere(value, axes, count):
    return lax.all_to_all(jnp.broadcast_to(value[None], (count,) + value.shape), axes, 0, 0)


def project_kernel(meta, mine, others, turns, own, right, ahead, behind, left, out):
    on_core_0 = meta[3 * REQS + 2] == 0
    here = meta[3 * REQS + 3]
    features = mine.shape[2] - 2
    count = 4
    total = jnp.zeros(out.shape, F32)
    squares = jnp.zeros((out.shape[0], 2), F32)
    for step in range(count):
        along = lax.rem(here + step, count)
        for block in range(count):
            at = block * count + along
            a, b = mine[at], others[at]
            rows = jnp.concatenate([jnp.where(on_core_0, a, b), jnp.where(on_core_0, b, a)], axis=0)
            squares += rows[:, features:].astype(F32)
            if step == 2:
                columns = (ahead if block < 2 else behind)[block % 2]
            else:
                columns = (own, right, None, left)[step][block]
            total += jnp.dot(rows[:, :features], columns[:features, :], preferred_element_type=F32)
    mean = jnp.sum(squares, axis=1, keepdims=True) * (1.0 / D)
    total = total * lax.rsqrt(mean + epsilon)
    for head in range(2):
        value = total[:, head * HD : (head + 1) * HD]
        value = value * turns[2 * head] + pltpu.roll(value, HD // 2, 1) * turns[2 * head + 1]
        out[:, head * HD : (head + 1) * HD] = value.astype(BF16)


def project(meta, mine, others, turns, columns):
    vmem = pl.BlockSpec(memory_space=pltpu.VMEM)
    return pl.pallas_call(
        project_kernel,
        out_shape=jax.ShapeDtypeStruct((2 * mine.shape[1], columns[0].shape[2]), BF16),
        in_specs=[pl.BlockSpec(memory_space=pltpu.SMEM)] + [vmem] * (3 + len(columns)),
        out_specs=vmem,
        compiler_params=pltpu.CompilerParams(vmem_limit_bytes=32 << 20),
        name="project",
    )(meta, mine, others, turns, *columns)


def attend_kernel(meta, mine, others, k_old, v_old, k_pool, v_pool, sums, num, den, totals):
    slots = k_old.shape[0]
    tiles = slots // TILE
    first = meta[3 * REQS]
    queries_here = meta[3 * REQS + 2] == 0
    chunk = sums.shape[1] // (REQS * NEWTOK // (3 * PIECE))
    heads = sums.shape[0]

    def rows_of(r, on_core_0, on_core_1):
        here = pl.ds(pl.multiple_of(r * NEWTOK, 64), NEWTOK)
        return jnp.where(queries_here, on_core_0[here, :], on_core_1[here, :])

    k_pool[...] = k_old[...]
    v_pool[...] = v_old[...]
    totals[...] = jnp.zeros_like(totals)

    def write_request(r, carry):
        cached, fresh, offset = meta[r], meta[REQS + r], meta[2 * REQS + r]
        begin = offset + cached - first
        for t in range(tiles):

            @pl.when((begin < (t + 1) * TILE) & (begin + fresh > t * TILE))
            def _():
                rows = rows_of(r, others, mine)
                slot = lax.broadcasted_iota(jnp.int32, (TILE, NEWTOK), 0) + (t * TILE - begin)
                index = lax.broadcasted_iota(jnp.int32, (TILE, NEWTOK), 1)
                pick = jnp.where((slot == index) & (index < fresh), 1.0, 0.0).astype(BF16)
                new = jnp.dot(pick, rows, preferred_element_type=F32)
                place = lax.broadcasted_iota(jnp.int32, (TILE, HD), 0) + (t * TILE - begin)
                written = (place >= 0) & (place < fresh)
                here = pl.ds(t * TILE, TILE)
                k_pool[here, :] = jnp.where(written, new[:, :HD], k_pool[here, :].astype(F32)).astype(BF16)
                v_pool[here, :] = jnp.where(written, new[:, HD:], v_pool[here, :].astype(F32)).astype(BF16)

        return carry

    lax.fori_loop(0, REQS, write_request, 0)

    def read_request(r, carry):
        cached, fresh, offset = meta[r], meta[REQS + r], meta[2 * REQS + r]
        begin = offset - first
        end = begin + cached + fresh
        num[...] = jnp.zeros_like(num)
        den[...] = jnp.zeros_like(den)

        @pl.when((begin < slots) & (end > 0))
        def _():
            rows = rows_of(r, mine, others)
            rows = jnp.concatenate([rows[:, h * HD : (h + 1) * HD] for h in range(heads)], axis=0)
            row = lax.broadcasted_iota(jnp.int32, (heads * NEWTOK, 1), 0)
            row = jnp.where(row >= NEWTOK, row - NEWTOK, row)
            last = cached + jnp.minimum(row, fresh - 1) + begin
            for t in range(tiles):

                @pl.when((begin < (t + 1) * TILE) & (end > t * TILE))
                def _():
                    here = pl.ds(t * TILE, TILE)
                    logits = lax.dot_general(
                        rows, k_pool[here, :], (((1,), (1,)), ((), ())), preferred_element_type=F32
                    )
                    slot = lax.broadcasted_iota(jnp.int32, logits.shape, 1) + t * TILE
                    visible = (slot >= begin) & (slot <= last)
                    weight = jnp.exp(soft_cap * jnp.tanh(logits * (1.0 / soft_cap)))
                    weight = jnp.where(visible, weight, 0.0).astype(BF16)
                    num[...] += jnp.dot(weight, v_pool[here, :], preferred_element_type=F32)
                    den[...] += lax.dot_general(
                        jnp.ones((8, TILE), BF16), weight, (((1,), (1,)), ((), ())), preferred_element_type=F32
                    )

        for piece in range(NEWTOK // PIECE):
            at = r * (NEWTOK // PIECE) + piece
            block, part = at // 3, at % 3
            to = pl.multiple_of(block * chunk + part * PIECE, 16)
            for h in range(heads):
                low = h * NEWTOK + piece * PIECE
                sums[h, pl.ds(to, PIECE), :] = num[low : low + PIECE, :].astype(BF16)
                totals[h, pl.ds(block * 8 + part, 1), 0:PIECE] = den[0:1, low : low + PIECE]
        return carry

    lax.fori_loop(0, REQS, read_request, 0)
    for h in range(heads):
        for block in range(REQS * NEWTOK // (3 * PIECE)):
            rows = totals[h, block * 8 : block * 8 + 8, :]
            rows = jnp.concatenate([rows, jnp.zeros_like(rows)], axis=0)
            sums[h, block * chunk + 3 * PIECE : (block + 1) * chunk, :] = rows.astype(BF16)


def attend(meta, mine, others, k_cache, v_cache):
    heads = 2
    blocks = REQS * NEWTOK // (3 * PIECE)
    chunk = 3 * PIECE + 16
    vmem = pl.BlockSpec(memory_space=pltpu.VMEM)
    return pl.pallas_call(
        attend_kernel,
        out_shape=(
            jax.ShapeDtypeStruct(k_cache.shape, BF16),
            jax.ShapeDtypeStruct(v_cache.shape, BF16),
            jax.ShapeDtypeStruct((heads, blocks * chunk, HD), BF16),
        ),
        in_specs=[pl.BlockSpec(memory_space=pltpu.SMEM), vmem, vmem, vmem, vmem],
        out_specs=(vmem, vmem, vmem),
        scratch_shapes=[
            pltpu.VMEM((heads * NEWTOK, HD), F32),
            pltpu.VMEM((8, heads * NEWTOK), F32),
            pltpu.VMEM((heads, blocks * 8, HD), F32),
        ],
        compiler_params=pltpu.CompilerParams(vmem_limit_bytes=32 << 20),
        name="attend",
    )(meta, mine, others, k_cache, v_cache)


def divide_kernel(meta, parts, out):
    fresh_at = REQS
    begin = meta[3 * REQS + 1]
    total = jnp.sum(parts[...].astype(F32), axis=0)
    for part in range(3):
        row = begin + part * PIECE
        request = row // NEWTOK
        fresh = meta[fresh_at + request]
        within = lax.broadcasted_iota(jnp.int32, (PIECE, HD), 0) + (row - request * NEWTOK)
        den = total[3 * PIECE + part : 3 * PIECE + part + 1, 0:PIECE]
        diagonal = lax.broadcasted_iota(jnp.int32, (PIECE, PIECE), 0) == lax.broadcasted_iota(
            jnp.int32, (PIECE, PIECE), 1
        )
        den = jnp.sum(jnp.where(diagonal, den, 0.0), axis=1, keepdims=True)
        value = total[part * PIECE : (part + 1) * PIECE, :] / den
        out[part * PIECE : (part + 1) * PIECE, :] = jnp.where(within < fresh, value, 0.0).astype(BF16)


def divide(meta, parts):
    vmem = pl.BlockSpec(memory_space=pltpu.VMEM)
    return pl.pallas_call(
        divide_kernel,
        out_shape=jax.ShapeDtypeStruct((3 * PIECE, HD), BF16),
        in_specs=[pl.BlockSpec(memory_space=pltpu.SMEM), vmem],
        out_specs=vmem,
        compiler_params=pltpu.CompilerParams(vmem_limit_bytes=16 << 20),
        name="divide",
    )(meta, parts)


def spread_kernel(meta, attended, mine, others, out):
    on_core_0 = meta[3 * REQS + 2] == 0
    here = meta[3 * REQS + 3]
    count = 4
    rows = attended.shape[1] // 2
    heads = [jnp.where(on_core_0, attended[h, :rows], attended[h, rows:]) for h in range(attended.shape[0])]
    heads = jnp.concatenate(heads, axis=1)
    padded = jnp.concatenate([heads, jnp.zeros((HD - rows, heads.shape[1]), BF16)], axis=0)
    last = (((1,), (1,)), ((), ()))
    for step in range(count):
        along = lax.rem(here + step, count)
        for block in range(count):
            at = block * count + along
            a, b = mine[step * count + block], others[step * count + block]
            weights = jnp.concatenate([jnp.where(on_core_0, a, b), jnp.where(on_core_0, b, a)], axis=0)
            wide = lax.dot_general(heads, weights[: 2 * HD], last, preferred_element_type=F32)
            rest = lax.dot_general(weights[2 * HD :], padded, last, preferred_element_type=F32)
            out[at, :rows, :] = wide[:, :HD].astype(BF16)
            out[at, rows : 2 * rows, :] = wide[:, HD:].astype(BF16)
            out[at, 2 * rows :, :] = rest.astype(BF16)


def spread(meta, attended, mine, others, chunks):
    vmem = pl.BlockSpec(memory_space=pltpu.VMEM)
    rows = attended.shape[1] + 2 * mine.shape[1] - 2 * HD
    return pl.pallas_call(
        spread_kernel,
        out_shape=jax.ShapeDtypeStruct((chunks, rows, HD), BF16),
        in_specs=[pl.BlockSpec(memory_space=pltpu.SMEM)] + [vmem] * 3,
        out_specs=vmem,
        compiler_params=pltpu.CompilerParams(vmem_limit_bytes=32 << 20),
        name="spread",
    )(meta, attended, mine, others)


def on_device(
    tokens, pre_gain, w_q, w_k, w_v, w_o, post_gain, k_cache, v_cache, cached_len, new_len, slot_offset
):
    tok_rows = tokens.shape[0]
    features = tokens.shape[1]
    n_gy = lax.axis_size(GY)
    n_chips = lax.axis_size(CHIPS)
    me = lax.axis_index(GX)
    core = lax.axis_index("c")
    cols = w_q.shape[1]

    float_in = tokens.astype(F32)
    squares = jnp.sum(float_in * float_in, axis=1, keepdims=True)
    high = lax.reduce_precision(squares, 8, 7)
    gained = float_in * (1.0 + pre_gain.astype(F32))
    gained = jnp.concatenate([gained, high, squares - high], axis=1).astype(BF16)
    weights = jnp.concatenate([w_q, w_k, w_v], axis=1)
    weights = lax.all_gather(weights, "c", axis=0, tiled=True)
    weights = lax.dynamic_slice_in_dim(weights, core * cols, cols, 1)
    inner = weights.shape[0]
    weights = jnp.concatenate([weights, w_o.T], axis=0)
    weights = lax.all_gather(weights, "zh", axis=0)
    from_right = [((i + 1) % 4, i) for i in range(4)]
    from_left = [((i - 1) % 4, i) for i in range(4)]
    right = lax.ppermute(weights, "x", from_right)
    left = lax.ppermute(weights, "x", from_left)
    ahead = lax.ppermute(right[:2], "x", from_right)
    behind = lax.ppermute(left[2:], "x", from_left)
    columns = [weights, right, ahead, behind, left]
    w_out = jnp.concatenate([part[:, inner:, :] for part in columns], axis=0)
    swap = [(0, 1), (1, 0)]
    w_out_other = lax.ppermute(w_out, "c", swap)

    gained, weights = lax.optimization_barrier((gained, weights))
    gained = lax.all_gather(gained, "zl", axis=0, tiled=True)
    gained = everywhere(gained, "y", n_gy // 2).reshape(n_gy, tok_rows, -1)
    other = lax.ppermute(gained, "c", swap)

    chip_rows = me // 2 * (2 * tok_rows)
    row_ids = chip_rows + jnp.arange(2 * tok_rows, dtype=jnp.int32)
    request = row_ids // NEWTOK
    owner_mask = request[:, None] == jnp.arange(REQS, dtype=jnp.int32)[None, :]
    position = jnp.sum(jnp.where(owner_mask, cached_len[None, :], 0), axis=1) + row_ids % NEWTOK
    half = HD // 2
    inverse = jnp.power(10000.0, -2.0 * jnp.arange(half, dtype=F32) / HD)
    angle = position.astype(F32)[:, None] * inverse[None, :]
    scale = jnp.where(core == 0, query_scale, 1.0).astype(F32)
    cosine, sine = jnp.cos(angle) * scale, jnp.sin(angle) * scale
    cosine = jnp.concatenate([cosine, cosine], axis=1)
    sine = jnp.concatenate([-sine, sine], axis=1)
    turns = jnp.stack([cosine, sine, jnp.where(core == 0, cosine, 1.0), jnp.where(core == 0, sine, 0.0)])
    meta = jnp.concatenate(
        [
            cached_len,
            new_len,
            slot_offset,
            jnp.stack([me * k_cache.shape[0], chip_rows, core, lax.axis_index("x")]).astype(jnp.int32),
        ]
    )
    mine = project(meta, gained, other, turns, columns)
    mine = everywhere(mine, CHIPS, n_chips).reshape(-1, cols)
    others = lax.ppermute(mine, "c", swap)

    k_pool, v_pool, sums = attend(meta, mine, others, k_cache, v_cache)

    both = lax.all_to_all(sums, "c", 0, 0)
    head = (both[0].astype(F32) + both[1].astype(F32)).astype(BF16)
    parts = lax.all_to_all(head.reshape(n_chips, -1, HD), CHIPS, 0, 0)
    attended = divide(meta, parts)
    attended = lax.all_gather(attended, "c", axis=0)
    partial_out = spread(meta, attended, w_out, w_out_other, n_gy)
    total = jnp.sum(lax.all_to_all(partial_out, GY, 0, 0).astype(F32), axis=0)
    branch = jnp.concatenate(
        [total[:tok_rows], total[tok_rows : 2 * tok_rows], total[2 * tok_rows :, :tok_rows].T], axis=1
    )
    squares = jnp.sum(branch * branch, axis=1)
    mean = jnp.sum(everywhere(squares[None, :], GY, n_gy), axis=(0, 1)) / D
    layer_out = float_in + branch * lax.rsqrt(mean + epsilon)[:, None] * (1.0 + post_gain.astype(F32))
    return (layer_out.astype(BF16), k_pool, v_pool)


def solution(mesh):
    parts = Mesh(mesh.devices.reshape(4, 4, 2, 8, 2), GX + GY)
    both = P(GX, GY)
    placed = (both, P(GY), both, both, both, P(GY, GX), P(GY), both, both, P(), P(), P())
    return jax.shard_map(
        on_device, mesh=parts, in_specs=placed, out_specs=(both, both, both), check_vma=False
    )
```

```python
import jax
import jax.numpy as jnp
from jax import lax
from jax.experimental import pallas as pl
from jax.experimental.pallas import tpu as pltpu
from jax.sharding import Mesh, PartitionSpec as P

D = 4608
HD = 128
REQS = 12
NEWTOK = 192
TILE = 256
PIECE = 48
epsilon = 1e-06
soft_cap = 50.0
query_scale = 144.0 ** (-0.5)
F32 = jnp.float32
BF16 = jnp.bfloat16

CHIPS = ("zh", "x")
GX = ("zh", "x", "c")
GY = ("y", "zl")


def everywhere(value, axes, count):
    return lax.all_to_all(jnp.broadcast_to(value[None], (count,) + value.shape), axes, 0, 0)


def project_kernel(meta, mine, others, turns, own, right, ahead, behind, left, out):
    on_core_0 = meta[3 * REQS + 2] == 0
    here = meta[3 * REQS + 3]
    features = mine.shape[2] - 2
    count = 4
    total = jnp.zeros(out.shape, F32)
    squares = jnp.zeros((out.shape[0], 2), F32)
    for step in range(count):
        along = lax.rem(here + step, count)
        for block in range(count):
            at = block * count + along
            a, b = mine[at], others[at]
            rows = jnp.concatenate([jnp.where(on_core_0, a, b), jnp.where(on_core_0, b, a)], axis=0)
            squares += rows[:, features:].astype(F32)
            if step == 2:
                columns = (ahead if block < 2 else behind)[block % 2]
            else:
                columns = (own, right, None, left)[step][block]
            total += jnp.dot(rows[:, :features], columns[:features, :], preferred_element_type=F32)
    mean = jnp.sum(squares, axis=1, keepdims=True) * (1.0 / D)
    total = total * lax.rsqrt(mean + epsilon)
    for head in range(2):
        value = total[:, head * HD : (head + 1) * HD]
        value = value * turns[2 * head] + pltpu.roll(value, HD // 2, 1) * turns[2 * head + 1]
        out[:, head * HD : (head + 1) * HD] = value.astype(BF16)


def project(meta, mine, others, turns, columns):
    vmem = pl.BlockSpec(memory_space=pltpu.VMEM)
    return pl.pallas_call(
        project_kernel,
        out_shape=jax.ShapeDtypeStruct((2 * mine.shape[1], columns[0].shape[2]), BF16),
        in_specs=[pl.BlockSpec(memory_space=pltpu.SMEM)] + [vmem] * (3 + len(columns)),
        out_specs=vmem,
        compiler_params=pltpu.CompilerParams(vmem_limit_bytes=32 << 20),
        name="project",
    )(meta, mine, others, turns, *columns)


def attend_kernel(meta, mine, others, k_old, v_old, k_pool, v_pool, sums, num, den, totals):
    slots = k_old.shape[0]
    tiles = slots // TILE
    first = meta[3 * REQS]
    queries_here = meta[3 * REQS + 2] == 0
    chunk = sums.shape[1] // (REQS * NEWTOK // (3 * PIECE))
    heads = sums.shape[0]

    def rows_of(r, on_core_0, on_core_1):
        here = pl.ds(pl.multiple_of(r * NEWTOK, 64), NEWTOK)
        return jnp.where(queries_here, on_core_0[here, :], on_core_1[here, :])

    k_pool[...] = k_old[...]
    v_pool[...] = v_old[...]
    totals[...] = jnp.zeros_like(totals)

    def write_request(r, carry):
        cached, fresh, offset = meta[r], meta[REQS + r], meta[2 * REQS + r]
        begin = offset + cached - first
        for t in range(tiles):

            @pl.when((begin < (t + 1) * TILE) & (begin + fresh > t * TILE))
            def _():
                rows = rows_of(r, others, mine)
                slot = lax.broadcasted_iota(jnp.int32, (TILE, NEWTOK), 0) + (t * TILE - begin)
                index = lax.broadcasted_iota(jnp.int32, (TILE, NEWTOK), 1)
                pick = jnp.where((slot == index) & (index < fresh), 1.0, 0.0).astype(BF16)
                new = jnp.dot(pick, rows, preferred_element_type=F32)
                place = lax.broadcasted_iota(jnp.int32, (TILE, HD), 0) + (t * TILE - begin)
                written = (place >= 0) & (place < fresh)
                here = pl.ds(t * TILE, TILE)
                k_pool[here, :] = jnp.where(written, new[:, :HD], k_pool[here, :].astype(F32)).astype(BF16)
                v_pool[here, :] = jnp.where(written, new[:, HD:], v_pool[here, :].astype(F32)).astype(BF16)

        return carry

    lax.fori_loop(0, REQS, write_request, 0)

    def read_request(r, carry):
        cached, fresh, offset = meta[r], meta[REQS + r], meta[2 * REQS + r]
        begin = offset - first
        end = begin + cached + fresh
        num[...] = jnp.zeros_like(num)
        den[...] = jnp.zeros_like(den)

        @pl.when((begin < slots) & (end > 0))
        def _():
            rows = rows_of(r, mine, others)
            rows = jnp.concatenate([rows[:, h * HD : (h + 1) * HD] for h in range(heads)], axis=0)
            row = lax.broadcasted_iota(jnp.int32, (heads * NEWTOK, 1), 0)
            row = jnp.where(row >= NEWTOK, row - NEWTOK, row)
            last = cached + jnp.minimum(row, fresh - 1) + begin
            for t in range(tiles):

                @pl.when((begin < (t + 1) * TILE) & (end > t * TILE))
                def _():
                    here = pl.ds(t * TILE, TILE)
                    logits = lax.dot_general(
                        rows, k_pool[here, :], (((1,), (1,)), ((), ())), preferred_element_type=F32
                    )
                    slot = lax.broadcasted_iota(jnp.int32, logits.shape, 1) + t * TILE
                    visible = (slot >= begin) & (slot <= last)
                    weight = jnp.exp(soft_cap * jnp.tanh(logits * (1.0 / soft_cap)))
                    weight = jnp.where(visible, weight, 0.0).astype(BF16)
                    num[...] += jnp.dot(weight, v_pool[here, :], preferred_element_type=F32)
                    den[...] += lax.dot_general(
                        jnp.ones((8, TILE), BF16), weight, (((1,), (1,)), ((), ())), preferred_element_type=F32
                    )

        for piece in range(NEWTOK // PIECE):
            at = r * (NEWTOK // PIECE) + piece
            block, part = at // 3, at % 3
            to = pl.multiple_of(block * chunk + part * PIECE, 16)
            for h in range(heads):
                low = h * NEWTOK + piece * PIECE
                sums[h, pl.ds(to, PIECE), :] = num[low : low + PIECE, :].astype(BF16)
                totals[h, pl.ds(block * 8 + part, 1), 0:PIECE] = den[0:1, low : low + PIECE]
        return carry

    lax.fori_loop(0, REQS, read_request, 0)
    for h in range(heads):
        for block in range(REQS * NEWTOK // (3 * PIECE)):
            rows = totals[h, block * 8 : block * 8 + 8, :]
            rows = jnp.concatenate([rows, jnp.zeros_like(rows)], axis=0)
            sums[h, block * chunk + 3 * PIECE : (block + 1) * chunk, :] = rows.astype(BF16)


def attend(meta, mine, others, k_cache, v_cache):
    heads = 2
    blocks = REQS * NEWTOK // (3 * PIECE)
    chunk = 3 * PIECE + 16
    vmem = pl.BlockSpec(memory_space=pltpu.VMEM)
    return pl.pallas_call(
        attend_kernel,
        out_shape=(
            jax.ShapeDtypeStruct(k_cache.shape, BF16),
            jax.ShapeDtypeStruct(v_cache.shape, BF16),
            jax.ShapeDtypeStruct((heads, blocks * chunk, HD), BF16),
        ),
        in_specs=[pl.BlockSpec(memory_space=pltpu.SMEM), vmem, vmem, vmem, vmem],
        out_specs=(vmem, vmem, vmem),
        scratch_shapes=[
            pltpu.VMEM((heads * NEWTOK, HD), F32),
            pltpu.VMEM((8, heads * NEWTOK), F32),
            pltpu.VMEM((heads, blocks * 8, HD), F32),
        ],
        compiler_params=pltpu.CompilerParams(vmem_limit_bytes=32 << 20),
        name="attend",
    )(meta, mine, others, k_cache, v_cache)


def divide_kernel(meta, parts, out):
    fresh_at = REQS
    begin = meta[3 * REQS + 1]
    total = jnp.sum(parts[...].astype(F32), axis=0)
    for part in range(3):
        row = begin + part * PIECE
        request = row // NEWTOK
        fresh = meta[fresh_at + request]
        within = lax.broadcasted_iota(jnp.int32, (PIECE, HD), 0) + (row - request * NEWTOK)
        den = total[3 * PIECE + part : 3 * PIECE + part + 1, 0:PIECE]
        diagonal = lax.broadcasted_iota(jnp.int32, (PIECE, PIECE), 0) == lax.broadcasted_iota(
            jnp.int32, (PIECE, PIECE), 1
        )
        den = jnp.sum(jnp.where(diagonal, den, 0.0), axis=1, keepdims=True)
        value = total[part * PIECE : (part + 1) * PIECE, :] / den
        out[part * PIECE : (part + 1) * PIECE, :] = jnp.where(within < fresh, value, 0.0).astype(BF16)


def divide(meta, parts):
    vmem = pl.BlockSpec(memory_space=pltpu.VMEM)
    return pl.pallas_call(
        divide_kernel,
        out_shape=jax.ShapeDtypeStruct((3 * PIECE, HD), BF16),
        in_specs=[pl.BlockSpec(memory_space=pltpu.SMEM), vmem],
        out_specs=vmem,
        compiler_params=pltpu.CompilerParams(vmem_limit_bytes=16 << 20),
        name="divide",
    )(meta, parts)


def spread_kernel(meta, attended, own, right, ahead, behind, left, out):
    here = meta[3 * REQS + 3]
    count = 4
    rows = attended.shape[1]
    heads = jnp.concatenate([attended[h] for h in range(attended.shape[0])], axis=1)
    padded = jnp.concatenate([heads, jnp.zeros((2 * HD - rows, heads.shape[1]), BF16)], axis=0)
    last = (((1,), (1,)), ((), ()))
    for step in range(count):
        along = lax.rem(here + step, count)
        for block in range(count):
            at = block * count + along
            if step == 2:
                weights = (ahead if block < 2 else behind)[block % 2]
            else:
                weights = (own, right, None, left)[step][block]
            wide = lax.dot_general(heads, weights[:HD], last, preferred_element_type=F32)
            rest = lax.dot_general(weights[HD:], padded, last, preferred_element_type=F32)
            out[at, :rows, :] = wide.astype(BF16)
            out[at, rows : rows + 16, :] = rest[:, :HD].astype(BF16)
            out[at, rows + 16 :, :] = rest[:, HD:].astype(BF16)


def spread(meta, attended, columns, chunks):
    vmem = pl.BlockSpec(memory_space=pltpu.VMEM)
    return pl.pallas_call(
        spread_kernel,
        out_shape=jax.ShapeDtypeStruct((chunks, attended.shape[1] + 32, HD), BF16),
        in_specs=[pl.BlockSpec(memory_space=pltpu.SMEM)] + [vmem] * (1 + len(columns)),
        out_specs=vmem,
        compiler_params=pltpu.CompilerParams(vmem_limit_bytes=32 << 20),
        name="spread",
    )(meta, attended, *columns)


def on_device(
    tokens, pre_gain, w_q, w_k, w_v, w_o, post_gain, k_cache, v_cache, cached_len, new_len, slot_offset
):
    tok_rows = tokens.shape[0]
    features = tokens.shape[1]
    n_gy = lax.axis_size(GY)
    n_chips = lax.axis_size(CHIPS)
    me = lax.axis_index(GX)
    core = lax.axis_index("c")
    cols = w_q.shape[1]

    float_in = tokens.astype(F32)
    squares = jnp.sum(float_in * float_in, axis=1, keepdims=True)
    high = lax.reduce_precision(squares, 8, 7)
    gained = float_in * (1.0 + pre_gain.astype(F32))
    gained = jnp.concatenate([gained, high, squares - high], axis=1).astype(BF16)
    weights = jnp.concatenate([w_q, w_k, w_v], axis=1)
    gained, weights = lax.optimization_barrier((gained, weights))
    gained = lax.all_gather(gained, "zl", axis=0, tiled=True)
    gained = everywhere(gained, "y", n_gy // 2).reshape(n_gy, tok_rows, -1)

    weights = lax.all_gather(weights, "c", axis=0, tiled=True)
    weights = lax.dynamic_slice_in_dim(weights, core * cols, cols, 1)
    inner = weights.shape[0]
    weights = jnp.concatenate([weights, w_o.T], axis=0)
    weights = lax.all_gather(weights, "zh", axis=0)
    w_out = weights[:, inner:, :]
    weights = weights[:, :inner, :]
    from_right = [((i + 1) % 4, i) for i in range(4)]
    from_left = [((i - 1) % 4, i) for i in range(4)]
    right = lax.ppermute(weights, "x", from_right)
    left = lax.ppermute(weights, "x", from_left)
    ahead = lax.ppermute(right[:2], "x", from_right)
    behind = lax.ppermute(left[2:], "x", from_left)
    columns = [weights, right, ahead, behind, left]
    swap = [(0, 1), (1, 0)]
    other = lax.ppermute(gained, "c", swap)

    chip_rows = me // 2 * (2 * tok_rows)
    row_ids = chip_rows + jnp.arange(2 * tok_rows, dtype=jnp.int32)
    request = row_ids // NEWTOK
    owner_mask = request[:, None] == jnp.arange(REQS, dtype=jnp.int32)[None, :]
    position = jnp.sum(jnp.where(owner_mask, cached_len[None, :], 0), axis=1) + row_ids % NEWTOK
    half = HD // 2
    inverse = jnp.power(10000.0, -2.0 * jnp.arange(half, dtype=F32) / HD)
    angle = position.astype(F32)[:, None] * inverse[None, :]
    scale = jnp.where(core == 0, query_scale, 1.0).astype(F32)
    cosine, sine = jnp.cos(angle) * scale, jnp.sin(angle) * scale
    cosine = jnp.concatenate([cosine, cosine], axis=1)
    sine = jnp.concatenate([-sine, sine], axis=1)
    turns = jnp.stack([cosine, sine, jnp.where(core == 0, cosine, 1.0), jnp.where(core == 0, sine, 0.0)])
    meta = jnp.concatenate(
        [
            cached_len,
            new_len,
            slot_offset,
            jnp.stack([me * k_cache.shape[0], chip_rows, core, lax.axis_index("x")]).astype(jnp.int32),
        ]
    )
    mine = project(meta, gained, other, turns, columns)
    mine, w_out = lax.optimization_barrier((mine, w_out))
    out_right = lax.ppermute(w_out, "x", from_right)
    out_left = lax.ppermute(w_out, "x", from_left)
    mine = everywhere(mine, CHIPS, n_chips).reshape(-1, cols)
    mine, out_right, out_left = lax.optimization_barrier((mine, out_right, out_left))
    others = lax.ppermute(mine, "c", swap)
    out_columns = [
        w_out,
        out_right,
        lax.ppermute(out_right[:2], "x", from_right),
        lax.ppermute(out_left[2:], "x", from_left),
        out_left,
    ]

    k_pool, v_pool, sums = attend(meta, mine, others, k_cache, v_cache)

    both = lax.all_to_all(sums, "c", 0, 0)
    head = (both[0].astype(F32) + both[1].astype(F32)).astype(BF16)
    parts = lax.all_to_all(head.reshape(n_chips, -1, HD), CHIPS, 0, 0)
    attended = divide(meta, parts)
    attended = lax.all_gather(attended, "c", axis=0)
    partial_out = spread(meta, attended, out_columns, n_gy)
    total = jnp.sum(lax.all_to_all(partial_out, GY, 0, 0).astype(F32), axis=0)
    rows = 2 * tok_rows
    rest = jnp.concatenate([total[rows : rows + 16], total[rows + 16 :, : rows - HD]], axis=1)
    branch = jnp.concatenate([total[:rows], rest.T], axis=1)
    squares = jnp.sum(branch * branch, axis=1).reshape(2, 1, 1, tok_rows)
    squares = jnp.broadcast_to(squares, (2, n_gy, 1, tok_rows)).reshape(2 * n_gy, 1, tok_rows)
    squares = lax.all_to_all(squares, ("c",) + GY, 0, 0)
    mean = jnp.sum(squares, axis=(0, 1)) / D
    kept = lax.dynamic_slice_in_dim(branch, core * tok_rows, tok_rows, 0)
    sent = lax.dynamic_slice_in_dim(branch, (1 - core) * tok_rows, tok_rows, 0)
    came = lax.ppermute(sent, "c", swap)
    branch = jnp.concatenate([jnp.where(core == 0, kept, came), jnp.where(core == 0, came, kept)], axis=1)
    layer_out = float_in + branch * lax.rsqrt(mean + epsilon)[:, None] * (1.0 + post_gain.astype(F32))
    return (layer_out.astype(BF16), k_pool, v_pool)


def solution(mesh):
    parts = Mesh(mesh.devices.reshape(4, 4, 2, 8, 2), GX + GY)
    both = P(GX, GY)
    placed = (both, P(GY), both, both, both, P(GY, GX), P(GY), both, both, P(), P(), P())
    return jax.shard_map(
        on_device, mesh=parts, in_specs=placed, out_specs=(both, both, both), check_vma=False
    )
```

```python
import jax
import jax.numpy as jnp
from jax import lax
from jax.experimental import pallas as pl
from jax.experimental.pallas import tpu as pltpu
from jax.sharding import Mesh, PartitionSpec as P

D = 4608
HD = 128
REQS = 12
NEWTOK = 192
READ_TILE = 512
WRITE_TILE = 256
PIECE = 48
epsilon = 1e-06
soft_cap = 50.0
query_scale = 144.0 ** (-0.5)
F32 = jnp.float32
BF16 = jnp.bfloat16

CHIPS = ("zh", "x")
GX = ("zh", "x", "c")
GY = ("y", "zl")


def everywhere(value, axes, count):
    return lax.all_to_all(jnp.broadcast_to(value[None], (count,) + value.shape), axes, 0, 0)


def project_kernel(meta, mine, others, turns, own, right, ahead, behind, left, out):
    on_core_0 = meta[3 * REQS + 2] == 0
    here = meta[3 * REQS + 3]
    features = mine.shape[2] - 2
    count = 4
    total = jnp.zeros(out.shape, F32)
    squares = jnp.zeros((out.shape[0], 2), F32)
    for step in range(count):
        along = lax.rem(here + step, count)
        for block in range(count):
            at = block * count + along
            a, b = mine[at], others[at]
            rows = jnp.concatenate([jnp.where(on_core_0, a, b), jnp.where(on_core_0, b, a)], axis=0)
            squares += rows[:, features:].astype(F32)
            if step == 2:
                columns = (ahead if block < 2 else behind)[block % 2]
            else:
                columns = (own, right, None, left)[step][block]
            total += jnp.dot(rows[:, :features], columns[:features, :], preferred_element_type=F32)
    mean = jnp.sum(squares, axis=1, keepdims=True) * (1.0 / D)
    total = total * lax.rsqrt(mean + epsilon)
    for head in range(2):
        value = total[:, head * HD : (head + 1) * HD]
        value = value * turns[2 * head] + pltpu.roll(value, HD // 2, 1) * turns[2 * head + 1]
        out[:, head * HD : (head + 1) * HD] = value.astype(BF16)


def project(meta, mine, others, turns, columns):
    vmem = pl.BlockSpec(memory_space=pltpu.VMEM)
    return pl.pallas_call(
        project_kernel,
        out_shape=jax.ShapeDtypeStruct((2 * mine.shape[1], columns[0].shape[2]), BF16),
        in_specs=[pl.BlockSpec(memory_space=pltpu.SMEM)] + [vmem] * (3 + len(columns)),
        out_specs=vmem,
        compiler_params=pltpu.CompilerParams(vmem_limit_bytes=32 << 20),
        name="project",
    )(meta, mine, others, turns, *columns)


def attend_kernel(meta, mine, others, k_old, v_old, k_other, v_other, k_pool, v_pool, sums, keys, values, num, den, totals):
    own = k_old.shape[0]
    slots = keys.shape[0]
    first = meta[3 * REQS]
    core = meta[3 * REQS + 2]
    on_core_0 = core == 0
    blocks = REQS * NEWTOK // (3 * PIECE)
    chunk = sums.shape[0] // blocks

    my_slots = pl.ds(pl.multiple_of(core * own, own), own)
    other_slots = pl.ds(pl.multiple_of((1 - core) * own, own), own)
    keys[my_slots, :] = k_old[...]
    keys[other_slots, :] = k_other[...]
    values[my_slots, :] = v_old[...]
    values[other_slots, :] = v_other[...]
    totals[...] = jnp.zeros_like(totals)

    def write_request(r, carry):
        cached, fresh, offset = meta[r], meta[REQS + r], meta[2 * REQS + r]
        begin = offset + cached - first

        def write_tile(t, carry):
            rows = pl.ds(pl.multiple_of(r * NEWTOK, 64), NEWTOK)
            a, b = mine[rows, HD:], others[rows, :]
            rows = jnp.concatenate([jnp.where(on_core_0, a, b), jnp.where(on_core_0, b, a)], axis=1)
            slot = lax.broadcasted_iota(jnp.int32, (WRITE_TILE, NEWTOK), 0) + (t * WRITE_TILE - begin)
            index = lax.broadcasted_iota(jnp.int32, (WRITE_TILE, NEWTOK), 1)
            pick = jnp.where((slot == index) & (index < fresh), 1.0, 0.0).astype(BF16)
            new = jnp.dot(pick, rows, preferred_element_type=F32)
            place = lax.broadcasted_iota(jnp.int32, (WRITE_TILE, HD), 0) + (t * WRITE_TILE - begin)
            written = (place >= 0) & (place < fresh)
            here = pl.ds(pl.multiple_of(t * WRITE_TILE, WRITE_TILE), WRITE_TILE)
            keys[here, :] = jnp.where(written, new[:, :HD], keys[here, :].astype(F32)).astype(BF16)
            values[here, :] = jnp.where(written, new[:, HD:], values[here, :].astype(F32)).astype(BF16)
            return carry

        low, high = jnp.maximum(begin, 0), jnp.minimum(begin + fresh, slots)
        tiles = jnp.where(high > low, pl.cdiv(high, WRITE_TILE), 0)
        lax.fori_loop(lax.div(low, WRITE_TILE), tiles, write_tile, 0)
        return carry

    lax.fori_loop(0, REQS, write_request, 0)
    k_pool[...] = keys[my_slots, :]
    v_pool[...] = values[my_slots, :]

    def read_request(r, carry):
        cached, fresh, offset = meta[r], meta[REQS + r], meta[2 * REQS + r]
        begin = offset - first
        end = begin + cached + fresh
        num[...] = jnp.zeros_like(num)
        den[...] = jnp.zeros_like(den)

        def read_tile(t, carry):
            rows = mine[pl.ds(pl.multiple_of(r * NEWTOK, 64), NEWTOK), :HD]
            row = lax.broadcasted_iota(jnp.int32, (NEWTOK, 1), 0)
            last = cached + jnp.minimum(row, fresh - 1) + begin
            here = pl.ds(pl.multiple_of(t * READ_TILE, READ_TILE), READ_TILE)
            logits = lax.dot_general(rows, keys[here, :], (((1,), (1,)), ((), ())), preferred_element_type=F32)
            slot = lax.broadcasted_iota(jnp.int32, logits.shape, 1) + t * READ_TILE
            visible = (slot >= begin) & (slot <= last)
            weight = jnp.exp(soft_cap * jnp.tanh(logits * (1.0 / soft_cap)))
            weight = jnp.where(visible, weight, 0.0).astype(BF16)
            num[...] += jnp.dot(weight, values[here, :], preferred_element_type=F32)
            den[...] += lax.dot_general(
                jnp.ones((8, READ_TILE), BF16), weight, (((1,), (1,)), ((), ())), preferred_element_type=F32
            )
            return carry

        low, high = jnp.maximum(begin, 0), jnp.minimum(end, slots)
        tiles = jnp.where(high > low, pl.cdiv(high, READ_TILE), 0)
        lax.fori_loop(lax.div(low, READ_TILE), tiles, read_tile, 0)

        for piece in range(NEWTOK // PIECE):
            at = r * (NEWTOK // PIECE) + piece
            block, part = lax.div(at, 3), lax.rem(at, 3)
            to = pl.multiple_of(block * chunk + part * PIECE, 16)
            at_row = piece * PIECE
            sums[pl.ds(to, PIECE), :] = num[at_row : at_row + PIECE, :].astype(BF16)
            totals[pl.ds(block * 8 + part, 1), 0:PIECE] = den[0:1, at_row : at_row + PIECE]
        return carry

    lax.fori_loop(0, REQS, read_request, 0)
    for block in range(blocks):
        rows = totals[block * 8 : block * 8 + 8, :]
        rows = jnp.concatenate([rows, jnp.zeros_like(rows)], axis=0)
        sums[block * chunk + 3 * PIECE : (block + 1) * chunk, :] = rows.astype(BF16)


def attend(meta, mine, others, k_cache, v_cache, k_other, v_other):
    blocks = REQS * NEWTOK // (3 * PIECE)
    chunk = 3 * PIECE + 16
    vmem = pl.BlockSpec(memory_space=pltpu.VMEM)
    slots = 2 * k_cache.shape[0]
    return pl.pallas_call(
        attend_kernel,
        out_shape=(
            jax.ShapeDtypeStruct(k_cache.shape, BF16),
            jax.ShapeDtypeStruct(v_cache.shape, BF16),
            jax.ShapeDtypeStruct((blocks * chunk, HD), BF16),
        ),
        in_specs=[pl.BlockSpec(memory_space=pltpu.SMEM)] + [vmem] * 6,
        out_specs=(vmem, vmem, vmem),
        scratch_shapes=[
            pltpu.VMEM((slots, HD), BF16),
            pltpu.VMEM((slots, HD), BF16),
            pltpu.VMEM((NEWTOK, HD), F32),
            pltpu.VMEM((8, NEWTOK), F32),
            pltpu.VMEM((blocks * 8, HD), F32),
        ],
        compiler_params=pltpu.CompilerParams(vmem_limit_bytes=32 << 20),
        name="attend",
    )(meta, mine, others, k_cache, v_cache, k_other, v_other)


def divide_kernel(meta, parts, out):
    fresh_at = REQS
    begin = meta[3 * REQS + 1]
    total = jnp.sum(parts[...].astype(F32), axis=0)
    for part in range(3):
        row = begin + part * PIECE
        request = row // NEWTOK
        fresh = meta[fresh_at + request]
        within = lax.broadcasted_iota(jnp.int32, (PIECE, HD), 0) + (row - request * NEWTOK)
        den = total[3 * PIECE + part : 3 * PIECE + part + 1, 0:PIECE]
        diagonal = lax.broadcasted_iota(jnp.int32, (PIECE, PIECE), 0) == lax.broadcasted_iota(
            jnp.int32, (PIECE, PIECE), 1
        )
        den = jnp.sum(jnp.where(diagonal, den, 0.0), axis=1, keepdims=True)
        value = total[part * PIECE : (part + 1) * PIECE, :] / den
        out[part * PIECE : (part + 1) * PIECE, :] = jnp.where(within < fresh, value, 0.0).astype(BF16)


def divide(meta, parts):
    vmem = pl.BlockSpec(memory_space=pltpu.VMEM)
    return pl.pallas_call(
        divide_kernel,
        out_shape=jax.ShapeDtypeStruct((3 * PIECE, HD), BF16),
        in_specs=[pl.BlockSpec(memory_space=pltpu.SMEM), vmem],
        out_specs=vmem,
        compiler_params=pltpu.CompilerParams(vmem_limit_bytes=16 << 20),
        name="divide",
    )(meta, parts)


def spread_kernel(meta, attended, own, right, ahead, behind, left, out):
    here = meta[3 * REQS + 3]
    count = 4
    rows = attended.shape[1]
    heads = jnp.concatenate([attended[h] for h in range(attended.shape[0])], axis=1)
    padded = jnp.concatenate([heads, jnp.zeros((2 * HD - rows, heads.shape[1]), BF16)], axis=0)
    last = (((1,), (1,)), ((), ()))
    for step in range(count):
        along = lax.rem(here + step, count)
        for block in range(count):
            at = block * count + along
            if step == 2:
                weights = (ahead if block < 2 else behind)[block % 2]
            else:
                weights = (own, right, None, left)[step][block]
            wide = lax.dot_general(heads, weights[:HD], last, preferred_element_type=F32)
            rest = lax.dot_general(weights[HD:], padded, last, preferred_element_type=F32)
            out[at, :rows, :] = wide.astype(BF16)
            out[at, rows : rows + 16, :] = rest[:, :HD].astype(BF16)
            out[at, rows + 16 :, :] = rest[:, HD:].astype(BF16)


def spread(meta, attended, columns, chunks):
    vmem = pl.BlockSpec(memory_space=pltpu.VMEM)
    return pl.pallas_call(
        spread_kernel,
        out_shape=jax.ShapeDtypeStruct((chunks, attended.shape[1] + 32, HD), BF16),
        in_specs=[pl.BlockSpec(memory_space=pltpu.SMEM)] + [vmem] * (1 + len(columns)),
        out_specs=vmem,
        compiler_params=pltpu.CompilerParams(vmem_limit_bytes=32 << 20),
        name="spread",
    )(meta, attended, *columns)


def on_device(
    tokens, pre_gain, w_q, w_k, w_v, w_o, post_gain, k_cache, v_cache, cached_len, new_len, slot_offset
):
    tok_rows = tokens.shape[0]
    features = tokens.shape[1]
    n_gy = lax.axis_size(GY)
    n_chips = lax.axis_size(CHIPS)
    me = lax.axis_index(GX)
    core = lax.axis_index("c")
    cols = w_q.shape[1]

    float_in = tokens.astype(F32)
    squares = jnp.sum(float_in * float_in, axis=1, keepdims=True)
    high = lax.reduce_precision(squares, 8, 7)
    gained = float_in * (1.0 + pre_gain.astype(F32))
    gained = jnp.concatenate([gained, high, squares - high], axis=1).astype(BF16)
    weights = jnp.concatenate([w_q[:, :HD], w_k, w_q[:, HD:], w_v], axis=1)
    gained, weights = lax.optimization_barrier((gained, weights))
    gained = lax.all_gather(gained, "zl", axis=0, tiled=True)
    gained = everywhere(gained, "y", n_gy // 2).reshape(n_gy, tok_rows, -1)

    weights = lax.all_gather(weights, "c", axis=0, tiled=True)
    weights = lax.dynamic_slice_in_dim(weights, core * cols, cols, 1)
    inner = weights.shape[0]
    weights = jnp.concatenate([weights, w_o.T], axis=0)
    weights = lax.all_gather(weights, "zh", axis=0)
    w_out = weights[:, inner:, :]
    weights = weights[:, :inner, :]
    from_right = [((i + 1) % 4, i) for i in range(4)]
    from_left = [((i - 1) % 4, i) for i in range(4)]
    right = lax.ppermute(weights, "x", from_right)
    left = lax.ppermute(weights, "x", from_left)
    ahead = lax.ppermute(right[:2], "x", from_right)
    behind = lax.ppermute(left[2:], "x", from_left)
    columns = [weights, right, ahead, behind, left]
    swap = [(0, 1), (1, 0)]
    other = lax.ppermute(gained, "c", swap)

    chip_rows = me // 2 * (2 * tok_rows)
    row_ids = chip_rows + jnp.arange(2 * tok_rows, dtype=jnp.int32)
    request = row_ids // NEWTOK
    owner_mask = request[:, None] == jnp.arange(REQS, dtype=jnp.int32)[None, :]
    position = jnp.sum(jnp.where(owner_mask, cached_len[None, :], 0), axis=1) + row_ids % NEWTOK
    half = HD // 2
    inverse = jnp.power(10000.0, -2.0 * jnp.arange(half, dtype=F32) / HD)
    angle = position.astype(F32)[:, None] * inverse[None, :]
    cosine, sine = jnp.cos(angle), jnp.sin(angle)
    cosine = jnp.concatenate([cosine, cosine], axis=1)
    sine = jnp.concatenate([-sine, sine], axis=1)
    turns = jnp.stack(
        [
            cosine * query_scale,
            sine * query_scale,
            jnp.where(core == 0, cosine, 1.0),
            jnp.where(core == 0, sine, 0.0),
        ]
    )
    meta = jnp.concatenate(
        [
            cached_len,
            new_len,
            slot_offset,
            jnp.stack([me // 2 * (2 * k_cache.shape[0]), chip_rows, core, lax.axis_index("x")]).astype(jnp.int32),
        ]
    )
    mine = project(meta, gained, other, turns, columns)
    mine, w_out = lax.optimization_barrier((mine, w_out))
    out_right = lax.ppermute(w_out, "x", from_right)
    out_left = lax.ppermute(w_out, "x", from_left)
    mine = everywhere(mine, CHIPS, n_chips).reshape(-1, cols)
    k_other = lax.ppermute(k_cache, "c", swap)
    v_other = lax.ppermute(v_cache, "c", swap)
    mine, out_right, out_left, k_other, v_other = lax.optimization_barrier(
        (mine, out_right, out_left, k_other, v_other)
    )
    others = lax.ppermute(mine[:, HD:], "c", swap)
    out_columns = [
        w_out,
        out_right,
        lax.ppermute(out_right[:2], "x", from_right),
        lax.ppermute(out_left[2:], "x", from_left),
        out_left,
    ]

    k_pool, v_pool, sums = attend(meta, mine, others, k_cache, v_cache, k_other, v_other)
    parts = lax.all_to_all(sums.reshape(n_chips, -1, HD), CHIPS, 0, 0)
    attended = divide(meta, parts)
    attended = lax.all_gather(attended, "c", axis=0)
    partial_out = spread(meta, attended, out_columns, n_gy)
    total = jnp.sum(lax.all_to_all(partial_out, GY, 0, 0).astype(F32), axis=0)
    rows = 2 * tok_rows
    rest = jnp.concatenate([total[rows : rows + 16], total[rows + 16 :, : rows - HD]], axis=1)
    branch = jnp.concatenate([total[:rows], rest.T], axis=1)
    squares = jnp.sum(branch * branch, axis=1).reshape(2, 1, 1, tok_rows)
    squares = jnp.broadcast_to(squares, (2, n_gy, 1, tok_rows)).reshape(2 * n_gy, 1, tok_rows)
    squares = lax.all_to_all(squares, ("c",) + GY, 0, 0)
    mean = jnp.sum(squares, axis=(0, 1)) / D
    kept = lax.dynamic_slice_in_dim(branch, core * tok_rows, tok_rows, 0)
    sent = lax.dynamic_slice_in_dim(branch, (1 - core) * tok_rows, tok_rows, 0)
    came = lax.ppermute(sent, "c", swap)
    branch = jnp.concatenate([jnp.where(core == 0, kept, came), jnp.where(core == 0, came, kept)], axis=1)
    layer_out = float_in + branch * lax.rsqrt(mean + epsilon)[:, None] * (1.0 + post_gain.astype(F32))
    return (layer_out.astype(BF16), k_pool, v_pool)


def solution(mesh):
    parts = Mesh(mesh.devices.reshape(4, 4, 2, 8, 2), GX + GY)
    both = P(GX, GY)
    placed = (both, P(GY), both, both, both, P(GY, GX), P(GY), both, both, P(), P(), P())
    return jax.shard_map(
        on_device, mesh=parts, in_specs=placed, out_specs=(both, both, both), check_vma=False
    )
```

```python
import jax
import jax.numpy as jnp
from jax import lax
from jax.experimental import pallas as pl
from jax.experimental.pallas import tpu as pltpu
from jax.sharding import Mesh, PartitionSpec as P

D = 4608
HD = 128
REQS = 12
NEWTOK = 192
READ_TILE = 512
WRITE_TILE = 256
PIECE = 48
epsilon = 1e-06
soft_cap = 50.0
query_scale = 144.0 ** (-0.5)
F32 = jnp.float32
BF16 = jnp.bfloat16

CHIPS = ("zh", "x")
GX = ("zh", "x", "c")
GY = ("y", "zl")


def everywhere(value, axes, count):
    return lax.all_to_all(jnp.broadcast_to(value[None], (count,) + value.shape), axes, 0, 0)


def project_kernel(meta, mine, others, turns, own, right, ahead, behind, left, *outs):
    on_core_0 = meta[3 * REQS + 2] == 0
    here = meta[3 * REQS + 3]
    features = mine.shape[2] - 2
    count = 4
    total = jnp.zeros((outs[0].shape[0], 2 * HD), F32)
    squares = jnp.zeros((outs[0].shape[0], 2), F32)
    for step in range(count):
        along = lax.rem(here + step, count)
        for block in range(count):
            at = block * count + along
            a, b = mine[at], others[at]
            rows = jnp.concatenate([jnp.where(on_core_0, a, b), jnp.where(on_core_0, b, a)], axis=0)
            squares += rows[:, features:].astype(F32)
            if step == 2:
                columns = (ahead if block < 2 else behind)[block % 2]
            else:
                columns = (own, right, None, left)[step][block]
            total += jnp.dot(rows[:, :features], columns[:features, :], preferred_element_type=F32)
    mean = jnp.sum(squares, axis=1, keepdims=True) * (1.0 / D)
    total = total * lax.rsqrt(mean + epsilon)
    for head in range(2):
        value = total[:, head * HD : (head + 1) * HD]
        value = value * turns[2 * head] + pltpu.roll(value, HD // 2, 1) * turns[2 * head + 1]
        outs[head][...] = value.astype(BF16)


def project(meta, mine, others, turns, columns):
    vmem = pl.BlockSpec(memory_space=pltpu.VMEM)
    return pl.pallas_call(
        project_kernel,
        out_shape=[jax.ShapeDtypeStruct((2 * mine.shape[1], HD), BF16)] * 2,
        in_specs=[pl.BlockSpec(memory_space=pltpu.SMEM)] + [vmem] * (3 + len(columns)),
        out_specs=[vmem, vmem],
        compiler_params=pltpu.CompilerParams(vmem_limit_bytes=32 << 20),
        name="project",
    )(meta, mine, others, turns, *columns)


def attend_kernel(meta, queries, k_own, v_own, k_other, v_other, sums, num, den, totals):
    own = k_own.shape[0]
    first = meta[3 * REQS]
    core = meta[3 * REQS + 2]
    blocks = REQS * NEWTOK // (3 * PIECE)
    chunk = sums.shape[0] // blocks
    totals[...] = jnp.zeros_like(totals)

    def read_request(r, carry):
        cached, offset = meta[r], meta[2 * REQS + r]
        num[...] = jnp.zeros_like(num)
        den[...] = jnp.zeros_like(den)
        for keys, values, at in ((k_own, v_own, core), (k_other, v_other, 1 - core)):
            begin = offset - first - at * own
            low, high = jnp.maximum(begin, 0), jnp.minimum(begin + cached, own)

            def read_tile(t, carry):
                rows = queries[pl.ds(pl.multiple_of(r * NEWTOK, 64), NEWTOK), :]
                here = pl.ds(pl.multiple_of(t * READ_TILE, READ_TILE), READ_TILE)
                logits = lax.dot_general(
                    rows, keys[here, :], (((1,), (1,)), ((), ())), preferred_element_type=F32
                )
                slot = lax.broadcasted_iota(jnp.int32, logits.shape, 1) + t * READ_TILE
                weight = jnp.exp(soft_cap * jnp.tanh(logits * (1.0 / soft_cap)))
                weight = jnp.where((slot >= low) & (slot < high), weight, 0.0).astype(BF16)
                num[...] += jnp.dot(weight, values[here, :], preferred_element_type=F32)
                den[...] += lax.dot_general(
                    jnp.ones((8, READ_TILE), BF16), weight, (((1,), (1,)), ((), ())), preferred_element_type=F32
                )
                return carry

            tiles = jnp.where(high > low, pl.cdiv(high, READ_TILE), 0)
            lax.fori_loop(lax.div(low, READ_TILE), tiles, read_tile, 0)

        for piece in range(NEWTOK // PIECE):
            at = r * (NEWTOK // PIECE) + piece
            block, part = lax.div(at, 3), lax.rem(at, 3)
            to = pl.multiple_of(block * chunk + part * PIECE, 16)
            at_row = piece * PIECE
            sums[pl.ds(to, PIECE), :] = num[at_row : at_row + PIECE, :].astype(BF16)
            totals[pl.ds(block * 8 + part, 1), 0:PIECE] = den[0:1, at_row : at_row + PIECE]
        return carry

    lax.fori_loop(0, REQS, read_request, 0)
    for block in range(blocks):
        rows = totals[block * 8 : block * 8 + 8, :]
        rows = jnp.concatenate([rows, jnp.zeros_like(rows)], axis=0)
        sums[block * chunk + 3 * PIECE : (block + 1) * chunk, :] = rows.astype(BF16)


def attend(meta, queries, k_cache, v_cache, k_other, v_other):
    blocks = REQS * NEWTOK // (3 * PIECE)
    chunk = 3 * PIECE + 16
    vmem = pl.BlockSpec(memory_space=pltpu.VMEM)
    return pl.pallas_call(
        attend_kernel,
        out_shape=jax.ShapeDtypeStruct((blocks * chunk, HD), BF16),
        in_specs=[pl.BlockSpec(memory_space=pltpu.SMEM)] + [vmem] * 5,
        out_specs=vmem,
        scratch_shapes=[
            pltpu.VMEM((NEWTOK, HD), F32),
            pltpu.VMEM((8, NEWTOK), F32),
            pltpu.VMEM((blocks * 8, HD), F32),
        ],
        compiler_params=pltpu.CompilerParams(vmem_limit_bytes=32 << 20),
        name="attend",
    )(meta, queries, k_cache, v_cache, k_other, v_other)


def attend_new_kernel(meta, queries, fresh_rows, num, den):
    here = meta[3 * REQS + 3]
    rows, count = queries.shape[0], fresh_rows.shape[0] // 2
    request = lax.div(meta[3 * REQS + 1] - here * rows, NEWTOK)
    row = lax.broadcasted_iota(jnp.int32, (rows, 1), 0) + here * rows
    start, limit = jnp.zeros_like(row), jnp.zeros_like(row)
    for part in range(count * rows // NEWTOK):
        at = part * NEWTOK
        inside = (row >= at) & (row < at + NEWTOK)
        start = jnp.where(inside, at, start)
        limit = jnp.where(inside, jnp.minimum(row, at + meta[REQS + request + part] - 1), limit)
    keys = jnp.concatenate([fresh_rows[2 * step] for step in range(count)], axis=0)
    values = jnp.concatenate([fresh_rows[2 * step + 1] for step in range(count)], axis=0)
    logits = lax.dot_general(queries[...], keys, (((1,), (1,)), ((), ())), preferred_element_type=F32)
    column = lax.broadcasted_iota(jnp.int32, logits.shape, 1)
    weight = jnp.exp(soft_cap * jnp.tanh(logits * (1.0 / soft_cap)))
    weight = jnp.where((column >= start) & (column <= limit), weight, 0.0)
    den[...] = jnp.sum(weight, axis=1, keepdims=True)
    num[...] = jnp.dot(weight.astype(BF16), values, preferred_element_type=F32)


def attend_new(meta, queries, fresh_rows):
    vmem = pl.BlockSpec(memory_space=pltpu.VMEM)
    rows = queries.shape[0]
    return pl.pallas_call(
        attend_new_kernel,
        out_shape=(jax.ShapeDtypeStruct((rows, HD), F32), jax.ShapeDtypeStruct((rows, 1), F32)),
        in_specs=[pl.BlockSpec(memory_space=pltpu.SMEM), vmem, vmem],
        out_specs=(vmem, vmem),
        compiler_params=pltpu.CompilerParams(vmem_limit_bytes=16 << 20),
        name="attend_new",
    )(meta, queries, fresh_rows)


def write_kernel(meta, mine, others, k_old, v_old, k_pool, v_pool):
    slots = k_old.shape[0]
    core = meta[3 * REQS + 2]
    on_core_0 = core == 0
    first = meta[3 * REQS] + core * slots
    k_pool[...] = k_old[...]
    v_pool[...] = v_old[...]

    def write_request(r, carry):
        cached, fresh, offset = meta[r], meta[REQS + r], meta[2 * REQS + r]
        begin = offset + cached - first

        def write_tile(t, carry):
            rows = pl.ds(pl.multiple_of(r * NEWTOK, 64), NEWTOK)
            a, b = mine[rows, :], others[rows, :]
            rows = jnp.concatenate([jnp.where(on_core_0, a, b), jnp.where(on_core_0, b, a)], axis=1)
            slot = lax.broadcasted_iota(jnp.int32, (WRITE_TILE, NEWTOK), 0) + (t * WRITE_TILE - begin)
            index = lax.broadcasted_iota(jnp.int32, (WRITE_TILE, NEWTOK), 1)
            pick = jnp.where((slot == index) & (index < fresh), 1.0, 0.0).astype(BF16)
            new = jnp.dot(pick, rows, preferred_element_type=F32)
            place = lax.broadcasted_iota(jnp.int32, (WRITE_TILE, HD), 0) + (t * WRITE_TILE - begin)
            written = (place >= 0) & (place < fresh)
            here = pl.ds(pl.multiple_of(t * WRITE_TILE, WRITE_TILE), WRITE_TILE)
            k_pool[here, :] = jnp.where(written, new[:, :HD], k_pool[here, :].astype(F32)).astype(BF16)
            v_pool[here, :] = jnp.where(written, new[:, HD:], v_pool[here, :].astype(F32)).astype(BF16)
            return carry

        low, high = jnp.maximum(begin, 0), jnp.minimum(begin + fresh, slots)
        tiles = jnp.where(high > low, pl.cdiv(high, WRITE_TILE), 0)
        lax.fori_loop(lax.div(low, WRITE_TILE), tiles, write_tile, 0)
        return carry

    lax.fori_loop(0, REQS, write_request, 0)


def write(meta, mine, others, k_cache, v_cache):
    vmem = pl.BlockSpec(memory_space=pltpu.VMEM)
    return pl.pallas_call(
        write_kernel,
        out_shape=(
            jax.ShapeDtypeStruct(k_cache.shape, BF16),
            jax.ShapeDtypeStruct(v_cache.shape, BF16),
        ),
        in_specs=[pl.BlockSpec(memory_space=pltpu.SMEM)] + [vmem] * 4,
        out_specs=(vmem, vmem),
        compiler_params=pltpu.CompilerParams(vmem_limit_bytes=32 << 20),
        name="write",
    )(meta, mine, others, k_cache, v_cache)


def divide_kernel(meta, parts, new_num, new_den, out):
    fresh_at = REQS
    begin = meta[3 * REQS + 1]
    total = jnp.sum(parts[...].astype(F32), axis=0)
    for part in range(3):
        row = begin + part * PIECE
        request = row // NEWTOK
        fresh = meta[fresh_at + request]
        within = lax.broadcasted_iota(jnp.int32, (PIECE, HD), 0) + (row - request * NEWTOK)
        den = total[3 * PIECE + part : 3 * PIECE + part + 1, 0:PIECE]
        diagonal = lax.broadcasted_iota(jnp.int32, (PIECE, PIECE), 0) == lax.broadcasted_iota(
            jnp.int32, (PIECE, PIECE), 1
        )
        here = slice(part * PIECE, (part + 1) * PIECE)
        den = jnp.sum(jnp.where(diagonal, den, 0.0), axis=1, keepdims=True) + new_den[here, :]
        value = (total[here, :] + new_num[here, :]) / den
        out[here, :] = jnp.where(within < fresh, value, 0.0).astype(BF16)


def divide(meta, parts, new_num, new_den):
    vmem = pl.BlockSpec(memory_space=pltpu.VMEM)
    return pl.pallas_call(
        divide_kernel,
        out_shape=jax.ShapeDtypeStruct((3 * PIECE, HD), BF16),
        in_specs=[pl.BlockSpec(memory_space=pltpu.SMEM), vmem, vmem, vmem],
        out_specs=vmem,
        compiler_params=pltpu.CompilerParams(vmem_limit_bytes=16 << 20),
        name="divide",
    )(meta, parts, new_num, new_den)


def spread_kernel(meta, attended, own, right, ahead, behind, left, out):
    here = meta[3 * REQS + 3]
    count = 4
    rows = attended.shape[1]
    heads = jnp.concatenate([attended[h] for h in range(attended.shape[0])], axis=1)
    padded = jnp.concatenate([heads, jnp.zeros((2 * HD - rows, heads.shape[1]), BF16)], axis=0)
    last = (((1,), (1,)), ((), ()))
    for step in range(count):
        along = lax.rem(here + step, count)
        for block in range(count):
            at = block * count + along
            if step == 2:
                weights = (ahead if block < 2 else behind)[block % 2]
            else:
                weights = (own, right, None, left)[step][block]
            wide = lax.dot_general(heads, weights[:HD], last, preferred_element_type=F32)
            rest = lax.dot_general(weights[HD:], padded, last, preferred_element_type=F32)
            out[at, :rows, :] = wide.astype(BF16)
            out[at, rows : rows + 16, :] = rest[:, :HD].astype(BF16)
            out[at, rows + 16 :, :] = rest[:, HD:].astype(BF16)


def spread(meta, attended, columns, chunks):
    vmem = pl.BlockSpec(memory_space=pltpu.VMEM)
    return pl.pallas_call(
        spread_kernel,
        out_shape=jax.ShapeDtypeStruct((chunks, attended.shape[1] + 32, HD), BF16),
        in_specs=[pl.BlockSpec(memory_space=pltpu.SMEM)] + [vmem] * (1 + len(columns)),
        out_specs=vmem,
        compiler_params=pltpu.CompilerParams(vmem_limit_bytes=32 << 20),
        name="spread",
    )(meta, attended, *columns)


def on_device(
    tokens, pre_gain, w_q, w_k, w_v, w_o, post_gain, k_cache, v_cache, cached_len, new_len, slot_offset
):
    tok_rows = tokens.shape[0]
    features = tokens.shape[1]
    n_gy = lax.axis_size(GY)
    n_chips = lax.axis_size(CHIPS)
    me = lax.axis_index(GX)
    core = lax.axis_index("c")
    cols = w_q.shape[1]

    float_in = tokens.astype(F32)
    squares = jnp.sum(float_in * float_in, axis=1, keepdims=True)
    high = lax.reduce_precision(squares, 8, 7)
    gained = float_in * (1.0 + pre_gain.astype(F32))
    gained = jnp.concatenate([gained, high, squares - high], axis=1).astype(BF16)
    weights = jnp.concatenate([w_q[:, :HD], w_k, w_q[:, HD:], w_v], axis=1)
    gained, weights = lax.optimization_barrier((gained, weights))
    gained = lax.all_gather(gained, "zl", axis=0, tiled=True)
    gained = everywhere(gained, "y", n_gy // 2).reshape(n_gy, tok_rows, -1)

    weights = lax.all_gather(weights, "c", axis=0, tiled=True)
    weights = lax.dynamic_slice_in_dim(weights, core * cols, cols, 1)
    inner = weights.shape[0]
    weights = jnp.concatenate([weights, w_o.T], axis=0)
    weights = lax.all_gather(weights, "zh", axis=0)
    w_out = weights[:, inner:, :]
    weights = weights[:, :inner, :]
    from_right = [((i + 1) % 4, i) for i in range(4)]
    from_left = [((i - 1) % 4, i) for i in range(4)]
    right = lax.ppermute(weights, "x", from_right)
    left = lax.ppermute(weights, "x", from_left)
    ahead = lax.ppermute(right[:2], "x", from_right)
    behind = lax.ppermute(left[2:], "x", from_left)
    columns = [weights, right, ahead, behind, left]
    swap = [(0, 1), (1, 0)]
    other = lax.ppermute(gained, "c", swap)

    chip_rows = me // 2 * (2 * tok_rows)
    row_ids = chip_rows + jnp.arange(2 * tok_rows, dtype=jnp.int32)
    request = row_ids // NEWTOK
    owner_mask = request[:, None] == jnp.arange(REQS, dtype=jnp.int32)[None, :]
    position = jnp.sum(jnp.where(owner_mask, cached_len[None, :], 0), axis=1) + row_ids % NEWTOK
    half = HD // 2
    inverse = jnp.power(10000.0, -2.0 * jnp.arange(half, dtype=F32) / HD)
    angle = position.astype(F32)[:, None] * inverse[None, :]
    cosine, sine = jnp.cos(angle), jnp.sin(angle)
    cosine = jnp.concatenate([cosine, cosine], axis=1)
    sine = jnp.concatenate([-sine, sine], axis=1)
    turns = jnp.stack(
        [
            cosine * query_scale,
            sine * query_scale,
            jnp.where(core == 0, cosine, 1.0),
            jnp.where(core == 0, sine, 0.0),
        ]
    )
    meta = jnp.concatenate(
        [
            cached_len,
            new_len,
            slot_offset,
            jnp.stack([me // 2 * (2 * k_cache.shape[0]), chip_rows, core, lax.axis_index("x")]).astype(jnp.int32),
        ]
    )
    k_other = lax.ppermute(k_cache, "c", swap)
    v_other = lax.ppermute(v_cache, "c", swap)
    other, k_other, v_other = lax.optimization_barrier((other, k_other, v_other))
    queries, fresh_rows = project(meta, gained, other, turns, columns)

    queries, fresh_rows, w_out = lax.optimization_barrier((queries, fresh_rows, w_out))
    out_right = lax.ppermute(w_out, "x", from_right)
    out_left = lax.ppermute(w_out, "x", from_left)
    near_rows = lax.all_gather(fresh_rows, ("x", "c"), axis=0)
    all_queries = everywhere(queries, CHIPS, n_chips).reshape(-1, HD)
    all_queries, near_rows, out_right, out_left = lax.optimization_barrier(
        (all_queries, near_rows, out_right, out_left)
    )
    out_columns = [
        w_out,
        out_right,
        lax.ppermute(out_right[:2], "x", from_right),
        lax.ppermute(out_left[2:], "x", from_left),
        out_left,
    ]

    sums = attend(meta, all_queries, k_cache, v_cache, k_other, v_other)
    sums, near_rows = lax.optimization_barrier((sums, near_rows))
    parts = lax.all_to_all(sums.reshape(n_chips, -1, HD), CHIPS, 0, 0)
    attended = divide(meta, parts, *attend_new(meta, queries, near_rows))
    attended = lax.all_gather(attended, "c", axis=0)
    partial_out = spread(meta, attended, out_columns, n_gy)
    partial_out, near_rows = lax.optimization_barrier((partial_out, near_rows))
    kind = lax.dynamic_index_in_dim(near_rows.reshape(4, 2, 2 * tok_rows, HD), core, 1, keepdims=False)
    kind = lax.all_gather(kind.reshape(-1, HD), "zh", axis=0, tiled=True)
    k_pool, v_pool = write(meta, kind, lax.ppermute(kind, "c", swap), k_cache, v_cache)
    total = jnp.sum(lax.all_to_all(partial_out, GY, 0, 0).astype(F32), axis=0)
    rows = 2 * tok_rows
    rest = jnp.concatenate([total[rows : rows + 16], total[rows + 16 :, : rows - HD]], axis=1)
    branch = jnp.concatenate([total[:rows], rest.T], axis=1)
    squares = jnp.sum(branch * branch, axis=1).reshape(2, 1, 1, tok_rows)
    squares = jnp.broadcast_to(squares, (2, n_gy, 1, tok_rows)).reshape(2 * n_gy, 1, tok_rows)
    squares = lax.all_to_all(squares, ("c",) + GY, 0, 0)
    mean = jnp.sum(squares, axis=(0, 1)) / D
    kept = lax.dynamic_slice_in_dim(branch, core * tok_rows, tok_rows, 0)
    sent = lax.dynamic_slice_in_dim(branch, (1 - core) * tok_rows, tok_rows, 0)
    came = lax.ppermute(sent, "c", swap)
    branch = jnp.concatenate([jnp.where(core == 0, kept, came), jnp.where(core == 0, came, kept)], axis=1)
    layer_out = float_in + branch * lax.rsqrt(mean + epsilon)[:, None] * (1.0 + post_gain.astype(F32))
    return (layer_out.astype(BF16), k_pool, v_pool)


def solution(mesh):
    parts = Mesh(mesh.devices.reshape(4, 4, 2, 8, 2), GX + GY)
    both = P(GX, GY)
    placed = (both, P(GY), both, both, both, P(GY, GX), P(GY), both, both, P(), P(), P())
    return jax.shard_map(
        on_device, mesh=parts, in_specs=placed, out_specs=(both, both, both), check_vma=False
    )
```

```python
import jax
import jax.numpy as jnp
from jax import lax
from jax.experimental import pallas as pl
from jax.experimental.pallas import tpu as pltpu
from jax.sharding import Mesh, PartitionSpec as P

D = 4608
HD = 128
REQS = 12
NEWTOK = 192
READ_TILE = 512
WRITE_TILE = 256
PIECE = 48
epsilon = 1e-06
soft_cap = 50.0
query_scale = 144.0 ** (-0.5)
F32 = jnp.float32
BF16 = jnp.bfloat16

CHIPS = ("zh", "x")
GX = ("zh", "x", "c")
GY = ("y", "zl")


def everywhere(value, axes, count):
    return lax.all_to_all(jnp.broadcast_to(value[None], (count,) + value.shape), axes, 0, 0)


def project_kernel(meta, mine, others, turns, own, right, ahead, behind, left, *outs):
    on_core_0 = meta[3 * REQS + 2] == 0
    here = meta[3 * REQS + 3]
    features = mine.shape[2] - 2
    count = 4
    total = jnp.zeros((outs[0].shape[0], 2 * HD), F32)
    squares = jnp.zeros((outs[0].shape[0], 2), F32)
    for step in range(count):
        along = lax.rem(here + step, count)
        for block in range(count):
            at = block * count + along
            a, b = mine[at], others[at]
            rows = jnp.concatenate([jnp.where(on_core_0, a, b), jnp.where(on_core_0, b, a)], axis=0)
            squares += rows[:, features:].astype(F32)
            if step == 2:
                columns = (ahead if block < 2 else behind)[block % 2]
            else:
                columns = (own, right, None, left)[step][block]
            total += jnp.dot(rows[:, :features], columns[:features, :], preferred_element_type=F32)
    mean = jnp.sum(squares, axis=1, keepdims=True) * (1.0 / D)
    total = total * lax.rsqrt(mean + epsilon)
    for head in range(2):
        value = total[:, head * HD : (head + 1) * HD]
        value = value * turns[2 * head] + pltpu.roll(value, HD // 2, 1) * turns[2 * head + 1]
        outs[head][...] = value.astype(BF16)


def project(meta, mine, others, turns, columns):
    vmem = pl.BlockSpec(memory_space=pltpu.VMEM)
    return pl.pallas_call(
        project_kernel,
        out_shape=[jax.ShapeDtypeStruct((2 * mine.shape[1], HD), BF16)] * 2,
        in_specs=[pl.BlockSpec(memory_space=pltpu.SMEM)] + [vmem] * (3 + len(columns)),
        out_specs=[vmem, vmem],
        compiler_params=pltpu.CompilerParams(vmem_limit_bytes=32 << 20),
        name="project",
    )(meta, mine, others, turns, *columns)


def attend_kernel(meta, queries, k_own, v_own, k_other, v_other, sums, num, den, totals):
    own = k_own.shape[0]
    first = meta[3 * REQS]
    core = meta[3 * REQS + 2]
    blocks = REQS * NEWTOK // (3 * PIECE)
    chunk = sums.shape[0] // blocks
    totals[...] = jnp.zeros_like(totals)

    def read_request(r, carry):
        cached, offset = meta[r], meta[2 * REQS + r]
        num[...] = jnp.zeros_like(num)
        den[...] = jnp.zeros_like(den)
        for keys, values, at in ((k_own, v_own, core), (k_other, v_other, 1 - core)):
            begin = offset - first - at * own
            low, high = jnp.maximum(begin, 0), jnp.minimum(begin + cached, own)

            def read_tile(t, carry):
                rows = queries[pl.ds(pl.multiple_of(r * NEWTOK, 64), NEWTOK), :]
                here = pl.ds(pl.multiple_of(t * READ_TILE, READ_TILE), READ_TILE)
                logits = lax.dot_general(
                    rows, keys[here, :], (((1,), (1,)), ((), ())), preferred_element_type=F32
                )
                slot = lax.broadcasted_iota(jnp.int32, logits.shape, 1) + t * READ_TILE
                weight = jnp.exp(soft_cap * jnp.tanh(logits * (1.0 / soft_cap)))
                weight = jnp.where((slot >= low) & (slot < high), weight, 0.0).astype(BF16)
                num[...] += jnp.dot(weight, values[here, :], preferred_element_type=F32)
                den[...] += lax.dot_general(
                    jnp.ones((8, READ_TILE), BF16), weight, (((1,), (1,)), ((), ())), preferred_element_type=F32
                )
                return carry

            tiles = jnp.where(high > low, pl.cdiv(high, READ_TILE), 0)
            lax.fori_loop(lax.div(low, READ_TILE), tiles, read_tile, 0)

        for piece in range(NEWTOK // PIECE):
            at = r * (NEWTOK // PIECE) + piece
            block, part = lax.div(at, 3), lax.rem(at, 3)
            to = pl.multiple_of(block * chunk + part * PIECE, 16)
            at_row = piece * PIECE
            sums[pl.ds(to, PIECE), :] = num[at_row : at_row + PIECE, :].astype(BF16)
            totals[pl.ds(block * 8 + part, 1), 0:PIECE] = den[0:1, at_row : at_row + PIECE]
        return carry

    lax.fori_loop(0, REQS, read_request, 0)
    for block in range(blocks):
        rows = totals[block * 8 : block * 8 + 8, :]
        rows = jnp.concatenate([rows, jnp.zeros_like(rows)], axis=0)
        sums[block * chunk + 3 * PIECE : (block + 1) * chunk, :] = rows.astype(BF16)


def attend(meta, queries, k_cache, v_cache, k_other, v_other):
    blocks = REQS * NEWTOK // (3 * PIECE)
    chunk = 3 * PIECE + 16
    vmem = pl.BlockSpec(memory_space=pltpu.VMEM)
    return pl.pallas_call(
        attend_kernel,
        out_shape=jax.ShapeDtypeStruct((blocks * chunk, HD), BF16),
        in_specs=[pl.BlockSpec(memory_space=pltpu.SMEM)] + [vmem] * 5,
        out_specs=vmem,
        scratch_shapes=[
            pltpu.VMEM((NEWTOK, HD), F32),
            pltpu.VMEM((8, NEWTOK), F32),
            pltpu.VMEM((blocks * 8, HD), F32),
        ],
        compiler_params=pltpu.CompilerParams(vmem_limit_bytes=32 << 20),
        name="attend",
    )(meta, queries, k_cache, v_cache, k_other, v_other)


def attend_new_kernel(meta, queries, fresh_rows, num, den):
    here = meta[3 * REQS + 3]
    rows, count = queries.shape[0], fresh_rows.shape[0] // 2
    request = lax.div(meta[3 * REQS + 1] - here * rows, NEWTOK)
    row = lax.broadcasted_iota(jnp.int32, (rows, 1), 0) + here * rows
    start, limit = jnp.zeros_like(row), jnp.zeros_like(row)
    for part in range(count * rows // NEWTOK):
        at = part * NEWTOK
        inside = (row >= at) & (row < at + NEWTOK)
        start = jnp.where(inside, at, start)
        limit = jnp.where(inside, jnp.minimum(row, at + meta[REQS + request + part] - 1), limit)
    keys = jnp.concatenate([fresh_rows[2 * step] for step in range(count)], axis=0)
    values = jnp.concatenate([fresh_rows[2 * step + 1] for step in range(count)], axis=0)
    logits = lax.dot_general(queries[...], keys, (((1,), (1,)), ((), ())), preferred_element_type=F32)
    column = lax.broadcasted_iota(jnp.int32, logits.shape, 1)
    weight = jnp.exp(soft_cap * jnp.tanh(logits * (1.0 / soft_cap)))
    weight = jnp.where((column >= start) & (column <= limit), weight, 0.0)
    den[...] = jnp.sum(weight, axis=1, keepdims=True)
    num[...] = jnp.dot(weight.astype(BF16), values, preferred_element_type=F32)


def attend_new(meta, queries, fresh_rows):
    vmem = pl.BlockSpec(memory_space=pltpu.VMEM)
    rows = queries.shape[0]
    return pl.pallas_call(
        attend_new_kernel,
        out_shape=(jax.ShapeDtypeStruct((rows, HD), F32), jax.ShapeDtypeStruct((rows, 1), F32)),
        in_specs=[pl.BlockSpec(memory_space=pltpu.SMEM), vmem, vmem],
        out_specs=(vmem, vmem),
        compiler_params=pltpu.CompilerParams(vmem_limit_bytes=16 << 20),
        name="attend_new",
    )(meta, queries, fresh_rows)


def write_kernel(meta, mine, others, k_old, v_old, k_pool, v_pool):
    slots = k_old.shape[0]
    core = meta[3 * REQS + 2]
    on_core_0 = core == 0
    first = meta[3 * REQS] + core * slots
    k_pool[...] = k_old[...]
    v_pool[...] = v_old[...]

    def write_request(r, carry):
        cached, fresh, offset = meta[r], meta[REQS + r], meta[2 * REQS + r]
        begin = offset + cached - first

        def write_tile(t, carry):
            rows = pl.ds(pl.multiple_of(r * NEWTOK, 64), NEWTOK)
            a, b = mine[rows, :], others[rows, :]
            rows = jnp.concatenate([jnp.where(on_core_0, a, b), jnp.where(on_core_0, b, a)], axis=1)
            slot = lax.broadcasted_iota(jnp.int32, (WRITE_TILE, NEWTOK), 0) + (t * WRITE_TILE - begin)
            index = lax.broadcasted_iota(jnp.int32, (WRITE_TILE, NEWTOK), 1)
            pick = jnp.where((slot == index) & (index < fresh), 1.0, 0.0).astype(BF16)
            new = jnp.dot(pick, rows, preferred_element_type=F32)
            place = lax.broadcasted_iota(jnp.int32, (WRITE_TILE, HD), 0) + (t * WRITE_TILE - begin)
            written = (place >= 0) & (place < fresh)
            here = pl.ds(pl.multiple_of(t * WRITE_TILE, WRITE_TILE), WRITE_TILE)
            k_pool[here, :] = jnp.where(written, new[:, :HD], k_pool[here, :].astype(F32)).astype(BF16)
            v_pool[here, :] = jnp.where(written, new[:, HD:], v_pool[here, :].astype(F32)).astype(BF16)
            return carry

        low, high = jnp.maximum(begin, 0), jnp.minimum(begin + fresh, slots)
        tiles = jnp.where(high > low, pl.cdiv(high, WRITE_TILE), 0)
        lax.fori_loop(lax.div(low, WRITE_TILE), tiles, write_tile, 0)
        return carry

    lax.fori_loop(0, REQS, write_request, 0)


def write(meta, mine, others, k_cache, v_cache):
    vmem = pl.BlockSpec(memory_space=pltpu.VMEM)
    return pl.pallas_call(
        write_kernel,
        out_shape=(
            jax.ShapeDtypeStruct(k_cache.shape, BF16),
            jax.ShapeDtypeStruct(v_cache.shape, BF16),
        ),
        in_specs=[pl.BlockSpec(memory_space=pltpu.SMEM)] + [vmem] * 4,
        out_specs=(vmem, vmem),
        compiler_params=pltpu.CompilerParams(vmem_limit_bytes=32 << 20),
        name="write",
    )(meta, mine, others, k_cache, v_cache)


def divide_kernel(meta, parts, new_num, new_den, out):
    fresh_at = REQS
    begin = meta[3 * REQS + 1]
    total = jnp.sum(parts[...].astype(F32), axis=0)
    for part in range(3):
        row = begin + part * PIECE
        request = row // NEWTOK
        fresh = meta[fresh_at + request]
        within = lax.broadcasted_iota(jnp.int32, (PIECE, HD), 0) + (row - request * NEWTOK)
        den = total[3 * PIECE + part : 3 * PIECE + part + 1, 0:PIECE]
        diagonal = lax.broadcasted_iota(jnp.int32, (PIECE, PIECE), 0) == lax.broadcasted_iota(
            jnp.int32, (PIECE, PIECE), 1
        )
        here = slice(part * PIECE, (part + 1) * PIECE)
        den = jnp.sum(jnp.where(diagonal, den, 0.0), axis=1, keepdims=True) + new_den[here, :]
        value = (total[here, :] + new_num[here, :]) / den
        out[here, :] = jnp.where(within < fresh, value, 0.0).astype(BF16)


def divide(meta, parts, new_num, new_den):
    vmem = pl.BlockSpec(memory_space=pltpu.VMEM)
    return pl.pallas_call(
        divide_kernel,
        out_shape=jax.ShapeDtypeStruct((3 * PIECE, HD), BF16),
        in_specs=[pl.BlockSpec(memory_space=pltpu.SMEM), vmem, vmem, vmem],
        out_specs=vmem,
        compiler_params=pltpu.CompilerParams(vmem_limit_bytes=16 << 20),
        name="divide",
    )(meta, parts, new_num, new_den)


def spread_kernel(meta, attended, own, right, ahead, behind, left, out):
    here = meta[3 * REQS + 3]
    count = 4
    rows = attended.shape[1]
    heads = jnp.concatenate([attended[h] for h in range(attended.shape[0])], axis=1)
    padded = jnp.concatenate([heads, jnp.zeros((2 * HD - rows, heads.shape[1]), BF16)], axis=0)
    last = (((1,), (1,)), ((), ()))
    for step in range(count):
        along = lax.rem(here + step, count)
        for block in range(count):
            at = block * count + along
            if step == 2:
                weights = (ahead if block < 2 else behind)[block % 2]
            else:
                weights = (own, right, None, left)[step][block]
            wide = lax.dot_general(heads, weights[:HD], last, preferred_element_type=F32)
            rest = lax.dot_general(weights[HD:], padded, last, preferred_element_type=F32)
            out[at, :rows, :] = wide.astype(BF16)
            out[at, rows : rows + 16, :] = rest[:, :HD].astype(BF16)
            out[at, rows + 16 :, :] = rest[:, HD:].astype(BF16)


def spread(meta, attended, columns, chunks):
    vmem = pl.BlockSpec(memory_space=pltpu.VMEM)
    return pl.pallas_call(
        spread_kernel,
        out_shape=jax.ShapeDtypeStruct((chunks, attended.shape[1] + 32, HD), BF16),
        in_specs=[pl.BlockSpec(memory_space=pltpu.SMEM)] + [vmem] * (1 + len(columns)),
        out_specs=vmem,
        compiler_params=pltpu.CompilerParams(vmem_limit_bytes=32 << 20),
        name="spread",
    )(meta, attended, *columns)


def on_device(
    tokens, pre_gain, w_q, w_k, w_v, w_o, post_gain, k_cache, v_cache, cached_len, new_len, slot_offset
):
    tok_rows = tokens.shape[0]
    features = tokens.shape[1]
    n_gy = lax.axis_size(GY)
    n_chips = lax.axis_size(CHIPS)
    me = lax.axis_index(GX)
    core = lax.axis_index("c")
    cols = w_q.shape[1]

    float_in = tokens.astype(F32)
    squares = jnp.sum(float_in * float_in, axis=1, keepdims=True)
    high = lax.reduce_precision(squares, 8, 7)
    gained = float_in * (1.0 + pre_gain.astype(F32))
    gained = jnp.concatenate([gained, high, squares - high], axis=1).astype(BF16)
    weights = jnp.concatenate([w_q[:, :HD], w_k, w_q[:, HD:], w_v], axis=1)
    gained, weights = lax.optimization_barrier((gained, weights))
    gained = lax.all_gather(gained, "zl", axis=0, tiled=True)
    gained = everywhere(gained, "y", n_gy // 2).reshape(n_gy, tok_rows, -1)

    weights = lax.all_gather(weights, "c", axis=0, tiled=True)
    weights = lax.dynamic_slice_in_dim(weights, core * cols, cols, 1)
    inner = weights.shape[0]
    weights = jnp.concatenate([weights, w_o.T], axis=0)
    weights = lax.all_gather(weights, "zh", axis=0)
    w_out = weights[:, inner:, :]
    weights = weights[:, :inner, :]
    from_right = [((i + 1) % 4, i) for i in range(4)]
    from_left = [((i - 1) % 4, i) for i in range(4)]
    right = lax.ppermute(weights, "x", from_right)
    left = lax.ppermute(weights, "x", from_left)
    ahead = lax.ppermute(right[:2], "x", from_right)
    behind = lax.ppermute(left[2:], "x", from_left)
    columns = [weights, right, ahead, behind, left]
    swap = [(0, 1), (1, 0)]
    other = lax.ppermute(gained, "c", swap)

    chip_rows = me // 2 * (2 * tok_rows)
    row_ids = chip_rows + jnp.arange(2 * tok_rows, dtype=jnp.int32)
    request = row_ids // NEWTOK
    owner_mask = request[:, None] == jnp.arange(REQS, dtype=jnp.int32)[None, :]
    position = jnp.sum(jnp.where(owner_mask, cached_len[None, :], 0), axis=1) + row_ids % NEWTOK
    half = HD // 2
    inverse = jnp.power(10000.0, -2.0 * jnp.arange(half, dtype=F32) / HD)
    angle = position.astype(F32)[:, None] * inverse[None, :]
    cosine, sine = jnp.cos(angle), jnp.sin(angle)
    cosine = jnp.concatenate([cosine, cosine], axis=1)
    sine = jnp.concatenate([-sine, sine], axis=1)
    turns = jnp.stack(
        [
            cosine * query_scale,
            sine * query_scale,
            jnp.where(core == 0, cosine, 1.0),
            jnp.where(core == 0, sine, 0.0),
        ]
    )
    meta = jnp.concatenate(
        [
            cached_len,
            new_len,
            slot_offset,
            jnp.stack([me // 2 * (2 * k_cache.shape[0]), chip_rows, core, lax.axis_index("x")]).astype(jnp.int32),
        ]
    )
    k_other = lax.ppermute(k_cache, "c", swap)
    v_other = lax.ppermute(v_cache, "c", swap)
    other, k_other, v_other = lax.optimization_barrier((other, k_other, v_other))
    queries, fresh_rows = project(meta, gained, other, turns, columns)

    queries, fresh_rows, w_out = lax.optimization_barrier((queries, fresh_rows, w_out))
    out_right = lax.ppermute(w_out, "x", from_right)
    out_left = lax.ppermute(w_out, "x", from_left)
    near_rows = lax.all_gather(fresh_rows, "c", axis=0)
    all_queries = everywhere(queries, CHIPS, n_chips).reshape(-1, HD)
    all_queries, near_rows, out_right, out_left = lax.optimization_barrier(
        (all_queries, near_rows, out_right, out_left)
    )
    out_columns = [
        w_out,
        out_right,
        lax.ppermute(out_right[:2], "x", from_right),
        lax.ppermute(out_left[2:], "x", from_left),
        out_left,
    ]

    sums = attend(meta, all_queries, k_cache, v_cache, k_other, v_other)
    sums, near_rows = lax.optimization_barrier((sums, near_rows))
    near_rows = lax.all_gather(near_rows, "x", axis=0, tiled=True)
    parts = lax.all_to_all(sums.reshape(n_chips, -1, HD), CHIPS, 0, 0)
    attended = divide(meta, parts, *attend_new(meta, queries, near_rows))
    attended = lax.all_gather(attended, "c", axis=0)
    partial_out = spread(meta, attended, out_columns, n_gy)
    partial_out, near_rows = lax.optimization_barrier((partial_out, near_rows))
    kind = lax.dynamic_index_in_dim(near_rows.reshape(4, 2, 2 * tok_rows, HD), core, 1, keepdims=False)
    kind = lax.all_gather(kind.reshape(-1, HD), "zh", axis=0, tiled=True)
    total = jnp.sum(lax.all_to_all(partial_out, GY, 0, 0).astype(F32), axis=0)
    rows = 2 * tok_rows
    rest = jnp.concatenate([total[rows : rows + 16], total[rows + 16 :, : rows - HD]], axis=1)
    branch = jnp.concatenate([total[:rows], rest.T], axis=1)
    squares = jnp.sum(branch * branch, axis=1).reshape(2, 1, 1, tok_rows)
    squares = jnp.broadcast_to(squares, (2, n_gy, 1, tok_rows)).reshape(2 * n_gy, 1, tok_rows)
    squares, kind = lax.optimization_barrier((squares, kind))
    squares = lax.all_to_all(squares, ("c",) + GY, 0, 0)
    k_pool, v_pool = write(meta, kind, lax.ppermute(kind, "c", swap), k_cache, v_cache)
    mean = jnp.sum(squares, axis=(0, 1)) / D
    kept = lax.dynamic_slice_in_dim(branch, core * tok_rows, tok_rows, 0)
    sent = lax.dynamic_slice_in_dim(branch, (1 - core) * tok_rows, tok_rows, 0)
    came = lax.ppermute(sent, "c", swap)
    branch = jnp.concatenate([jnp.where(core == 0, kept, came), jnp.where(core == 0, came, kept)], axis=1)
    layer_out = float_in + branch * lax.rsqrt(mean + epsilon)[:, None] * (1.0 + post_gain.astype(F32))
    return (layer_out.astype(BF16), k_pool, v_pool)


def solution(mesh):
    parts = Mesh(mesh.devices.reshape(4, 4, 2, 8, 2), GX + GY)
    both = P(GX, GY)
    placed = (both, P(GY), both, both, both, P(GY, GX), P(GY), both, both, P(), P(), P())
    return jax.shard_map(
        on_device, mesh=parts, in_specs=placed, out_specs=(both, both, both), check_vma=False
    )
```

```python
import jax
import jax.numpy as jnp
from jax import lax
from jax.experimental import pallas as pl
from jax.experimental.pallas import tpu as pltpu
from jax.sharding import Mesh, PartitionSpec as P

D = 4608
HD = 128
REQS = 12
NEWTOK = 192
READ_TILE = 512
WRITE_TILE = 256
PIECE = 48
epsilon = 1e-06
soft_cap = 50.0
query_scale = 144.0 ** (-0.5)
F32 = jnp.float32
BF16 = jnp.bfloat16

CHIPS = ("zh", "x")
GX = ("zh", "x", "c")
GY = ("y", "zl")


def everywhere(value, axes, count):
    return lax.all_to_all(jnp.broadcast_to(value[None], (count,) + value.shape), axes, 0, 0)


def project_kernel(meta, mine, others, turns, own, right, ahead, behind, left, *outs):
    on_core_0 = meta[3 * REQS + 2] == 0
    here = meta[3 * REQS + 3]
    features = mine.shape[2] - 2
    count = 4
    total = jnp.zeros((outs[0].shape[0], 2 * HD), F32)
    squares = jnp.zeros((outs[0].shape[0], 2), F32)
    for step in range(count):
        along = lax.rem(here + step, count)
        for block in range(count):
            at = block * count + along
            a, b = mine[at], others[at]
            rows = jnp.concatenate([jnp.where(on_core_0, a, b), jnp.where(on_core_0, b, a)], axis=0)
            squares += rows[:, features:].astype(F32)
            if step == 2:
                columns = (ahead if block < 2 else behind)[block % 2]
            else:
                columns = (own, right, None, left)[step][block]
            total += jnp.dot(rows[:, :features], columns[:features, :], preferred_element_type=F32)
    mean = jnp.sum(squares, axis=1, keepdims=True) * (1.0 / D)
    total = total * lax.rsqrt(mean + epsilon)
    for head in range(2):
        value = total[:, head * HD : (head + 1) * HD]
        value = value * turns[2 * head] + pltpu.roll(value, HD // 2, 1) * turns[2 * head + 1]
        outs[head][...] = value.astype(BF16)


def project(meta, mine, others, turns, columns):
    vmem = pl.BlockSpec(memory_space=pltpu.VMEM)
    return pl.pallas_call(
        project_kernel,
        out_shape=[jax.ShapeDtypeStruct((2 * mine.shape[1], HD), BF16)] * 2,
        in_specs=[pl.BlockSpec(memory_space=pltpu.SMEM)] + [vmem] * (3 + len(columns)),
        out_specs=[vmem, vmem],
        compiler_params=pltpu.CompilerParams(vmem_limit_bytes=32 << 20),
        name="project",
    )(meta, mine, others, turns, *columns)


def attend_kernel(meta, queries, k_own, v_own, k_other, v_other, sums, num, den, totals):
    own = k_own.shape[0]
    first = meta[3 * REQS]
    core = meta[3 * REQS + 2]
    blocks = REQS * NEWTOK // (3 * PIECE)
    chunk = sums.shape[0] // blocks
    totals[...] = jnp.zeros_like(totals)

    def read_request(r, carry):
        cached, offset = meta[r], meta[2 * REQS + r]
        num[...] = jnp.zeros_like(num)
        den[...] = jnp.zeros_like(den)
        for keys, values, at in ((k_own, v_own, core), (k_other, v_other, 1 - core)):
            begin = offset - first - at * own
            low, high = jnp.maximum(begin, 0), jnp.minimum(begin + cached, own)

            def read_tile(t, carry):
                rows = queries[pl.ds(pl.multiple_of(r * NEWTOK, 64), NEWTOK), :]
                here = pl.ds(pl.multiple_of(t * READ_TILE, READ_TILE), READ_TILE)
                logits = lax.dot_general(
                    rows, keys[here, :], (((1,), (1,)), ((), ())), preferred_element_type=F32
                )
                slot = lax.broadcasted_iota(jnp.int32, logits.shape, 1) + t * READ_TILE
                weight = jnp.exp(soft_cap * jnp.tanh(logits * (1.0 / soft_cap)))
                weight = jnp.where((slot >= low) & (slot < high), weight, 0.0).astype(BF16)
                num[...] += jnp.dot(weight, values[here, :], preferred_element_type=F32)
                den[...] += lax.dot_general(
                    jnp.ones((8, READ_TILE), BF16), weight, (((1,), (1,)), ((), ())), preferred_element_type=F32
                )
                return carry

            tiles = jnp.where(high > low, pl.cdiv(high, READ_TILE), 0)
            lax.fori_loop(lax.div(low, READ_TILE), tiles, read_tile, 0)

        for piece in range(NEWTOK // PIECE):
            at = r * (NEWTOK // PIECE) + piece
            block, part = lax.div(at, 3), lax.rem(at, 3)
            to = pl.multiple_of(block * chunk + part * PIECE, 16)
            at_row = piece * PIECE
            sums[pl.ds(to, PIECE), :] = num[at_row : at_row + PIECE, :].astype(BF16)
            totals[pl.ds(block * 8 + part, 1), 0:PIECE] = den[0:1, at_row : at_row + PIECE]
        return carry

    lax.fori_loop(0, REQS, read_request, 0)
    for block in range(blocks):
        rows = totals[block * 8 : block * 8 + 8, :]
        rows = jnp.concatenate([rows, jnp.zeros_like(rows)], axis=0)
        sums[block * chunk + 3 * PIECE : (block + 1) * chunk, :] = rows.astype(BF16)


def attend(meta, queries, k_cache, v_cache, k_other, v_other):
    blocks = REQS * NEWTOK // (3 * PIECE)
    chunk = 3 * PIECE + 16
    vmem = pl.BlockSpec(memory_space=pltpu.VMEM)
    return pl.pallas_call(
        attend_kernel,
        out_shape=jax.ShapeDtypeStruct((blocks * chunk, HD), BF16),
        in_specs=[pl.BlockSpec(memory_space=pltpu.SMEM)] + [vmem] * 5,
        out_specs=vmem,
        scratch_shapes=[
            pltpu.VMEM((NEWTOK, HD), F32),
            pltpu.VMEM((8, NEWTOK), F32),
            pltpu.VMEM((blocks * 8, HD), F32),
        ],
        compiler_params=pltpu.CompilerParams(vmem_limit_bytes=32 << 20),
        name="attend",
    )(meta, queries, k_cache, v_cache, k_other, v_other)


def attend_new_kernel(meta, queries, own, right, far, left, num, den, kind):
    here = meta[3 * REQS + 3]
    on_core_0 = meta[3 * REQS + 2] == 0
    rows, count = queries.shape[0], 4
    request = lax.div(meta[3 * REQS + 1] - here * rows, NEWTOK)
    row = lax.broadcasted_iota(jnp.int32, (rows, 1), 0) + here * rows
    start, limit = jnp.zeros_like(row), jnp.zeros_like(row)
    for part in range(count * rows // NEWTOK):
        at = part * NEWTOK
        inside = (row >= at) & (row < at + NEWTOK)
        start = jnp.where(inside, at, start)
        limit = jnp.where(inside, jnp.minimum(row, at + meta[REQS + request + part] - 1), limit)
    total, weights = jnp.zeros((rows, HD), F32), jnp.zeros((rows, 1), F32)
    for step, block in enumerate((own, right, far, left)):
        at = lax.rem(here + step, count) * rows
        logits = lax.dot_general(queries[...], block[0], (((1,), (1,)), ((), ())), preferred_element_type=F32)
        column = lax.broadcasted_iota(jnp.int32, logits.shape, 1) + at
        weight = jnp.exp(soft_cap * jnp.tanh(logits * (1.0 / soft_cap)))
        weight = jnp.where((column >= start) & (column <= limit), weight, 0.0)
        weights += jnp.sum(weight, axis=1, keepdims=True)
        total += jnp.dot(weight.astype(BF16), block[1], preferred_element_type=F32)
        kind[pl.ds(pl.multiple_of(at, 16), rows), :] = jnp.where(on_core_0, block[0], block[1])
    num[...] = total
    den[...] = weights


def attend_new(meta, queries, fresh_rows):
    vmem = pl.BlockSpec(memory_space=pltpu.VMEM)
    rows = queries.shape[0]
    return pl.pallas_call(
        attend_new_kernel,
        out_shape=(
            jax.ShapeDtypeStruct((rows, HD), F32),
            jax.ShapeDtypeStruct((rows, 1), F32),
            jax.ShapeDtypeStruct((len(fresh_rows) * rows, HD), BF16),
        ),
        in_specs=[pl.BlockSpec(memory_space=pltpu.SMEM)] + [vmem] * (1 + len(fresh_rows)),
        out_specs=(vmem, vmem, vmem),
        compiler_params=pltpu.CompilerParams(vmem_limit_bytes=16 << 20),
        name="attend_new",
    )(meta, queries, *fresh_rows)


def write_kernel(meta, mine, others, k_old, v_old, k_pool, v_pool):
    slots = k_old.shape[0]
    core = meta[3 * REQS + 2]
    on_core_0 = core == 0
    first = meta[3 * REQS] + core * slots
    k_pool[...] = k_old[...]
    v_pool[...] = v_old[...]

    def write_request(r, carry):
        cached, fresh, offset = meta[r], meta[REQS + r], meta[2 * REQS + r]
        begin = offset + cached - first

        def write_tile(t, carry):
            rows = pl.ds(pl.multiple_of(r * NEWTOK, 64), NEWTOK)
            a, b = mine[rows, :], others[rows, :]
            rows = jnp.concatenate([jnp.where(on_core_0, a, b), jnp.where(on_core_0, b, a)], axis=1)
            slot = lax.broadcasted_iota(jnp.int32, (WRITE_TILE, NEWTOK), 0) + (t * WRITE_TILE - begin)
            index = lax.broadcasted_iota(jnp.int32, (WRITE_TILE, NEWTOK), 1)
            pick = jnp.where((slot == index) & (index < fresh), 1.0, 0.0).astype(BF16)
            new = jnp.dot(pick, rows, preferred_element_type=F32)
            place = lax.broadcasted_iota(jnp.int32, (WRITE_TILE, HD), 0) + (t * WRITE_TILE - begin)
            written = (place >= 0) & (place < fresh)
            here = pl.ds(pl.multiple_of(t * WRITE_TILE, WRITE_TILE), WRITE_TILE)
            k_pool[here, :] = jnp.where(written, new[:, :HD], k_pool[here, :].astype(F32)).astype(BF16)
            v_pool[here, :] = jnp.where(written, new[:, HD:], v_pool[here, :].astype(F32)).astype(BF16)
            return carry

        low, high = jnp.maximum(begin, 0), jnp.minimum(begin + fresh, slots)
        tiles = jnp.where(high > low, pl.cdiv(high, WRITE_TILE), 0)
        lax.fori_loop(lax.div(low, WRITE_TILE), tiles, write_tile, 0)
        return carry

    lax.fori_loop(0, REQS, write_request, 0)


def write(meta, mine, others, k_cache, v_cache):
    vmem = pl.BlockSpec(memory_space=pltpu.VMEM)
    return pl.pallas_call(
        write_kernel,
        out_shape=(
            jax.ShapeDtypeStruct(k_cache.shape, BF16),
            jax.ShapeDtypeStruct(v_cache.shape, BF16),
        ),
        in_specs=[pl.BlockSpec(memory_space=pltpu.SMEM)] + [vmem] * 4,
        out_specs=(vmem, vmem),
        compiler_params=pltpu.CompilerParams(vmem_limit_bytes=32 << 20),
        name="write",
    )(meta, mine, others, k_cache, v_cache)


def divide_kernel(meta, parts, new_num, new_den, out):
    fresh_at = REQS
    begin = meta[3 * REQS + 1]
    total = jnp.sum(parts[...].astype(F32), axis=0)
    for part in range(3):
        row = begin + part * PIECE
        request = row // NEWTOK
        fresh = meta[fresh_at + request]
        within = lax.broadcasted_iota(jnp.int32, (PIECE, HD), 0) + (row - request * NEWTOK)
        den = total[3 * PIECE + part : 3 * PIECE + part + 1, 0:PIECE]
        diagonal = lax.broadcasted_iota(jnp.int32, (PIECE, PIECE), 0) == lax.broadcasted_iota(
            jnp.int32, (PIECE, PIECE), 1
        )
        here = slice(part * PIECE, (part + 1) * PIECE)
        den = jnp.sum(jnp.where(diagonal, den, 0.0), axis=1, keepdims=True) + new_den[here, :]
        value = (total[here, :] + new_num[here, :]) / den
        out[here, :] = jnp.where(within < fresh, value, 0.0).astype(BF16)


def divide(meta, parts, new_num, new_den):
    vmem = pl.BlockSpec(memory_space=pltpu.VMEM)
    return pl.pallas_call(
        divide_kernel,
        out_shape=jax.ShapeDtypeStruct((3 * PIECE, HD), BF16),
        in_specs=[pl.BlockSpec(memory_space=pltpu.SMEM), vmem, vmem, vmem],
        out_specs=vmem,
        compiler_params=pltpu.CompilerParams(vmem_limit_bytes=16 << 20),
        name="divide",
    )(meta, parts, new_num, new_den)


def spread_kernel(meta, attended, own, right, ahead, behind, left, out):
    here = meta[3 * REQS + 3]
    count = 4
    rows = attended.shape[1]
    heads = jnp.concatenate([attended[h] for h in range(attended.shape[0])], axis=1)
    padded = jnp.concatenate([heads, jnp.zeros((2 * HD - rows, heads.shape[1]), BF16)], axis=0)
    last = (((1,), (1,)), ((), ()))
    for step in range(count):
        along = lax.rem(here + step, count)
        for block in range(count):
            at = block * count + along
            if step == 2:
                weights = (ahead if block < 2 else behind)[block % 2]
            else:
                weights = (own, right, None, left)[step][block]
            wide = lax.dot_general(heads, weights[:HD], last, preferred_element_type=F32)
            rest = lax.dot_general(weights[HD:], padded, last, preferred_element_type=F32)
            out[at, :rows, :] = wide.astype(BF16)
            out[at, rows : rows + 16, :] = rest[:, :HD].astype(BF16)
            out[at, rows + 16 :, :] = rest[:, HD:].astype(BF16)


def spread(meta, attended, columns, chunks):
    vmem = pl.BlockSpec(memory_space=pltpu.VMEM)
    return pl.pallas_call(
        spread_kernel,
        out_shape=jax.ShapeDtypeStruct((chunks, attended.shape[1] + 32, HD), BF16),
        in_specs=[pl.BlockSpec(memory_space=pltpu.SMEM)] + [vmem] * (1 + len(columns)),
        out_specs=vmem,
        compiler_params=pltpu.CompilerParams(vmem_limit_bytes=32 << 20),
        name="spread",
    )(meta, attended, *columns)


def on_device(
    tokens, pre_gain, w_q, w_k, w_v, w_o, post_gain, k_cache, v_cache, cached_len, new_len, slot_offset
):
    tok_rows = tokens.shape[0]
    features = tokens.shape[1]
    n_gy = lax.axis_size(GY)
    n_chips = lax.axis_size(CHIPS)
    me = lax.axis_index(GX)
    core = lax.axis_index("c")
    cols = w_q.shape[1]

    float_in = tokens.astype(F32)
    squares = jnp.sum(float_in * float_in, axis=1, keepdims=True)
    high = lax.reduce_precision(squares, 8, 7)
    gained = float_in * (1.0 + pre_gain.astype(F32))
    gained = jnp.concatenate([gained, high, squares - high], axis=1).astype(BF16)
    weights = jnp.concatenate([w_q[:, :HD], w_k, w_q[:, HD:], w_v], axis=1)
    gained, weights = lax.optimization_barrier((gained, weights))
    gained = lax.all_gather(gained, "zl", axis=0, tiled=True)
    gained = everywhere(gained, "y", n_gy // 2).reshape(n_gy, tok_rows, -1)

    weights = lax.all_gather(weights, "c", axis=0, tiled=True)
    weights = lax.dynamic_slice_in_dim(weights, core * cols, cols, 1)
    inner = weights.shape[0]
    weights = jnp.concatenate([weights, w_o.T], axis=0)
    weights = lax.all_gather(weights, "zh", axis=0)
    w_out = weights[:, inner:, :]
    weights = weights[:, :inner, :]
    from_right = [((i + 1) % 4, i) for i in range(4)]
    from_left = [((i - 1) % 4, i) for i in range(4)]
    right = lax.ppermute(weights, "x", from_right)
    left = lax.ppermute(weights, "x", from_left)
    ahead = lax.ppermute(right[:2], "x", from_right)
    behind = lax.ppermute(left[2:], "x", from_left)
    columns = [weights, right, ahead, behind, left]
    swap = [(0, 1), (1, 0)]
    other = lax.ppermute(gained, "c", swap)

    chip_rows = me // 2 * (2 * tok_rows)
    row_ids = chip_rows + jnp.arange(2 * tok_rows, dtype=jnp.int32)
    request = row_ids // NEWTOK
    owner_mask = request[:, None] == jnp.arange(REQS, dtype=jnp.int32)[None, :]
    position = jnp.sum(jnp.where(owner_mask, cached_len[None, :], 0), axis=1) + row_ids % NEWTOK
    half = HD // 2
    inverse = jnp.power(10000.0, -2.0 * jnp.arange(half, dtype=F32) / HD)
    angle = position.astype(F32)[:, None] * inverse[None, :]
    cosine, sine = jnp.cos(angle), jnp.sin(angle)
    cosine = jnp.concatenate([cosine, cosine], axis=1)
    sine = jnp.concatenate([-sine, sine], axis=1)
    turns = jnp.stack(
        [
            cosine * query_scale,
            sine * query_scale,
            jnp.where(core == 0, cosine, 1.0),
            jnp.where(core == 0, sine, 0.0),
        ]
    )
    meta = jnp.concatenate(
        [
            cached_len,
            new_len,
            slot_offset,
            jnp.stack([me // 2 * (2 * k_cache.shape[0]), chip_rows, core, lax.axis_index("x")]).astype(jnp.int32),
        ]
    )
    k_other = lax.ppermute(k_cache, "c", swap)
    v_other = lax.ppermute(v_cache, "c", swap)
    other, k_other, v_other = lax.optimization_barrier((other, k_other, v_other))
    queries, fresh_rows = project(meta, gained, other, turns, columns)

    queries, fresh_rows, w_out = lax.optimization_barrier((queries, fresh_rows, w_out))
    out_right = lax.ppermute(w_out, "x", from_right)
    out_left = lax.ppermute(w_out, "x", from_left)
    near_rows = lax.all_gather(fresh_rows, "c", axis=0)
    all_queries = everywhere(queries, CHIPS, n_chips).reshape(-1, HD)
    all_queries, near_rows = lax.optimization_barrier((all_queries, near_rows))
    sums = attend(meta, all_queries, k_cache, v_cache, k_other, v_other)
    sums, near_rows, out_right, out_left = lax.optimization_barrier((sums, near_rows, out_right, out_left))
    near_rows = [near_rows] + [
        lax.ppermute(near_rows, "x", [((i + step) % 4, i) for i in range(4)]) for step in (1, 2, 3)
    ]
    out_columns = [
        w_out,
        out_right,
        lax.ppermute(out_right[:2], "x", from_right),
        lax.ppermute(out_left[2:], "x", from_left),
        out_left,
    ]

    parts = lax.all_to_all(sums.reshape(n_chips, -1, HD), CHIPS, 0, 0)
    new_num, new_den, kind = attend_new(meta, queries, near_rows)
    attended = divide(meta, parts, new_num, new_den)
    attended = lax.all_gather(attended, "c", axis=0)
    partial_out = spread(meta, attended, out_columns, n_gy)
    partial_out, kind = lax.optimization_barrier((partial_out, kind))
    kind = lax.all_gather(kind, "zh", axis=0, tiled=True)
    total = jnp.sum(lax.all_to_all(partial_out, GY, 0, 0).astype(F32), axis=0)
    rows = 2 * tok_rows
    rest = jnp.concatenate([total[rows : rows + 16], total[rows + 16 :, : rows - HD]], axis=1)
    branch = jnp.concatenate([total[:rows], rest.T], axis=1)
    squares = jnp.sum(branch * branch, axis=1).reshape(2, 1, 1, tok_rows)
    squares = jnp.broadcast_to(squares, (2, n_gy, 1, tok_rows)).reshape(2 * n_gy, 1, tok_rows)
    squares, kind = lax.optimization_barrier((squares, kind))
    squares = lax.all_to_all(squares, ("c",) + GY, 0, 0)
    k_pool, v_pool = write(meta, kind, lax.ppermute(kind, "c", swap), k_cache, v_cache)
    mean = jnp.sum(squares, axis=(0, 1)) / D
    kept = lax.dynamic_slice_in_dim(branch, core * tok_rows, tok_rows, 0)
    sent = lax.dynamic_slice_in_dim(branch, (1 - core) * tok_rows, tok_rows, 0)
    came = lax.ppermute(sent, "c", swap)
    branch = jnp.concatenate([jnp.where(core == 0, kept, came), jnp.where(core == 0, came, kept)], axis=1)
    layer_out = float_in + branch * lax.rsqrt(mean + epsilon)[:, None] * (1.0 + post_gain.astype(F32))
    return (layer_out.astype(BF16), k_pool, v_pool)


def solution(mesh):
    parts = Mesh(mesh.devices.reshape(4, 4, 2, 8, 2), GX + GY)
    both = P(GX, GY)
    placed = (both, P(GY), both, both, both, P(GY, GX), P(GY), both, both, P(), P(), P())
    return jax.shard_map(
        on_device, mesh=parts, in_specs=placed, out_specs=(both, both, both), check_vma=False
    )
```

```python
import jax
import jax.numpy as jnp
from jax import lax
from jax.experimental import pallas as pl
from jax.experimental.pallas import tpu as pltpu
from jax.sharding import Mesh, PartitionSpec as P

D = 4608
HD = 128
REQS = 12
NEWTOK = 192
READ_TILE = 512
WRITE_TILE = 256
PIECE = 48
epsilon = 1e-06
soft_cap = 50.0
query_scale = 144.0 ** (-0.5)
F32 = jnp.float32
BF16 = jnp.bfloat16

CHIPS = ("zh", "x")
GX = ("zh", "x", "c")
GY = ("y", "zl")


def everywhere(value, axes, count):
    return lax.all_to_all(jnp.broadcast_to(value[None], (count,) + value.shape), axes, 0, 0)


def project_kernel(meta, mine, others, turns, own, right, ahead, behind, left, *outs):
    on_core_0 = meta[3 * REQS + 2] == 0
    here = meta[3 * REQS + 3]
    features = mine.shape[2] - 2
    count = 4
    total = jnp.zeros((outs[0].shape[0], 2 * HD), F32)
    squares = jnp.zeros((outs[0].shape[0], 2), F32)
    for step in range(count):
        along = lax.rem(here + step, count)
        for block in range(count):
            at = block * count + along
            a, b = mine[at], others[at]
            rows = jnp.concatenate([jnp.where(on_core_0, a, b), jnp.where(on_core_0, b, a)], axis=0)
            squares += rows[:, features:].astype(F32)
            if step == 2:
                columns = (ahead if block < 2 else behind)[block % 2]
            else:
                columns = (own, right, None, left)[step][block]
            total += jnp.dot(rows[:, :features], columns[:features, :], preferred_element_type=F32)
    mean = jnp.sum(squares, axis=1, keepdims=True) * (1.0 / D)
    total = total * lax.rsqrt(mean + epsilon)
    for head in range(2):
        value = total[:, head * HD : (head + 1) * HD]
        value = value * turns[2 * head] + pltpu.roll(value, HD // 2, 1) * turns[2 * head + 1]
        outs[head][...] = value.astype(BF16)


def project(meta, mine, others, turns, columns):
    vmem = pl.BlockSpec(memory_space=pltpu.VMEM)
    return pl.pallas_call(
        project_kernel,
        out_shape=[jax.ShapeDtypeStruct((2 * mine.shape[1], HD), BF16)] * 2,
        in_specs=[pl.BlockSpec(memory_space=pltpu.SMEM)] + [vmem] * (3 + len(columns)),
        out_specs=[vmem, vmem],
        compiler_params=pltpu.CompilerParams(vmem_limit_bytes=32 << 20),
        name="project",
    )(meta, mine, others, turns, *columns)


def attend_kernel(meta, queries, k_own, v_own, k_other, v_other, sums, num, den, totals):
    own = k_own.shape[0]
    first = meta[3 * REQS]
    core = meta[3 * REQS + 2]
    blocks = REQS * NEWTOK // (3 * PIECE)
    chunk = sums.shape[0] // blocks
    totals[...] = jnp.zeros_like(totals)

    def read_request(r, carry):
        cached, offset = meta[r], meta[2 * REQS + r]
        num[...] = jnp.zeros_like(num)
        den[...] = jnp.zeros_like(den)
        for keys, values, at in ((k_own, v_own, core), (k_other, v_other, 1 - core)):
            begin = offset - first - at * own
            low, high = jnp.maximum(begin, 0), jnp.minimum(begin + cached, own)

            def read_tile(t, carry):
                rows = queries[pl.ds(pl.multiple_of(r * NEWTOK, 64), NEWTOK), :]
                here = pl.ds(pl.multiple_of(t * READ_TILE, READ_TILE), READ_TILE)
                logits = lax.dot_general(
                    rows, keys[here, :], (((1,), (1,)), ((), ())), preferred_element_type=F32
                )
                slot = lax.broadcasted_iota(jnp.int32, logits.shape, 1) + t * READ_TILE
                weight = jnp.exp(soft_cap * jnp.tanh(logits * (1.0 / soft_cap)))
                weight = jnp.where((slot >= low) & (slot < high), weight, 0.0).astype(BF16)
                num[...] += jnp.dot(weight, values[here, :], preferred_element_type=F32)
                den[...] += lax.dot_general(
                    jnp.ones((8, READ_TILE), BF16), weight, (((1,), (1,)), ((), ())), preferred_element_type=F32
                )
                return carry

            tiles = jnp.where(high > low, pl.cdiv(high, READ_TILE), 0)
            lax.fori_loop(lax.div(low, READ_TILE), tiles, read_tile, 0)

        for piece in range(NEWTOK // PIECE):
            at = r * (NEWTOK // PIECE) + piece
            block, part = lax.div(at, 3), lax.rem(at, 3)
            to = pl.multiple_of(block * chunk + part * PIECE, 16)
            at_row = piece * PIECE
            sums[pl.ds(to, PIECE), :] = num[at_row : at_row + PIECE, :].astype(BF16)
            totals[pl.ds(block * 8 + part, 1), 0:PIECE] = den[0:1, at_row : at_row + PIECE]
        return carry

    lax.fori_loop(0, REQS, read_request, 0)
    for block in range(blocks):
        rows = totals[block * 8 : block * 8 + 8, :]
        rows = jnp.concatenate([rows, jnp.zeros_like(rows)], axis=0)
        sums[block * chunk + 3 * PIECE : (block + 1) * chunk, :] = rows.astype(BF16)


def attend(meta, queries, k_cache, v_cache, k_other, v_other):
    blocks = REQS * NEWTOK // (3 * PIECE)
    chunk = 3 * PIECE + 16
    vmem = pl.BlockSpec(memory_space=pltpu.VMEM)
    return pl.pallas_call(
        attend_kernel,
        out_shape=jax.ShapeDtypeStruct((blocks * chunk, HD), BF16),
        in_specs=[pl.BlockSpec(memory_space=pltpu.SMEM)] + [vmem] * 5,
        out_specs=vmem,
        scratch_shapes=[
            pltpu.VMEM((NEWTOK, HD), F32),
            pltpu.VMEM((8, NEWTOK), F32),
            pltpu.VMEM((blocks * 8, HD), F32),
        ],
        compiler_params=pltpu.CompilerParams(vmem_limit_bytes=32 << 20),
        name="attend",
    )(meta, queries, k_cache, v_cache, k_other, v_other)


def attend_new_kernel(meta, queries, near, far, num, den, kind):
    here = meta[3 * REQS + 3]
    on_core_0 = meta[3 * REQS + 2] == 0
    rows, count = queries.shape[0], 4
    request = lax.div(meta[3 * REQS + 1] - here * rows, NEWTOK)
    row = lax.broadcasted_iota(jnp.int32, (rows, 1), 0) + here * rows
    start, limit = jnp.zeros_like(row), jnp.zeros_like(row)
    for part in range(count * rows // NEWTOK):
        at = part * NEWTOK
        inside = (row >= at) & (row < at + NEWTOK)
        start = jnp.where(inside, at, start)
        limit = jnp.where(inside, jnp.minimum(row, at + meta[REQS + request + part] - 1), limit)
    total, weights = jnp.zeros((rows, HD), F32), jnp.zeros((rows, 1), F32)
    for step in range(count):
        block = (near if step < 2 else far)[step % 2]
        at = lax.bitwise_xor(here, step) * rows
        logits = lax.dot_general(queries[...], block[0], (((1,), (1,)), ((), ())), preferred_element_type=F32)
        column = lax.broadcasted_iota(jnp.int32, logits.shape, 1) + at
        weight = jnp.exp(soft_cap * jnp.tanh(logits * (1.0 / soft_cap)))
        weight = jnp.where((column >= start) & (column <= limit), weight, 0.0)
        weights += jnp.sum(weight, axis=1, keepdims=True)
        total += jnp.dot(weight.astype(BF16), block[1], preferred_element_type=F32)
        kind[pl.ds(pl.multiple_of(at, 16), rows), :] = jnp.where(on_core_0, block[0], block[1])
    num[...] = total
    den[...] = weights


def attend_new(meta, queries, near, far):
    vmem = pl.BlockSpec(memory_space=pltpu.VMEM)
    rows = queries.shape[0]
    return pl.pallas_call(
        attend_new_kernel,
        out_shape=(
            jax.ShapeDtypeStruct((rows, HD), F32),
            jax.ShapeDtypeStruct((rows, 1), F32),
            jax.ShapeDtypeStruct((4 * rows, HD), BF16),
        ),
        in_specs=[pl.BlockSpec(memory_space=pltpu.SMEM)] + [vmem] * 3,
        out_specs=(vmem, vmem, vmem),
        compiler_params=pltpu.CompilerParams(vmem_limit_bytes=16 << 20),
        name="attend_new",
    )(meta, queries, near, far)


def write_kernel(meta, mine, others, k_old, v_old, k_pool, v_pool):
    slots = k_old.shape[0]
    core = meta[3 * REQS + 2]
    on_core_0 = core == 0
    first = meta[3 * REQS] + core * slots
    k_pool[...] = k_old[...]
    v_pool[...] = v_old[...]

    def write_request(r, carry):
        cached, fresh, offset = meta[r], meta[REQS + r], meta[2 * REQS + r]
        begin = offset + cached - first

        def write_tile(t, carry):
            rows = pl.ds(pl.multiple_of(r * NEWTOK, 64), NEWTOK)
            a, b = mine[rows, :], others[rows, :]
            rows = jnp.concatenate([jnp.where(on_core_0, a, b), jnp.where(on_core_0, b, a)], axis=1)
            slot = lax.broadcasted_iota(jnp.int32, (WRITE_TILE, NEWTOK), 0) + (t * WRITE_TILE - begin)
            index = lax.broadcasted_iota(jnp.int32, (WRITE_TILE, NEWTOK), 1)
            pick = jnp.where((slot == index) & (index < fresh), 1.0, 0.0).astype(BF16)
            new = jnp.dot(pick, rows, preferred_element_type=F32)
            place = lax.broadcasted_iota(jnp.int32, (WRITE_TILE, HD), 0) + (t * WRITE_TILE - begin)
            written = (place >= 0) & (place < fresh)
            here = pl.ds(pl.multiple_of(t * WRITE_TILE, WRITE_TILE), WRITE_TILE)
            k_pool[here, :] = jnp.where(written, new[:, :HD], k_pool[here, :].astype(F32)).astype(BF16)
            v_pool[here, :] = jnp.where(written, new[:, HD:], v_pool[here, :].astype(F32)).astype(BF16)
            return carry

        low, high = jnp.maximum(begin, 0), jnp.minimum(begin + fresh, slots)
        tiles = jnp.where(high > low, pl.cdiv(high, WRITE_TILE), 0)
        lax.fori_loop(lax.div(low, WRITE_TILE), tiles, write_tile, 0)
        return carry

    lax.fori_loop(0, REQS, write_request, 0)


def write(meta, mine, others, k_cache, v_cache):
    vmem = pl.BlockSpec(memory_space=pltpu.VMEM)
    return pl.pallas_call(
        write_kernel,
        out_shape=(
            jax.ShapeDtypeStruct(k_cache.shape, BF16),
            jax.ShapeDtypeStruct(v_cache.shape, BF16),
        ),
        in_specs=[pl.BlockSpec(memory_space=pltpu.SMEM)] + [vmem] * 4,
        out_specs=(vmem, vmem),
        compiler_params=pltpu.CompilerParams(vmem_limit_bytes=32 << 20),
        name="write",
    )(meta, mine, others, k_cache, v_cache)


def divide_kernel(meta, parts, new_num, new_den, out):
    fresh_at = REQS
    begin = meta[3 * REQS + 1]
    total = jnp.sum(parts[...].astype(F32), axis=0)
    for part in range(3):
        row = begin + part * PIECE
        request = row // NEWTOK
        fresh = meta[fresh_at + request]
        within = lax.broadcasted_iota(jnp.int32, (PIECE, HD), 0) + (row - request * NEWTOK)
        den = total[3 * PIECE + part : 3 * PIECE + part + 1, 0:PIECE]
        diagonal = lax.broadcasted_iota(jnp.int32, (PIECE, PIECE), 0) == lax.broadcasted_iota(
            jnp.int32, (PIECE, PIECE), 1
        )
        here = slice(part * PIECE, (part + 1) * PIECE)
        den = jnp.sum(jnp.where(diagonal, den, 0.0), axis=1, keepdims=True) + new_den[here, :]
        value = (total[here, :] + new_num[here, :]) / den
        out[here, :] = jnp.where(within < fresh, value, 0.0).astype(BF16)


def divide(meta, parts, new_num, new_den):
    vmem = pl.BlockSpec(memory_space=pltpu.VMEM)
    return pl.pallas_call(
        divide_kernel,
        out_shape=jax.ShapeDtypeStruct((3 * PIECE, HD), BF16),
        in_specs=[pl.BlockSpec(memory_space=pltpu.SMEM), vmem, vmem, vmem],
        out_specs=vmem,
        compiler_params=pltpu.CompilerParams(vmem_limit_bytes=16 << 20),
        name="divide",
    )(meta, parts, new_num, new_den)


def spread_kernel(meta, attended, own, right, ahead, behind, left, out):
    here = meta[3 * REQS + 3]
    count = 4
    rows = attended.shape[1]
    heads = jnp.concatenate([attended[h] for h in range(attended.shape[0])], axis=1)
    padded = jnp.concatenate([heads, jnp.zeros((2 * HD - rows, heads.shape[1]), BF16)], axis=0)
    last = (((1,), (1,)), ((), ()))
    for step in range(count):
        along = lax.rem(here + step, count)
        for block in range(count):
            at = block * count + along
            if step == 2:
                weights = (ahead if block < 2 else behind)[block % 2]
            else:
                weights = (own, right, None, left)[step][block]
            wide = lax.dot_general(heads, weights[:HD], last, preferred_element_type=F32)
            rest = lax.dot_general(weights[HD:], padded, last, preferred_element_type=F32)
            out[at, :rows, :] = wide.astype(BF16)
            out[at, rows : rows + 16, :] = rest[:, :HD].astype(BF16)
            out[at, rows + 16 :, :] = rest[:, HD:].astype(BF16)


def spread(meta, attended, columns, chunks):
    vmem = pl.BlockSpec(memory_space=pltpu.VMEM)
    return pl.pallas_call(
        spread_kernel,
        out_shape=jax.ShapeDtypeStruct((chunks, attended.shape[1] + 32, HD), BF16),
        in_specs=[pl.BlockSpec(memory_space=pltpu.SMEM)] + [vmem] * (1 + len(columns)),
        out_specs=vmem,
        compiler_params=pltpu.CompilerParams(vmem_limit_bytes=32 << 20),
        name="spread",
    )(meta, attended, *columns)


def on_device(
    tokens, pre_gain, w_q, w_k, w_v, w_o, post_gain, k_cache, v_cache, cached_len, new_len, slot_offset
):
    tok_rows = tokens.shape[0]
    features = tokens.shape[1]
    n_gy = lax.axis_size(GY)
    n_chips = lax.axis_size(CHIPS)
    me = lax.axis_index(GX)
    core = lax.axis_index("c")
    cols = w_q.shape[1]

    float_in = tokens.astype(F32)
    squares = jnp.sum(float_in * float_in, axis=1, keepdims=True)
    high = lax.reduce_precision(squares, 8, 7)
    gained = float_in * (1.0 + pre_gain.astype(F32))
    gained = jnp.concatenate([gained, high, squares - high], axis=1).astype(BF16)
    weights = jnp.concatenate([w_q[:, :HD], w_k, w_q[:, HD:], w_v], axis=1)
    gained, weights = lax.optimization_barrier((gained, weights))
    gained = lax.all_gather(gained, "zl", axis=0, tiled=True)
    gained = everywhere(gained, "y", n_gy // 2).reshape(n_gy, tok_rows, -1)

    weights = lax.all_gather(weights, "c", axis=0, tiled=True)
    weights = lax.dynamic_slice_in_dim(weights, core * cols, cols, 1)
    inner = weights.shape[0]
    weights = jnp.concatenate([weights, w_o.T], axis=0)
    weights = lax.all_gather(weights, "zh", axis=0)
    w_out = weights[:, inner:, :]
    weights = weights[:, :inner, :]
    from_right = [((i + 1) % 4, i) for i in range(4)]
    from_left = [((i - 1) % 4, i) for i in range(4)]
    right = lax.ppermute(weights, "x", from_right)
    left = lax.ppermute(weights, "x", from_left)
    ahead = lax.ppermute(right[:2], "x", from_right)
    behind = lax.ppermute(left[2:], "x", from_left)
    columns = [weights, right, ahead, behind, left]
    swap = [(0, 1), (1, 0)]
    other = lax.ppermute(gained, "c", swap)

    chip_rows = me // 2 * (2 * tok_rows)
    row_ids = chip_rows + jnp.arange(2 * tok_rows, dtype=jnp.int32)
    request = row_ids // NEWTOK
    owner_mask = request[:, None] == jnp.arange(REQS, dtype=jnp.int32)[None, :]
    position = jnp.sum(jnp.where(owner_mask, cached_len[None, :], 0), axis=1) + row_ids % NEWTOK
    half = HD // 2
    inverse = jnp.power(10000.0, -2.0 * jnp.arange(half, dtype=F32) / HD)
    angle = position.astype(F32)[:, None] * inverse[None, :]
    cosine, sine = jnp.cos(angle), jnp.sin(angle)
    cosine = jnp.concatenate([cosine, cosine], axis=1)
    sine = jnp.concatenate([-sine, sine], axis=1)
    turns = jnp.stack(
        [
            cosine * query_scale,
            sine * query_scale,
            jnp.where(core == 0, cosine, 1.0),
            jnp.where(core == 0, sine, 0.0),
        ]
    )
    meta = jnp.concatenate(
        [
            cached_len,
            new_len,
            slot_offset,
            jnp.stack([me // 2 * (2 * k_cache.shape[0]), chip_rows, core, lax.axis_index("x")]).astype(jnp.int32),
        ]
    )
    k_other = lax.ppermute(k_cache, "c", swap)
    v_other = lax.ppermute(v_cache, "c", swap)
    other, k_other, v_other = lax.optimization_barrier((other, k_other, v_other))
    queries, fresh_rows = project(meta, gained, other, turns, columns)

    queries, fresh_rows, w_out = lax.optimization_barrier((queries, fresh_rows, w_out))
    out_right = lax.ppermute(w_out, "x", from_right)
    out_left = lax.ppermute(w_out, "x", from_left)
    near_rows = lax.all_gather(fresh_rows, "c", axis=0)
    near_rows = jnp.stack([near_rows, lax.ppermute(near_rows, "x", [(i, i ^ 1) for i in range(4)])])
    all_queries = everywhere(queries, CHIPS, n_chips).reshape(-1, HD)
    all_queries, near_rows = lax.optimization_barrier((all_queries, near_rows))
    sums = attend(meta, all_queries, k_cache, v_cache, k_other, v_other)
    sums, near_rows, out_right, out_left = lax.optimization_barrier((sums, near_rows, out_right, out_left))
    far_rows = lax.ppermute(near_rows, "x", [(i, i ^ 2) for i in range(4)])
    out_columns = [
        w_out,
        out_right,
        lax.ppermute(out_right[:2], "x", from_right),
        lax.ppermute(out_left[2:], "x", from_left),
        out_left,
    ]

    parts = lax.all_to_all(sums.reshape(n_chips, -1, HD), CHIPS, 0, 0)
    new_num, new_den, kind = attend_new(meta, queries, near_rows, far_rows)
    attended = divide(meta, parts, new_num, new_den)
    attended = lax.all_gather(attended, "c", axis=0)
    partial_out = spread(meta, attended, out_columns, n_gy)
    partial_out, kind = lax.optimization_barrier((partial_out, kind))
    kind = lax.all_gather(kind, "zh", axis=0, tiled=True)
    total = jnp.sum(lax.all_to_all(partial_out, GY, 0, 0).astype(F32), axis=0)
    rows = 2 * tok_rows
    rest = jnp.concatenate([total[rows : rows + 16], total[rows + 16 :, : rows - HD]], axis=1)
    branch = jnp.concatenate([total[:rows], rest.T], axis=1)
    squares = jnp.sum(branch * branch, axis=1).reshape(2, 1, 1, tok_rows)
    squares = jnp.broadcast_to(squares, (2, n_gy, 1, tok_rows)).reshape(2 * n_gy, 1, tok_rows)
    squares, kind = lax.optimization_barrier((squares, kind))
    squares = lax.all_to_all(squares, ("c",) + GY, 0, 0)
    k_pool, v_pool = write(meta, kind, lax.ppermute(kind, "c", swap), k_cache, v_cache)
    mean = jnp.sum(squares, axis=(0, 1)) / D
    kept = lax.dynamic_slice_in_dim(branch, core * tok_rows, tok_rows, 0)
    sent = lax.dynamic_slice_in_dim(branch, (1 - core) * tok_rows, tok_rows, 0)
    came = lax.ppermute(sent, "c", swap)
    branch = jnp.concatenate([jnp.where(core == 0, kept, came), jnp.where(core == 0, came, kept)], axis=1)
    layer_out = float_in + branch * lax.rsqrt(mean + epsilon)[:, None] * (1.0 + post_gain.astype(F32))
    return (layer_out.astype(BF16), k_pool, v_pool)


def solution(mesh):
    parts = Mesh(mesh.devices.reshape(4, 4, 2, 8, 2), GX + GY)
    both = P(GX, GY)
    placed = (both, P(GY), both, both, both, P(GY, GX), P(GY), both, both, P(), P(), P())
    return jax.shard_map(
        on_device, mesh=parts, in_specs=placed, out_specs=(both, both, both), check_vma=False
    )
```

```python
import jax
import jax.numpy as jnp
from jax import lax
from jax.experimental import pallas as pl
from jax.experimental.pallas import tpu as pltpu
from jax.sharding import Mesh, PartitionSpec as P

D = 4608
HD = 128
REQS = 12
NEWTOK = 192
READ_TILE = 512
WRITE_TILE = 256
PIECE = 48
epsilon = 1e-06
soft_cap = 50.0
query_scale = 144.0 ** (-0.5)
F32 = jnp.float32
BF16 = jnp.bfloat16

CHIPS = ("zh", "x")
GX = ("zh", "x", "c")
GY = ("y", "zl")


def everywhere(value, axes, count):
    return lax.all_to_all(jnp.broadcast_to(value[None], (count,) + value.shape), axes, 0, 0)


def project_kernel(meta, mine, others, turns, own, right, ahead, behind, left, *outs):
    on_core_0 = meta[3 * REQS + 2] == 0
    here = meta[3 * REQS + 3]
    features = mine.shape[2] - 2
    count = 4
    total = jnp.zeros((outs[0].shape[0], 2 * HD), F32)
    squares = jnp.zeros((outs[0].shape[0], 2), F32)
    for step in range(count):
        along = lax.rem(here + step, count)
        for block in range(count):
            at = block * count + along
            a, b = mine[at], others[at]
            rows = jnp.concatenate([jnp.where(on_core_0, a, b), jnp.where(on_core_0, b, a)], axis=0)
            squares += rows[:, features:].astype(F32)
            if step == 2:
                columns = (ahead if block < 2 else behind)[block % 2]
            else:
                columns = (own, right, None, left)[step][block]
            total += jnp.dot(rows[:, :features], columns[:features, :], preferred_element_type=F32)
    mean = jnp.sum(squares, axis=1, keepdims=True) * (1.0 / D)
    total = total * lax.rsqrt(mean + epsilon)
    for head in range(2):
        value = total[:, head * HD : (head + 1) * HD]
        value = value * turns[2 * head] + pltpu.roll(value, HD // 2, 1) * turns[2 * head + 1]
        outs[head][...] = value.astype(BF16)


def project(meta, mine, others, turns, columns):
    vmem = pl.BlockSpec(memory_space=pltpu.VMEM)
    return pl.pallas_call(
        project_kernel,
        out_shape=[jax.ShapeDtypeStruct((2 * mine.shape[1], HD), BF16)] * 2,
        in_specs=[pl.BlockSpec(memory_space=pltpu.SMEM)] + [vmem] * (3 + len(columns)),
        out_specs=[vmem, vmem],
        compiler_params=pltpu.CompilerParams(vmem_limit_bytes=32 << 20),
        name="project",
    )(meta, mine, others, turns, *columns)


def attend_kernel(meta, queries, k_own, v_own, k_other, v_other, sums, num, den, totals):
    own = k_own.shape[0]
    first = meta[3 * REQS]
    core = meta[3 * REQS + 2]
    blocks = REQS * NEWTOK // (3 * PIECE)
    chunk = sums.shape[0] // blocks
    totals[...] = jnp.zeros_like(totals)

    def read_request(r, carry):
        cached, offset = meta[r], meta[2 * REQS + r]
        num[...] = jnp.zeros_like(num)
        den[...] = jnp.zeros_like(den)
        for keys, values, at in ((k_own, v_own, core), (k_other, v_other, 1 - core)):
            begin = offset - first - at * own
            low, high = jnp.maximum(begin, 0), jnp.minimum(begin + cached, own)

            def read_tile(t, carry):
                rows = queries[pl.ds(pl.multiple_of(r * NEWTOK, 64), NEWTOK), :]
                here = pl.ds(pl.multiple_of(t * READ_TILE, READ_TILE), READ_TILE)
                logits = lax.dot_general(
                    rows, keys[here, :], (((1,), (1,)), ((), ())), preferred_element_type=F32
                )
                slot = lax.broadcasted_iota(jnp.int32, logits.shape, 1) + t * READ_TILE
                weight = jnp.exp(soft_cap * jnp.tanh(logits * (1.0 / soft_cap)))
                weight = jnp.where((slot >= low) & (slot < high), weight, 0.0).astype(BF16)
                num[...] += jnp.dot(weight, values[here, :], preferred_element_type=F32)
                den[...] += lax.dot_general(
                    jnp.ones((8, READ_TILE), BF16), weight, (((1,), (1,)), ((), ())), preferred_element_type=F32
                )
                return carry

            tiles = jnp.where(high > low, pl.cdiv(high, READ_TILE), 0)
            lax.fori_loop(lax.div(low, READ_TILE), tiles, read_tile, 0)

        for piece in range(NEWTOK // PIECE):
            at = r * (NEWTOK // PIECE) + piece
            block, part = lax.div(at, 3), lax.rem(at, 3)
            to = pl.multiple_of(block * chunk + part * PIECE, 16)
            at_row = piece * PIECE
            sums[pl.ds(to, PIECE), :] = num[at_row : at_row + PIECE, :].astype(BF16)
            totals[pl.ds(block * 8 + part, 1), 0:PIECE] = den[0:1, at_row : at_row + PIECE]
        return carry

    lax.fori_loop(0, REQS, read_request, 0)
    for block in range(blocks):
        rows = totals[block * 8 : block * 8 + 8, :]
        rows = jnp.concatenate([rows, jnp.zeros_like(rows)], axis=0)
        sums[block * chunk + 3 * PIECE : (block + 1) * chunk, :] = rows.astype(BF16)


def attend(meta, queries, k_cache, v_cache, k_other, v_other):
    blocks = REQS * NEWTOK // (3 * PIECE)
    chunk = 3 * PIECE + 16
    vmem = pl.BlockSpec(memory_space=pltpu.VMEM)
    return pl.pallas_call(
        attend_kernel,
        out_shape=jax.ShapeDtypeStruct((blocks * chunk, HD), BF16),
        in_specs=[pl.BlockSpec(memory_space=pltpu.SMEM)] + [vmem] * 5,
        out_specs=vmem,
        scratch_shapes=[
            pltpu.VMEM((NEWTOK, HD), F32),
            pltpu.VMEM((8, NEWTOK), F32),
            pltpu.VMEM((blocks * 8, HD), F32),
        ],
        compiler_params=pltpu.CompilerParams(vmem_limit_bytes=32 << 20),
        name="attend",
    )(meta, queries, k_cache, v_cache, k_other, v_other)


def attend_new_kernel(meta, queries, near, far, num, den, kind):
    here = meta[3 * REQS + 3]
    on_core_0 = meta[3 * REQS + 2] == 0
    rows, count = queries.shape[0], 4
    request = lax.div(meta[3 * REQS + 1] - here * rows, NEWTOK)
    row = lax.broadcasted_iota(jnp.int32, (rows, 1), 0) + here * rows
    start, limit = jnp.zeros_like(row), jnp.zeros_like(row)
    for part in range(count * rows // NEWTOK):
        at = part * NEWTOK
        inside = (row >= at) & (row < at + NEWTOK)
        start = jnp.where(inside, at, start)
        limit = jnp.where(inside, jnp.minimum(row, at + meta[REQS + request + part] - 1), limit)
    total, weights = jnp.zeros((rows, HD), F32), jnp.zeros((rows, 1), F32)
    for step in range(count):
        block = (near if step < 2 else far)[step % 2]
        at = lax.bitwise_xor(here, step) * rows
        logits = lax.dot_general(queries[...], block[0], (((1,), (1,)), ((), ())), preferred_element_type=F32)
        column = lax.broadcasted_iota(jnp.int32, logits.shape, 1) + at
        weight = jnp.exp(soft_cap * jnp.tanh(logits * (1.0 / soft_cap)))
        weight = jnp.where((column >= start) & (column <= limit), weight, 0.0)
        weights += jnp.sum(weight, axis=1, keepdims=True)
        total += jnp.dot(weight.astype(BF16), block[1], preferred_element_type=F32)
        kind[pl.ds(pl.multiple_of(at, 16), rows), :] = jnp.where(on_core_0, block[0], block[1])
    num[...] = total
    den[...] = weights


def attend_new(meta, queries, near, far):
    vmem = pl.BlockSpec(memory_space=pltpu.VMEM)
    rows = queries.shape[0]
    return pl.pallas_call(
        attend_new_kernel,
        out_shape=(
            jax.ShapeDtypeStruct((rows, HD), F32),
            jax.ShapeDtypeStruct((rows, 1), F32),
            jax.ShapeDtypeStruct((4 * rows, HD), BF16),
        ),
        in_specs=[pl.BlockSpec(memory_space=pltpu.SMEM)] + [vmem] * 3,
        out_specs=(vmem, vmem, vmem),
        compiler_params=pltpu.CompilerParams(vmem_limit_bytes=16 << 20),
        name="attend_new",
    )(meta, queries, near, far)


def write_kernel(meta, mine, others, k_old, v_old, k_pool, v_pool):
    slots = k_old.shape[0]
    core = meta[3 * REQS + 2]
    on_core_0 = core == 0
    first = meta[3 * REQS] + core * slots
    k_pool[...] = k_old[...]
    v_pool[...] = v_old[...]

    def write_request(r, carry):
        cached, fresh, offset = meta[r], meta[REQS + r], meta[2 * REQS + r]
        begin = offset + cached - first

        def write_tile(t, carry):
            rows = pl.ds(pl.multiple_of(r * NEWTOK, 64), NEWTOK)
            a, b = mine[rows, :], others[rows, :]
            rows = jnp.concatenate([jnp.where(on_core_0, a, b), jnp.where(on_core_0, b, a)], axis=1)
            slot = lax.broadcasted_iota(jnp.int32, (WRITE_TILE, NEWTOK), 0) + (t * WRITE_TILE - begin)
            index = lax.broadcasted_iota(jnp.int32, (WRITE_TILE, NEWTOK), 1)
            pick = jnp.where((slot == index) & (index < fresh), 1.0, 0.0).astype(BF16)
            new = jnp.dot(pick, rows, preferred_element_type=F32)
            place = lax.broadcasted_iota(jnp.int32, (WRITE_TILE, HD), 0) + (t * WRITE_TILE - begin)
            written = (place >= 0) & (place < fresh)
            here = pl.ds(pl.multiple_of(t * WRITE_TILE, WRITE_TILE), WRITE_TILE)
            k_pool[here, :] = jnp.where(written, new[:, :HD], k_pool[here, :].astype(F32)).astype(BF16)
            v_pool[here, :] = jnp.where(written, new[:, HD:], v_pool[here, :].astype(F32)).astype(BF16)
            return carry

        low, high = jnp.maximum(begin, 0), jnp.minimum(begin + fresh, slots)
        tiles = jnp.where(high > low, pl.cdiv(high, WRITE_TILE), 0)
        lax.fori_loop(lax.div(low, WRITE_TILE), tiles, write_tile, 0)
        return carry

    lax.fori_loop(0, REQS, write_request, 0)


def write(meta, mine, others, k_cache, v_cache):
    vmem = pl.BlockSpec(memory_space=pltpu.VMEM)
    return pl.pallas_call(
        write_kernel,
        out_shape=(
            jax.ShapeDtypeStruct(k_cache.shape, BF16),
            jax.ShapeDtypeStruct(v_cache.shape, BF16),
        ),
        in_specs=[pl.BlockSpec(memory_space=pltpu.SMEM)] + [vmem] * 4,
        out_specs=(vmem, vmem),
        compiler_params=pltpu.CompilerParams(vmem_limit_bytes=32 << 20),
        name="write",
    )(meta, mine, others, k_cache, v_cache)


def divide_kernel(meta, parts, new_num, new_den, out):
    fresh_at = REQS
    begin = meta[3 * REQS + 1]
    total = jnp.sum(parts[...].astype(F32), axis=0)
    for part in range(3):
        row = begin + part * PIECE
        request = row // NEWTOK
        fresh = meta[fresh_at + request]
        within = lax.broadcasted_iota(jnp.int32, (PIECE, HD), 0) + (row - request * NEWTOK)
        den = total[3 * PIECE + part : 3 * PIECE + part + 1, 0:PIECE]
        diagonal = lax.broadcasted_iota(jnp.int32, (PIECE, PIECE), 0) == lax.broadcasted_iota(
            jnp.int32, (PIECE, PIECE), 1
        )
        here = slice(part * PIECE, (part + 1) * PIECE)
        den = jnp.sum(jnp.where(diagonal, den, 0.0), axis=1, keepdims=True) + new_den[here, :]
        value = (total[here, :] + new_num[here, :]) / den
        out[here, :] = jnp.where(within < fresh, value, 0.0).astype(BF16)


def divide(meta, parts, new_num, new_den):
    vmem = pl.BlockSpec(memory_space=pltpu.VMEM)
    return pl.pallas_call(
        divide_kernel,
        out_shape=jax.ShapeDtypeStruct((3 * PIECE, HD), BF16),
        in_specs=[pl.BlockSpec(memory_space=pltpu.SMEM), vmem, vmem, vmem],
        out_specs=vmem,
        compiler_params=pltpu.CompilerParams(vmem_limit_bytes=16 << 20),
        name="divide",
    )(meta, parts, new_num, new_den)


def spread_kernel(meta, attended, own, right, ahead, behind, left, out):
    here = meta[3 * REQS + 3]
    count = 4
    rows = attended.shape[1]
    heads = jnp.concatenate([attended[h] for h in range(attended.shape[0])], axis=1)
    padded = jnp.concatenate([heads, jnp.zeros((2 * HD - rows, heads.shape[1]), BF16)], axis=0)
    last = (((1,), (1,)), ((), ()))
    for step in range(count):
        along = lax.rem(here + step, count)
        for block in range(count):
            at = block * count + along
            if step == 2:
                weights = (ahead if block < 2 else behind)[block % 2]
            else:
                weights = (own, right, None, left)[step][block]
            wide = lax.dot_general(heads, weights[:HD], last, preferred_element_type=F32)
            rest = lax.dot_general(weights[HD:], padded, last, preferred_element_type=F32)
            out[at, :rows, :] = wide.astype(BF16)
            out[at, rows : rows + 16, :] = rest[:, :HD].astype(BF16)
            out[at, rows + 16 :, :] = rest[:, HD:].astype(BF16)


def spread(meta, attended, columns, chunks):
    vmem = pl.BlockSpec(memory_space=pltpu.VMEM)
    return pl.pallas_call(
        spread_kernel,
        out_shape=jax.ShapeDtypeStruct((chunks, attended.shape[1] + 32, HD), BF16),
        in_specs=[pl.BlockSpec(memory_space=pltpu.SMEM)] + [vmem] * (1 + len(columns)),
        out_specs=vmem,
        compiler_params=pltpu.CompilerParams(vmem_limit_bytes=32 << 20),
        name="spread",
    )(meta, attended, *columns)


def on_device(
    tokens, pre_gain, w_q, w_k, w_v, w_o, post_gain, k_cache, v_cache, cached_len, new_len, slot_offset
):
    tok_rows = tokens.shape[0]
    features = tokens.shape[1]
    n_gy = lax.axis_size(GY)
    n_chips = lax.axis_size(CHIPS)
    me = lax.axis_index(GX)
    core = lax.axis_index("c")
    cols = w_q.shape[1]

    float_in = tokens.astype(F32)
    squares = jnp.sum(float_in * float_in, axis=1, keepdims=True)
    high = lax.reduce_precision(squares, 8, 7)
    gained = float_in * (1.0 + pre_gain.astype(F32))
    gained = jnp.concatenate([gained, high, squares - high], axis=1).astype(BF16)
    swap = [(0, 1), (1, 0)]
    first, second = jnp.concatenate([w_q[:, :HD], w_k], axis=1), jnp.concatenate([w_q[:, HD:], w_v], axis=1)
    weights = jnp.where(core == 0, first, second)
    came = lax.ppermute(jnp.where(core == 0, second, first), "c", swap)
    gained, weights = lax.optimization_barrier((gained, weights))
    gained = lax.all_gather(gained, "zl", axis=0, tiled=True)
    gained, came = lax.optimization_barrier((gained, came))
    gained = everywhere(gained, "y", n_gy // 2).reshape(n_gy, tok_rows, -1)
    weights = jnp.concatenate([jnp.where(core == 0, weights, came), jnp.where(core == 0, came, weights)], axis=0)
    inner = weights.shape[0]
    weights = jnp.concatenate([weights, w_o.T], axis=0)
    weights = lax.all_gather(weights, "zh", axis=0)
    w_out = weights[:, inner:, :]
    weights = weights[:, :inner, :]
    from_right = [((i + 1) % 4, i) for i in range(4)]
    from_left = [((i - 1) % 4, i) for i in range(4)]
    right = lax.ppermute(weights, "x", from_right)
    left = lax.ppermute(weights, "x", from_left)
    ahead = lax.ppermute(right[:2], "x", from_right)
    behind = lax.ppermute(left[2:], "x", from_left)
    columns = [weights, right, ahead, behind, left]
    other = lax.ppermute(gained, "c", swap)

    chip_rows = me // 2 * (2 * tok_rows)
    row_ids = chip_rows + jnp.arange(2 * tok_rows, dtype=jnp.int32)
    request = row_ids // NEWTOK
    owner_mask = request[:, None] == jnp.arange(REQS, dtype=jnp.int32)[None, :]
    position = jnp.sum(jnp.where(owner_mask, cached_len[None, :], 0), axis=1) + row_ids % NEWTOK
    half = HD // 2
    inverse = jnp.power(10000.0, -2.0 * jnp.arange(half, dtype=F32) / HD)
    angle = position.astype(F32)[:, None] * inverse[None, :]
    cosine, sine = jnp.cos(angle), jnp.sin(angle)
    cosine = jnp.concatenate([cosine, cosine], axis=1)
    sine = jnp.concatenate([-sine, sine], axis=1)
    turns = jnp.stack(
        [
            cosine * query_scale,
            sine * query_scale,
            jnp.where(core == 0, cosine, 1.0),
            jnp.where(core == 0, sine, 0.0),
        ]
    )
    meta = jnp.concatenate(
        [
            cached_len,
            new_len,
            slot_offset,
            jnp.stack([me // 2 * (2 * k_cache.shape[0]), chip_rows, core, lax.axis_index("x")]).astype(jnp.int32),
        ]
    )
    k_other = lax.ppermute(k_cache, "c", swap)
    v_other = lax.ppermute(v_cache, "c", swap)
    other, k_other, v_other = lax.optimization_barrier((other, k_other, v_other))
    queries, fresh_rows = project(meta, gained, other, turns, columns)

    queries, fresh_rows, w_out = lax.optimization_barrier((queries, fresh_rows, w_out))
    out_right = lax.ppermute(w_out, "x", from_right)
    out_left = lax.ppermute(w_out, "x", from_left)
    near_rows = lax.all_gather(fresh_rows, "c", axis=0)
    partner_rows = lax.ppermute(near_rows, "x", [(i, i ^ 1) for i in range(4)])
    all_queries = everywhere(queries, CHIPS, n_chips).reshape(-1, HD)
    all_queries, near_rows = lax.optimization_barrier((all_queries, near_rows))
    sums = attend(meta, all_queries, k_cache, v_cache, k_other, v_other)
    sums, near_rows, partner_rows, out_right, out_left = lax.optimization_barrier(
        (sums, near_rows, partner_rows, out_right, out_left)
    )
    near_rows = jnp.stack([near_rows, partner_rows])
    far_rows = lax.ppermute(near_rows, "x", [(i, i ^ 2) for i in range(4)])
    out_columns = [
        w_out,
        out_right,
        lax.ppermute(out_right[:2], "x", from_right),
        lax.ppermute(out_left[2:], "x", from_left),
        out_left,
    ]

    parts = lax.all_to_all(sums.reshape(n_chips, -1, HD), CHIPS, 0, 0)
    new_num, new_den, kind = attend_new(meta, queries, near_rows, far_rows)
    attended = divide(meta, parts, new_num, new_den)
    attended = lax.all_gather(attended, "c", axis=0)
    partial_out = spread(meta, attended, out_columns, n_gy)
    partial_out, kind = lax.optimization_barrier((partial_out, kind))
    kind = lax.all_gather(kind, "zh", axis=0, tiled=True)
    total = jnp.sum(lax.all_to_all(partial_out, GY, 0, 0).astype(F32), axis=0)
    rows = 2 * tok_rows
    rest = jnp.concatenate([total[rows : rows + 16], total[rows + 16 :, : rows - HD]], axis=1)
    branch = jnp.concatenate([total[:rows], rest.T], axis=1)
    squares = jnp.sum(branch * branch, axis=1).reshape(2, 1, 1, tok_rows)
    squares = jnp.broadcast_to(squares, (2, n_gy, 1, tok_rows)).reshape(2 * n_gy, 1, tok_rows)
    squares, kind = lax.optimization_barrier((squares, kind))
    squares = lax.all_to_all(squares, ("c",) + GY, 0, 0)
    k_pool, v_pool = write(meta, kind, lax.ppermute(kind, "c", swap), k_cache, v_cache)
    mean = jnp.sum(squares, axis=(0, 1)) / D
    kept = lax.dynamic_slice_in_dim(branch, core * tok_rows, tok_rows, 0)
    sent = lax.dynamic_slice_in_dim(branch, (1 - core) * tok_rows, tok_rows, 0)
    came = lax.ppermute(sent, "c", swap)
    branch = jnp.concatenate([jnp.where(core == 0, kept, came), jnp.where(core == 0, came, kept)], axis=1)
    layer_out = float_in + branch * lax.rsqrt(mean + epsilon)[:, None] * (1.0 + post_gain.astype(F32))
    return (layer_out.astype(BF16), k_pool, v_pool)


def solution(mesh):
    parts = Mesh(mesh.devices.reshape(4, 4, 2, 8, 2), GX + GY)
    both = P(GX, GY)
    placed = (both, P(GY), both, both, both, P(GY, GX), P(GY), both, both, P(), P(), P())
    return jax.shard_map(
        on_device, mesh=parts, in_specs=placed, out_specs=(both, both, both), check_vma=False
    )
```

```python
import jax
import jax.numpy as jnp
from jax import lax
from jax.experimental import pallas as pl
from jax.experimental.pallas import tpu as pltpu
from jax.sharding import Mesh, PartitionSpec as P

D = 4608
HD = 128
REQS = 12
NEWTOK = 192
READ_TILE = 512
WRITE_TILE = 256
PIECE = 48
epsilon = 1e-06
soft_cap = 50.0
query_scale = 144.0 ** (-0.5)
F32 = jnp.float32
BF16 = jnp.bfloat16

CHIPS = ("zh", "x")
GX = ("zh", "x", "c")
GY = ("y", "zl")


def everywhere(value, axes, count):
    return lax.all_to_all(jnp.broadcast_to(value[None], (count,) + value.shape), axes, 0, 0)


def project_kernel(meta, mine, others, turns, own, right, ahead, behind, left, *outs):
    on_core_0 = meta[3 * REQS + 2] == 0
    here = meta[3 * REQS + 3]
    features = mine.shape[2] - 2
    count = 4
    total = jnp.zeros((outs[0].shape[0], 2 * HD), F32)
    squares = jnp.zeros((outs[0].shape[0], 2), F32)
    for step in range(count):
        along = lax.rem(here + step, count)
        for block in range(count):
            at = block * count + along
            a, b = mine[at], others[at]
            rows = jnp.concatenate([jnp.where(on_core_0, a, b), jnp.where(on_core_0, b, a)], axis=0)
            squares += rows[:, features:].astype(F32)
            if step == 2:
                columns = (ahead if block < 2 else behind)[block % 2]
            else:
                columns = (own, right, None, left)[step][block]
            total += jnp.dot(rows[:, :features], columns[:features, :], preferred_element_type=F32)
    mean = jnp.sum(squares, axis=1, keepdims=True) * (1.0 / D)
    total = total * lax.rsqrt(mean + epsilon)
    for head in range(2):
        value = total[:, head * HD : (head + 1) * HD]
        value = value * turns[2 * head] + pltpu.roll(value, HD // 2, 1) * turns[2 * head + 1]
        outs[head][...] = value.astype(BF16)


def project(meta, mine, others, turns, columns):
    vmem = pl.BlockSpec(memory_space=pltpu.VMEM)
    return pl.pallas_call(
        project_kernel,
        out_shape=[jax.ShapeDtypeStruct((2 * mine.shape[1], HD), BF16)] * 2,
        in_specs=[pl.BlockSpec(memory_space=pltpu.SMEM)] + [vmem] * (3 + len(columns)),
        out_specs=[vmem, vmem],
        compiler_params=pltpu.CompilerParams(vmem_limit_bytes=32 << 20),
        name="project",
    )(meta, mine, others, turns, *columns)


def attend_kernel(meta, queries, k_own, v_own, others, sums, num, den, totals):
    own = k_own.shape[0]
    first = meta[3 * REQS]
    core = meta[3 * REQS + 2]
    blocks = REQS * NEWTOK // (3 * PIECE)
    chunk = sums.shape[0] // blocks
    totals[...] = jnp.zeros_like(totals)

    def read_request(r, carry):
        cached, offset = meta[r], meta[2 * REQS + r]
        num[...] = jnp.zeros_like(num)
        den[...] = jnp.zeros_like(den)
        for keys, values, at in ((k_own, v_own, core), (others.at[:own, :], others.at[own:, :], 1 - core)):
            begin = offset - first - at * own
            low, high = jnp.maximum(begin, 0), jnp.minimum(begin + cached, own)

            def read_tile(t, carry):
                rows = queries[pl.ds(pl.multiple_of(r * NEWTOK, 64), NEWTOK), :]
                here = pl.ds(pl.multiple_of(t * READ_TILE, READ_TILE), READ_TILE)
                logits = lax.dot_general(
                    rows, keys[here, :], (((1,), (1,)), ((), ())), preferred_element_type=F32
                )
                slot = lax.broadcasted_iota(jnp.int32, logits.shape, 1) + t * READ_TILE
                weight = jnp.exp(soft_cap * jnp.tanh(logits * (1.0 / soft_cap)))
                weight = jnp.where((slot >= low) & (slot < high), weight, 0.0).astype(BF16)
                num[...] += jnp.dot(weight, values[here, :], preferred_element_type=F32)
                den[...] += lax.dot_general(
                    jnp.ones((8, READ_TILE), BF16), weight, (((1,), (1,)), ((), ())), preferred_element_type=F32
                )
                return carry

            tiles = jnp.where(high > low, pl.cdiv(high, READ_TILE), 0)
            lax.fori_loop(lax.div(low, READ_TILE), tiles, read_tile, 0)

        for piece in range(NEWTOK // PIECE):
            at = r * (NEWTOK // PIECE) + piece
            block, part = lax.div(at, 3), lax.rem(at, 3)
            to = pl.multiple_of(block * chunk + part * PIECE, 16)
            at_row = piece * PIECE
            sums[pl.ds(to, PIECE), :] = num[at_row : at_row + PIECE, :].astype(BF16)
            totals[pl.ds(block * 8 + part, 1), 0:PIECE] = den[0:1, at_row : at_row + PIECE]
        return carry

    lax.fori_loop(0, REQS, read_request, 0)
    for block in range(blocks):
        rows = totals[block * 8 : block * 8 + 8, :]
        rows = jnp.concatenate([rows, jnp.zeros_like(rows)], axis=0)
        sums[block * chunk + 3 * PIECE : (block + 1) * chunk, :] = rows.astype(BF16)


def attend(meta, queries, k_cache, v_cache, others):
    blocks = REQS * NEWTOK // (3 * PIECE)
    chunk = 3 * PIECE + 16
    vmem = pl.BlockSpec(memory_space=pltpu.VMEM)
    return pl.pallas_call(
        attend_kernel,
        out_shape=jax.ShapeDtypeStruct((blocks * chunk, HD), BF16),
        in_specs=[pl.BlockSpec(memory_space=pltpu.SMEM)] + [vmem] * 4,
        out_specs=vmem,
        scratch_shapes=[
            pltpu.VMEM((NEWTOK, HD), F32),
            pltpu.VMEM((8, NEWTOK), F32),
            pltpu.VMEM((blocks * 8, HD), F32),
        ],
        compiler_params=pltpu.CompilerParams(vmem_limit_bytes=32 << 20),
        name="attend",
    )(meta, queries, k_cache, v_cache, others)


def attend_new_kernel(meta, queries, near, far, num, den, kind):
    here = meta[3 * REQS + 3]
    on_core_0 = meta[3 * REQS + 2] == 0
    rows, count = queries.shape[0], 4
    request = lax.div(meta[3 * REQS + 1] - here * rows, NEWTOK)
    row = lax.broadcasted_iota(jnp.int32, (rows, 1), 0) + here * rows
    start, limit = jnp.zeros_like(row), jnp.zeros_like(row)
    for part in range(count * rows // NEWTOK):
        at = part * NEWTOK
        inside = (row >= at) & (row < at + NEWTOK)
        start = jnp.where(inside, at, start)
        limit = jnp.where(inside, jnp.minimum(row, at + meta[REQS + request + part] - 1), limit)
    total, weights = jnp.zeros((rows, HD), F32), jnp.zeros((rows, 1), F32)
    for step in range(count):
        block = (near if step < 2 else far)[step % 2]
        at = lax.bitwise_xor(here, step) * rows
        logits = lax.dot_general(queries[...], block[0], (((1,), (1,)), ((), ())), preferred_element_type=F32)
        column = lax.broadcasted_iota(jnp.int32, logits.shape, 1) + at
        weight = jnp.exp(soft_cap * jnp.tanh(logits * (1.0 / soft_cap)))
        weight = jnp.where((column >= start) & (column <= limit), weight, 0.0)
        weights += jnp.sum(weight, axis=1, keepdims=True)
        total += jnp.dot(weight.astype(BF16), block[1], preferred_element_type=F32)
        kind[pl.ds(pl.multiple_of(at, 16), rows), :] = jnp.where(on_core_0, block[0], block[1])
    num[...] = total
    den[...] = weights


def attend_new(meta, queries, near, far):
    vmem = pl.BlockSpec(memory_space=pltpu.VMEM)
    rows = queries.shape[0]
    return pl.pallas_call(
        attend_new_kernel,
        out_shape=(
            jax.ShapeDtypeStruct((rows, HD), F32),
            jax.ShapeDtypeStruct((rows, 1), F32),
            jax.ShapeDtypeStruct((4 * rows, HD), BF16),
        ),
        in_specs=[pl.BlockSpec(memory_space=pltpu.SMEM)] + [vmem] * 3,
        out_specs=(vmem, vmem, vmem),
        compiler_params=pltpu.CompilerParams(vmem_limit_bytes=16 << 20),
        name="attend_new",
    )(meta, queries, near, far)


def write_kernel(meta, mine, others, k_old, v_old, k_pool, v_pool):
    slots = k_old.shape[0]
    core = meta[3 * REQS + 2]
    on_core_0 = core == 0
    first = meta[3 * REQS] + core * slots
    k_pool[...] = k_old[...]
    v_pool[...] = v_old[...]

    def write_request(r, carry):
        cached, fresh, offset = meta[r], meta[REQS + r], meta[2 * REQS + r]
        begin = offset + cached - first

        def write_tile(t, carry):
            rows = pl.ds(pl.multiple_of(r * NEWTOK, 64), NEWTOK)
            a, b = mine[rows, :], others[rows, :]
            rows = jnp.concatenate([jnp.where(on_core_0, a, b), jnp.where(on_core_0, b, a)], axis=1)
            slot = lax.broadcasted_iota(jnp.int32, (WRITE_TILE, NEWTOK), 0) + (t * WRITE_TILE - begin)
            index = lax.broadcasted_iota(jnp.int32, (WRITE_TILE, NEWTOK), 1)
            pick = jnp.where((slot == index) & (index < fresh), 1.0, 0.0).astype(BF16)
            new = jnp.dot(pick, rows, preferred_element_type=F32)
            place = lax.broadcasted_iota(jnp.int32, (WRITE_TILE, HD), 0) + (t * WRITE_TILE - begin)
            written = (place >= 0) & (place < fresh)
            here = pl.ds(pl.multiple_of(t * WRITE_TILE, WRITE_TILE), WRITE_TILE)
            k_pool[here, :] = jnp.where(written, new[:, :HD], k_pool[here, :].astype(F32)).astype(BF16)
            v_pool[here, :] = jnp.where(written, new[:, HD:], v_pool[here, :].astype(F32)).astype(BF16)
            return carry

        low, high = jnp.maximum(begin, 0), jnp.minimum(begin + fresh, slots)
        tiles = jnp.where(high > low, pl.cdiv(high, WRITE_TILE), 0)
        lax.fori_loop(lax.div(low, WRITE_TILE), tiles, write_tile, 0)
        return carry

    lax.fori_loop(0, REQS, write_request, 0)


def write(meta, mine, others, k_cache, v_cache):
    vmem = pl.BlockSpec(memory_space=pltpu.VMEM)
    return pl.pallas_call(
        write_kernel,
        out_shape=(
            jax.ShapeDtypeStruct(k_cache.shape, BF16),
            jax.ShapeDtypeStruct(v_cache.shape, BF16),
        ),
        in_specs=[pl.BlockSpec(memory_space=pltpu.SMEM)] + [vmem] * 4,
        out_specs=(vmem, vmem),
        compiler_params=pltpu.CompilerParams(vmem_limit_bytes=32 << 20),
        name="write",
    )(meta, mine, others, k_cache, v_cache)


def divide_kernel(meta, parts, new_num, new_den, out):
    fresh_at = REQS
    begin = meta[3 * REQS + 1]
    total = jnp.sum(parts[...].astype(F32), axis=0)
    for part in range(3):
        row = begin + part * PIECE
        request = row // NEWTOK
        fresh = meta[fresh_at + request]
        within = lax.broadcasted_iota(jnp.int32, (PIECE, HD), 0) + (row - request * NEWTOK)
        den = total[3 * PIECE + part : 3 * PIECE + part + 1, 0:PIECE]
        diagonal = lax.broadcasted_iota(jnp.int32, (PIECE, PIECE), 0) == lax.broadcasted_iota(
            jnp.int32, (PIECE, PIECE), 1
        )
        here = slice(part * PIECE, (part + 1) * PIECE)
        den = jnp.sum(jnp.where(diagonal, den, 0.0), axis=1, keepdims=True) + new_den[here, :]
        value = (total[here, :] + new_num[here, :]) / den
        out[here, :] = jnp.where(within < fresh, value, 0.0).astype(BF16)


def divide(meta, parts, new_num, new_den):
    vmem = pl.BlockSpec(memory_space=pltpu.VMEM)
    return pl.pallas_call(
        divide_kernel,
        out_shape=jax.ShapeDtypeStruct((3 * PIECE, HD), BF16),
        in_specs=[pl.BlockSpec(memory_space=pltpu.SMEM), vmem, vmem, vmem],
        out_specs=vmem,
        compiler_params=pltpu.CompilerParams(vmem_limit_bytes=16 << 20),
        name="divide",
    )(meta, parts, new_num, new_den)


def spread_kernel(meta, attended, own, right, ahead, behind, left, out):
    here = meta[3 * REQS + 3]
    count = 4
    rows = attended.shape[1]
    heads = jnp.concatenate([attended[h] for h in range(attended.shape[0])], axis=1)
    padded = jnp.concatenate([heads, jnp.zeros((2 * HD - rows, heads.shape[1]), BF16)], axis=0)
    last = (((1,), (1,)), ((), ()))
    for step in range(count):
        along = lax.rem(here + step, count)
        for block in range(count):
            at = block * count + along
            if step == 2:
                weights = (ahead if block < 2 else behind)[block % 2]
            else:
                weights = (own, right, None, left)[step][block]
            wide = lax.dot_general(heads, weights[:HD], last, preferred_element_type=F32)
            rest = lax.dot_general(weights[HD:], padded, last, preferred_element_type=F32)
            out[at, :rows, :] = wide.astype(BF16)
            out[at, rows : rows + 16, :] = rest[:, :HD].astype(BF16)
            out[at, rows + 16 :, :] = rest[:, HD:].astype(BF16)


def spread(meta, attended, columns, chunks):
    vmem = pl.BlockSpec(memory_space=pltpu.VMEM)
    return pl.pallas_call(
        spread_kernel,
        out_shape=jax.ShapeDtypeStruct((chunks, attended.shape[1] + 32, HD), BF16),
        in_specs=[pl.BlockSpec(memory_space=pltpu.SMEM)] + [vmem] * (1 + len(columns)),
        out_specs=vmem,
        compiler_params=pltpu.CompilerParams(vmem_limit_bytes=32 << 20),
        name="spread",
    )(meta, attended, *columns)


def on_device(
    tokens, pre_gain, w_q, w_k, w_v, w_o, post_gain, k_cache, v_cache, cached_len, new_len, slot_offset
):
    tok_rows = tokens.shape[0]
    features = tokens.shape[1]
    n_gy = lax.axis_size(GY)
    n_chips = lax.axis_size(CHIPS)
    me = lax.axis_index(GX)
    core = lax.axis_index("c")
    cols = w_q.shape[1]

    float_in = tokens.astype(F32)
    squares = jnp.sum(float_in * float_in, axis=1, keepdims=True)
    high = lax.reduce_precision(squares, 8, 7)
    gained = float_in * (1.0 + pre_gain.astype(F32))
    gained = jnp.concatenate([gained, high, squares - high], axis=1).astype(BF16)
    swap = [(0, 1), (1, 0)]
    first, second = jnp.concatenate([w_q[:, :HD], w_k], axis=1), jnp.concatenate([w_q[:, HD:], w_v], axis=1)
    weights = jnp.where(core == 0, first, second)
    came = lax.ppermute(jnp.where(core == 0, second, first), "c", swap)
    gained, weights = lax.optimization_barrier((gained, weights))
    gained = lax.all_gather(gained, "zl", axis=0, tiled=True)
    gained, came = lax.optimization_barrier((gained, came))
    gained = everywhere(gained, "y", n_gy // 2).reshape(n_gy, tok_rows, -1)
    weights = jnp.concatenate([jnp.where(core == 0, weights, came), jnp.where(core == 0, came, weights)], axis=0)
    inner = weights.shape[0]
    weights = jnp.concatenate([weights, w_o.T], axis=0)
    weights = lax.all_gather(weights, "zh", axis=0)
    w_out = weights[:, inner:, :]
    weights = weights[:, :inner, :]
    from_right = [((i + 1) % 4, i) for i in range(4)]
    from_left = [((i - 1) % 4, i) for i in range(4)]
    right = lax.ppermute(weights, "x", from_right)
    left = lax.ppermute(weights, "x", from_left)
    ahead = lax.ppermute(right[:2], "x", from_right)
    behind = lax.ppermute(left[2:], "x", from_left)
    columns = [weights, right, ahead, behind, left]
    other = lax.ppermute(gained, "c", swap)

    chip_rows = me // 2 * (2 * tok_rows)
    row_ids = chip_rows + jnp.arange(2 * tok_rows, dtype=jnp.int32)
    request = row_ids // NEWTOK
    owner_mask = request[:, None] == jnp.arange(REQS, dtype=jnp.int32)[None, :]
    position = jnp.sum(jnp.where(owner_mask, cached_len[None, :], 0), axis=1) + row_ids % NEWTOK
    half = HD // 2
    inverse = jnp.power(10000.0, -2.0 * jnp.arange(half, dtype=F32) / HD)
    angle = position.astype(F32)[:, None] * inverse[None, :]
    cosine, sine = jnp.cos(angle), jnp.sin(angle)
    cosine = jnp.concatenate([cosine, cosine], axis=1)
    sine = jnp.concatenate([-sine, sine], axis=1)
    turns = jnp.stack(
        [
            cosine * query_scale,
            sine * query_scale,
            jnp.where(core == 0, cosine, 1.0),
            jnp.where(core == 0, sine, 0.0),
        ]
    )
    meta = jnp.concatenate(
        [
            cached_len,
            new_len,
            slot_offset,
            jnp.stack([me // 2 * (2 * k_cache.shape[0]), chip_rows, core, lax.axis_index("x")]).astype(jnp.int32),
        ]
    )
    caches = jnp.concatenate([k_cache, v_cache], axis=0)
    queries, fresh_rows = project(meta, gained, other, turns, columns)

    queries, fresh_rows, w_out, caches = lax.optimization_barrier((queries, fresh_rows, w_out, caches))
    caches = lax.ppermute(caches, "c", swap)
    out_right = lax.ppermute(w_out, "x", from_right)
    out_left = lax.ppermute(w_out, "x", from_left)
    near_rows = lax.all_gather(fresh_rows, "c", axis=0)
    partner_rows = lax.ppermute(near_rows, "x", [(i, i ^ 1) for i in range(4)])
    all_queries = everywhere(queries, CHIPS, n_chips).reshape(-1, HD)
    all_queries, near_rows = lax.optimization_barrier((all_queries, near_rows))
    sums = attend(meta, all_queries, k_cache, v_cache, caches)
    sums, near_rows, partner_rows, out_right, out_left = lax.optimization_barrier(
        (sums, near_rows, partner_rows, out_right, out_left)
    )
    near_rows = jnp.stack([near_rows, partner_rows])
    far_rows = lax.ppermute(near_rows, "x", [(i, i ^ 2) for i in range(4)])
    out_columns = [
        w_out,
        out_right,
        lax.ppermute(out_right[:2], "x", from_right),
        lax.ppermute(out_left[2:], "x", from_left),
        out_left,
    ]

    parts = lax.all_to_all(sums.reshape(n_chips, -1, HD), CHIPS, 0, 0)
    new_num, new_den, kind = attend_new(meta, queries, near_rows, far_rows)
    attended = divide(meta, parts, new_num, new_den)
    attended = lax.all_gather(attended, "c", axis=0)
    partial_out = spread(meta, attended, out_columns, n_gy)
    partial_out, kind = lax.optimization_barrier((partial_out, kind))
    kind = lax.all_gather(kind, "zh", axis=0, tiled=True)
    total = jnp.sum(lax.all_to_all(partial_out, GY, 0, 0).astype(F32), axis=0)
    rows = 2 * tok_rows
    rest = jnp.concatenate([total[rows : rows + 16], total[rows + 16 :, : rows - HD]], axis=1)
    branch = jnp.concatenate([total[:rows], rest.T], axis=1)
    squares = jnp.sum(branch * branch, axis=1).reshape(2, 1, 1, tok_rows)
    squares = jnp.broadcast_to(squares, (2, n_gy, 1, tok_rows)).reshape(2 * n_gy, 1, tok_rows)
    squares, kind = lax.optimization_barrier((squares, kind))
    squares = lax.all_to_all(squares, ("c",) + GY, 0, 0)
    k_pool, v_pool = write(meta, kind, lax.ppermute(kind, "c", swap), k_cache, v_cache)
    mean = jnp.sum(squares, axis=(0, 1)) / D
    kept = lax.dynamic_slice_in_dim(branch, core * tok_rows, tok_rows, 0)
    sent = lax.dynamic_slice_in_dim(branch, (1 - core) * tok_rows, tok_rows, 0)
    came = lax.ppermute(sent, "c", swap)
    branch = jnp.concatenate([jnp.where(core == 0, kept, came), jnp.where(core == 0, came, kept)], axis=1)
    layer_out = float_in + branch * lax.rsqrt(mean + epsilon)[:, None] * (1.0 + post_gain.astype(F32))
    return (layer_out.astype(BF16), k_pool, v_pool)


def solution(mesh):
    parts = Mesh(mesh.devices.reshape(4, 4, 2, 8, 2), GX + GY)
    both = P(GX, GY)
    placed = (both, P(GY), both, both, both, P(GY, GX), P(GY), both, both, P(), P(), P())
    return jax.shard_map(
        on_device, mesh=parts, in_specs=placed, out_specs=(both, both, both), check_vma=False
    )
```

```python
import jax
import jax.numpy as jnp
from jax import lax
from jax.experimental import pallas as pl
from jax.experimental.pallas import tpu as pltpu
from jax.sharding import Mesh, PartitionSpec as P

D = 4608
HD = 128
REQS = 12
NEWTOK = 192
READ_TILE = 512
WRITE_TILE = 256
PIECE = 48
epsilon = 1e-06
soft_cap = 50.0
query_scale = 144.0 ** (-0.5)
F32 = jnp.float32
BF16 = jnp.bfloat16

CHIPS = ("zh", "x")
GX = ("zh", "x", "c")
GY = ("y", "zl")


def everywhere(value, axes, count):
    return lax.all_to_all(jnp.broadcast_to(value[None], (count,) + value.shape), axes, 0, 0)


def project_kernel(meta, mine, others, turns, own, right, ahead, behind, left, *outs):
    on_core_0 = meta[3 * REQS + 2] == 0
    here = meta[3 * REQS + 3]
    features = mine.shape[2] - 2
    count = 4
    total = jnp.zeros((outs[0].shape[0], 2 * HD), F32)
    squares = jnp.zeros((outs[0].shape[0], 2), F32)
    for step in range(count):
        along = lax.rem(here + step, count)
        for block in range(count):
            at = block * count + along
            a, b = mine[at], others[at]
            rows = jnp.concatenate([jnp.where(on_core_0, a, b), jnp.where(on_core_0, b, a)], axis=0)
            squares += rows[:, features:].astype(F32)
            if step == 2:
                columns = (ahead if block < 2 else behind)[block % 2]
            else:
                columns = (own, right, None, left)[step][block]
            total += jnp.dot(rows[:, :features], columns[:features, :], preferred_element_type=F32)
    mean = jnp.sum(squares, axis=1, keepdims=True) * (1.0 / D)
    total = total * lax.rsqrt(mean + epsilon)
    for head in range(2):
        value = total[:, head * HD : (head + 1) * HD]
        value = value * turns[2 * head] + pltpu.roll(value, HD // 2, 1) * turns[2 * head + 1]
        outs[head][...] = value.astype(BF16)


def project(meta, mine, others, turns, columns):
    vmem = pl.BlockSpec(memory_space=pltpu.VMEM)
    return pl.pallas_call(
        project_kernel,
        out_shape=[jax.ShapeDtypeStruct((2 * mine.shape[1], HD), BF16)] * 2,
        in_specs=[pl.BlockSpec(memory_space=pltpu.SMEM)] + [vmem] * (3 + len(columns)),
        out_specs=[vmem, vmem],
        compiler_params=pltpu.CompilerParams(vmem_limit_bytes=32 << 20),
        name="project",
    )(meta, mine, others, turns, *columns)


def attend_kernel(meta, queries, k_own, v_own, others, sums, num, den, totals):
    own = k_own.shape[0]
    first = meta[3 * REQS]
    core = meta[3 * REQS + 2]
    blocks = REQS * NEWTOK // (3 * PIECE)
    chunk = sums.shape[0] // blocks
    totals[...] = jnp.zeros_like(totals)

    def read_request(r, carry):
        cached, offset = meta[r], meta[2 * REQS + r]
        num[...] = jnp.zeros_like(num)
        den[...] = jnp.zeros_like(den)
        for keys, values, at in ((k_own, v_own, core), (others.at[:own, :], others.at[own:, :], 1 - core)):
            begin = offset - first - at * own
            low, high = jnp.maximum(begin, 0), jnp.minimum(begin + cached, own)

            def read_tile(t, carry):
                rows = queries[pl.ds(pl.multiple_of(r * NEWTOK, 64), NEWTOK), :]
                here = pl.ds(pl.multiple_of(t * READ_TILE, READ_TILE), READ_TILE)
                logits = lax.dot_general(
                    rows, keys[here, :], (((1,), (1,)), ((), ())), preferred_element_type=F32
                )
                slot = lax.broadcasted_iota(jnp.int32, logits.shape, 1) + t * READ_TILE
                weight = jnp.exp(soft_cap * jnp.tanh(logits * (1.0 / soft_cap)))
                weight = jnp.where((slot >= low) & (slot < high), weight, 0.0).astype(BF16)
                num[...] += jnp.dot(weight, values[here, :], preferred_element_type=F32)
                den[...] += lax.dot_general(
                    jnp.ones((8, READ_TILE), BF16), weight, (((1,), (1,)), ((), ())), preferred_element_type=F32
                )
                return carry

            tiles = jnp.where(high > low, pl.cdiv(high, READ_TILE), 0)
            lax.fori_loop(lax.div(low, READ_TILE), tiles, read_tile, 0)

        for piece in range(NEWTOK // PIECE):
            at = r * (NEWTOK // PIECE) + piece
            block, part = lax.div(at, 3), lax.rem(at, 3)
            to = pl.multiple_of(block * chunk + part * PIECE, 16)
            at_row = piece * PIECE
            sums[pl.ds(to, PIECE), :] = num[at_row : at_row + PIECE, :].astype(BF16)
            totals[pl.ds(block * 8 + part, 1), 0:PIECE] = den[0:1, at_row : at_row + PIECE]
        return carry

    lax.fori_loop(0, REQS, read_request, 0)
    for block in range(blocks):
        rows = totals[block * 8 : block * 8 + 8, :]
        rows = jnp.concatenate([rows, jnp.zeros_like(rows)], axis=0)
        sums[block * chunk + 3 * PIECE : (block + 1) * chunk, :] = rows.astype(BF16)


def attend(meta, queries, k_cache, v_cache, others):
    blocks = REQS * NEWTOK // (3 * PIECE)
    chunk = 3 * PIECE + 16
    vmem = pl.BlockSpec(memory_space=pltpu.VMEM)
    return pl.pallas_call(
        attend_kernel,
        out_shape=jax.ShapeDtypeStruct((blocks * chunk, HD), BF16),
        in_specs=[pl.BlockSpec(memory_space=pltpu.SMEM)] + [vmem] * 4,
        out_specs=vmem,
        scratch_shapes=[
            pltpu.VMEM((NEWTOK, HD), F32),
            pltpu.VMEM((8, NEWTOK), F32),
            pltpu.VMEM((blocks * 8, HD), F32),
        ],
        compiler_params=pltpu.CompilerParams(vmem_limit_bytes=32 << 20),
        name="attend",
    )(meta, queries, k_cache, v_cache, others)


def attend_new_kernel(meta, queries, near, far, num, den, kind):
    here = meta[3 * REQS + 3]
    on_core_0 = meta[3 * REQS + 2] == 0
    rows, count = queries.shape[0], 4
    request = lax.div(meta[3 * REQS + 1] - here * rows, NEWTOK)
    row = lax.broadcasted_iota(jnp.int32, (rows, 1), 0) + here * rows
    start, limit = jnp.zeros_like(row), jnp.zeros_like(row)
    for part in range(count * rows // NEWTOK):
        at = part * NEWTOK
        inside = (row >= at) & (row < at + NEWTOK)
        start = jnp.where(inside, at, start)
        limit = jnp.where(inside, jnp.minimum(row, at + meta[REQS + request + part] - 1), limit)
    total, weights = jnp.zeros((rows, HD), F32), jnp.zeros((rows, 1), F32)
    for step in range(count):
        block = (near if step < 2 else far)[step % 2]
        at = lax.bitwise_xor(here, step) * rows
        logits = lax.dot_general(queries[...], block[0], (((1,), (1,)), ((), ())), preferred_element_type=F32)
        column = lax.broadcasted_iota(jnp.int32, logits.shape, 1) + at
        weight = jnp.exp(soft_cap * jnp.tanh(logits * (1.0 / soft_cap)))
        weight = jnp.where((column >= start) & (column <= limit), weight, 0.0)
        weights += jnp.sum(weight, axis=1, keepdims=True)
        total += jnp.dot(weight.astype(BF16), block[1], preferred_element_type=F32)
        kind[pl.ds(pl.multiple_of(at, 16), rows), :] = jnp.where(on_core_0, block[0], block[1])
    num[...] = total
    den[...] = weights


def attend_new(meta, queries, near, far):
    vmem = pl.BlockSpec(memory_space=pltpu.VMEM)
    rows = queries.shape[0]
    return pl.pallas_call(
        attend_new_kernel,
        out_shape=(
            jax.ShapeDtypeStruct((rows, HD), F32),
            jax.ShapeDtypeStruct((rows, 1), F32),
            jax.ShapeDtypeStruct((4 * rows, HD), BF16),
        ),
        in_specs=[pl.BlockSpec(memory_space=pltpu.SMEM)] + [vmem] * 3,
        out_specs=(vmem, vmem, vmem),
        compiler_params=pltpu.CompilerParams(vmem_limit_bytes=16 << 20),
        name="attend_new",
    )(meta, queries, near, far)


def write_kernel(meta, mine, others, k_old, v_old, k_pool, v_pool):
    slots = k_old.shape[0]
    core = meta[3 * REQS + 2]
    on_core_0 = core == 0
    first = meta[3 * REQS] + core * slots
    k_pool[...] = k_old[...]
    v_pool[...] = v_old[...]

    def write_request(r, carry):
        cached, fresh, offset = meta[r], meta[REQS + r], meta[2 * REQS + r]
        begin = offset + cached - first

        def write_tile(t, carry):
            rows = pl.ds(pl.multiple_of(r * NEWTOK, 64), NEWTOK)
            a, b = mine[rows, :], others[rows, :]
            rows = jnp.concatenate([jnp.where(on_core_0, a, b), jnp.where(on_core_0, b, a)], axis=1)
            slot = lax.broadcasted_iota(jnp.int32, (WRITE_TILE, NEWTOK), 0) + (t * WRITE_TILE - begin)
            index = lax.broadcasted_iota(jnp.int32, (WRITE_TILE, NEWTOK), 1)
            pick = jnp.where((slot == index) & (index < fresh), 1.0, 0.0).astype(BF16)
            new = jnp.dot(pick, rows, preferred_element_type=F32)
            place = lax.broadcasted_iota(jnp.int32, (WRITE_TILE, HD), 0) + (t * WRITE_TILE - begin)
            written = (place >= 0) & (place < fresh)
            here = pl.ds(pl.multiple_of(t * WRITE_TILE, WRITE_TILE), WRITE_TILE)
            k_pool[here, :] = jnp.where(written, new[:, :HD], k_pool[here, :].astype(F32)).astype(BF16)
            v_pool[here, :] = jnp.where(written, new[:, HD:], v_pool[here, :].astype(F32)).astype(BF16)
            return carry

        low, high = jnp.maximum(begin, 0), jnp.minimum(begin + fresh, slots)
        tiles = jnp.where(high > low, pl.cdiv(high, WRITE_TILE), 0)
        lax.fori_loop(lax.div(low, WRITE_TILE), tiles, write_tile, 0)
        return carry

    lax.fori_loop(0, REQS, write_request, 0)


def write(meta, mine, others, k_cache, v_cache):
    vmem = pl.BlockSpec(memory_space=pltpu.VMEM)
    return pl.pallas_call(
        write_kernel,
        out_shape=(
            jax.ShapeDtypeStruct(k_cache.shape, BF16),
            jax.ShapeDtypeStruct(v_cache.shape, BF16),
        ),
        in_specs=[pl.BlockSpec(memory_space=pltpu.SMEM)] + [vmem] * 4,
        out_specs=(vmem, vmem),
        compiler_params=pltpu.CompilerParams(vmem_limit_bytes=32 << 20),
        name="write",
    )(meta, mine, others, k_cache, v_cache)


def divide_kernel(meta, parts, new_num, new_den, out):
    fresh_at = REQS
    begin = meta[3 * REQS + 1]
    total = jnp.sum(parts[...].astype(F32), axis=0)
    for part in range(3):
        row = begin + part * PIECE
        request = row // NEWTOK
        fresh = meta[fresh_at + request]
        within = lax.broadcasted_iota(jnp.int32, (PIECE, HD), 0) + (row - request * NEWTOK)
        den = total[3 * PIECE + part : 3 * PIECE + part + 1, 0:PIECE]
        diagonal = lax.broadcasted_iota(jnp.int32, (PIECE, PIECE), 0) == lax.broadcasted_iota(
            jnp.int32, (PIECE, PIECE), 1
        )
        here = slice(part * PIECE, (part + 1) * PIECE)
        den = jnp.sum(jnp.where(diagonal, den, 0.0), axis=1, keepdims=True) + new_den[here, :]
        value = (total[here, :] + new_num[here, :]) / den
        out[here, :] = jnp.where(within < fresh, value, 0.0).astype(BF16)


def divide(meta, parts, new_num, new_den):
    vmem = pl.BlockSpec(memory_space=pltpu.VMEM)
    return pl.pallas_call(
        divide_kernel,
        out_shape=jax.ShapeDtypeStruct((3 * PIECE, HD), BF16),
        in_specs=[pl.BlockSpec(memory_space=pltpu.SMEM), vmem, vmem, vmem],
        out_specs=vmem,
        compiler_params=pltpu.CompilerParams(vmem_limit_bytes=16 << 20),
        name="divide",
    )(meta, parts, new_num, new_den)


def spread_kernel(meta, attended, own, right, ahead, behind, left, out):
    here = meta[3 * REQS + 3]
    count = 4
    rows = attended.shape[1]
    heads = jnp.concatenate([attended[h] for h in range(attended.shape[0])], axis=1)
    tail, empty = heads[HD:], jnp.zeros((HD, heads.shape[1]), BF16)
    low = jnp.concatenate([tail, empty[16:]], axis=0)
    high = jnp.concatenate([empty[:16], tail, empty[32:]], axis=0)
    last = (((1,), (1,)), ((), ()))
    for step in range(count):
        along = lax.rem(here + step, count)
        for block in range(count):
            at = block * count + along
            if step == 2:
                weights = (ahead if block < 2 else behind)[block % 2]
            else:
                weights = (own, right, None, left)[step][block]
            wide = lax.dot_general(heads, weights[:HD], last, preferred_element_type=F32)
            rest = lax.dot_general(weights[HD:], heads[:HD], last, preferred_element_type=F32)
            out[at, :rows, :] = wide.astype(BF16)
            out[at, rows : rows + 16, :] = rest.astype(BF16)
            corner = lax.dot_general(weights[HD : HD + 8], low, last, preferred_element_type=F32)
            corner += lax.dot_general(weights[HD + 8 :], high, last, preferred_element_type=F32)
            out[at, rows + 16 :, :] = corner.astype(BF16)


def spread(meta, attended, columns, chunks):
    vmem = pl.BlockSpec(memory_space=pltpu.VMEM)
    return pl.pallas_call(
        spread_kernel,
        out_shape=jax.ShapeDtypeStruct((chunks, attended.shape[1] + 24, HD), BF16),
        in_specs=[pl.BlockSpec(memory_space=pltpu.SMEM)] + [vmem] * (1 + len(columns)),
        out_specs=vmem,
        compiler_params=pltpu.CompilerParams(vmem_limit_bytes=32 << 20),
        name="spread",
    )(meta, attended, *columns)


def on_device(
    tokens, pre_gain, w_q, w_k, w_v, w_o, post_gain, k_cache, v_cache, cached_len, new_len, slot_offset
):
    tok_rows = tokens.shape[0]
    features = tokens.shape[1]
    n_gy = lax.axis_size(GY)
    n_chips = lax.axis_size(CHIPS)
    me = lax.axis_index(GX)
    core = lax.axis_index("c")
    cols = w_q.shape[1]

    float_in = tokens.astype(F32)
    squares = jnp.sum(float_in * float_in, axis=1, keepdims=True)
    high = lax.reduce_precision(squares, 8, 7)
    gained = float_in * (1.0 + pre_gain.astype(F32))
    gained = jnp.concatenate([gained, high, squares - high], axis=1).astype(BF16)
    swap = [(0, 1), (1, 0)]
    first, second = jnp.concatenate([w_q[:, :HD], w_k], axis=1), jnp.concatenate([w_q[:, HD:], w_v], axis=1)
    weights = jnp.where(core == 0, first, second)
    came = lax.ppermute(jnp.where(core == 0, second, first), "c", swap)
    gained, weights = lax.optimization_barrier((gained, weights))
    gained = lax.all_gather(gained, "zl", axis=0, tiled=True)
    gained, came = lax.optimization_barrier((gained, came))
    gained = everywhere(gained, "y", n_gy // 2).reshape(n_gy, tok_rows, -1)
    weights = jnp.concatenate([jnp.where(core == 0, weights, came), jnp.where(core == 0, came, weights)], axis=0)
    inner = weights.shape[0]
    weights = jnp.concatenate([weights, w_o.T], axis=0)
    weights = lax.all_gather(weights, "zh", axis=0)
    w_out = weights[:, inner:, :]
    weights = weights[:, :inner, :]
    from_right = [((i + 1) % 4, i) for i in range(4)]
    from_left = [((i - 1) % 4, i) for i in range(4)]
    right = lax.ppermute(weights, "x", from_right)
    left = lax.ppermute(weights, "x", from_left)
    ahead = lax.ppermute(right[:2], "x", from_right)
    behind = lax.ppermute(left[2:], "x", from_left)
    columns = [weights, right, ahead, behind, left]
    other = lax.ppermute(gained, "c", swap)

    chip_rows = me // 2 * (2 * tok_rows)
    row_ids = chip_rows + jnp.arange(2 * tok_rows, dtype=jnp.int32)
    request = row_ids // NEWTOK
    owner_mask = request[:, None] == jnp.arange(REQS, dtype=jnp.int32)[None, :]
    position = jnp.sum(jnp.where(owner_mask, cached_len[None, :], 0), axis=1) + row_ids % NEWTOK
    half = HD // 2
    inverse = jnp.power(10000.0, -2.0 * jnp.arange(half, dtype=F32) / HD)
    angle = position.astype(F32)[:, None] * inverse[None, :]
    cosine, sine = jnp.cos(angle), jnp.sin(angle)
    cosine = jnp.concatenate([cosine, cosine], axis=1)
    sine = jnp.concatenate([-sine, sine], axis=1)
    turns = jnp.stack(
        [
            cosine * query_scale,
            sine * query_scale,
            jnp.where(core == 0, cosine, 1.0),
            jnp.where(core == 0, sine, 0.0),
        ]
    )
    meta = jnp.concatenate(
        [
            cached_len,
            new_len,
            slot_offset,
            jnp.stack([me // 2 * (2 * k_cache.shape[0]), chip_rows, core, lax.axis_index("x")]).astype(jnp.int32),
        ]
    )
    caches = jnp.concatenate([k_cache, v_cache], axis=0)
    queries, fresh_rows = project(meta, gained, other, turns, columns)

    queries, fresh_rows, w_out, caches = lax.optimization_barrier((queries, fresh_rows, w_out, caches))
    caches = lax.ppermute(caches, "c", swap)
    out_right = lax.ppermute(w_out, "x", from_right)
    out_left = lax.ppermute(w_out, "x", from_left)
    near_rows = lax.all_gather(fresh_rows, "c", axis=0)
    partner_rows = lax.ppermute(near_rows, "x", [(i, i ^ 1) for i in range(4)])
    all_queries = everywhere(queries, CHIPS, n_chips).reshape(-1, HD)
    all_queries, near_rows = lax.optimization_barrier((all_queries, near_rows))
    sums = attend(meta, all_queries, k_cache, v_cache, caches)
    sums, near_rows, partner_rows, out_right, out_left = lax.optimization_barrier(
        (sums, near_rows, partner_rows, out_right, out_left)
    )
    near_rows = jnp.stack([near_rows, partner_rows])
    far_rows = lax.ppermute(near_rows, "x", [(i, i ^ 2) for i in range(4)])
    out_columns = [
        w_out,
        out_right,
        lax.ppermute(out_right[:2], "x", from_right),
        lax.ppermute(out_left[2:], "x", from_left),
        out_left,
    ]

    parts = lax.all_to_all(sums.reshape(n_chips, -1, HD), CHIPS, 0, 0)
    new_num, new_den, kind = attend_new(meta, queries, near_rows, far_rows)
    attended = divide(meta, parts, new_num, new_den)
    attended = lax.all_gather(attended, "c", axis=0)
    partial_out = spread(meta, attended, out_columns, n_gy)
    partial_out, kind = lax.optimization_barrier((partial_out, kind))
    kind = lax.all_gather(kind, "zh", axis=0, tiled=True)
    total = jnp.sum(lax.all_to_all(partial_out, GY, 0, 0).astype(F32), axis=0)
    rows = 2 * tok_rows
    corner = jnp.concatenate([total[rows + 16 :, :16], total[rows + 16 :, 16:32]], axis=0)
    rest = jnp.concatenate([total[rows : rows + 16], corner], axis=1)
    branch = jnp.concatenate([total[:rows], rest.T], axis=1)
    squares = jnp.sum(branch * branch, axis=1).reshape(2, 1, 1, tok_rows)
    squares = jnp.broadcast_to(squares, (2, n_gy, 1, tok_rows)).reshape(2 * n_gy, 1, tok_rows)
    squares, kind = lax.optimization_barrier((squares, kind))
    squares = lax.all_to_all(squares, ("c",) + GY, 0, 0)
    k_pool, v_pool = write(meta, kind, lax.ppermute(kind, "c", swap), k_cache, v_cache)
    mean = jnp.sum(squares, axis=(0, 1)) / D
    kept = lax.dynamic_slice_in_dim(branch, core * tok_rows, tok_rows, 0)
    sent = lax.dynamic_slice_in_dim(branch, (1 - core) * tok_rows, tok_rows, 0)
    came = lax.ppermute(sent, "c", swap)
    branch = jnp.concatenate([jnp.where(core == 0, kept, came), jnp.where(core == 0, came, kept)], axis=1)
    layer_out = float_in + branch * lax.rsqrt(mean + epsilon)[:, None] * (1.0 + post_gain.astype(F32))
    return (layer_out.astype(BF16), k_pool, v_pool)


def solution(mesh):
    parts = Mesh(mesh.devices.reshape(4, 4, 2, 8, 2), GX + GY)
    both = P(GX, GY)
    placed = (both, P(GY), both, both, both, P(GY, GX), P(GY), both, both, P(), P(), P())
    return jax.shard_map(
        on_device, mesh=parts, in_specs=placed, out_specs=(both, both, both), check_vma=False
    )
```
